32 devices in a mesh: groups: 2 (over y), seqin: 4 (over z), seqout: 2 (over x), chan: 2 (over core).
Axes of the slice: x: 2, y: 2, z: 4, core: 2. Of those that a mesh axis runs over, the one named last changes fastest.
Arguments:
- inputs: bfloat16 [4, 512, 2048], P(('groups', 'seqout'), 'seqin', 'chan'), parts along dimension 0, may hold values from -6 to 6
- time_step: float32 [2048], P('chan'), may hold values from 0 to 0.06, as said below
- decay_rate: float32 [32, 2048], P(None, 'chan'), may hold values from 0.25 to 1
- frequency: float32 [32, 2048], P(None, 'chan'), may hold values from 0 to 200
- output_real: float32 [32, 2048], P(None, 'chan'), may hold values from -0.5 to 0.5
- output_imag: float32 [32, 2048], P(None, 'chan'), may hold values from -0.5 to 0.5
- skip_gain: float32 [2048], P('chan'), may hold values from 0.5 to 1.5
Outputs:
- outputs: float32 [4, 512, 2048], P(('groups', 'seqout'), 'seqin', 'chan'), parts along dimension 0
The draws below stay inside these ranges and needn't reach their ends.
There are 2 independent parts, one for each index of `groups`. The reference program is written for one: setup_inputs(seed, part) draws one part's arguments, and reference() takes and returns one part's arrays. A program takes and returns all parts, laid end to end along the dimension named above; an argument that names none is the same for every part. Nothing has to cross between parts.
Inputs may be any that keep to these rules, and one draw needn't show every extreme that they name: `time_step`: every step is positive.
All inputs are finite; a program needn't handle non-finite values.
Results may differ from the reference program's by a relative error of at most 0.0003.
Values may be sent and summed in bfloat16 or wider, within the bound.
No kernel may reach another device: no remote copies, remote signals or barrier semaphores. Data moves between devices by JAX's collectives and lax.ppermute only.
A program may use at most 128 MiB of HBM per device.

```python
import math
import jax
import jax.numpy as jnp
from jax import lax

TOK_DEV = 128
CHANNELS = 2048
STATES = 32
BLOCK = 512
SEQ = 1024
N_SEQOUT = 2


def draw_time_step(key, part):
    choose_key, slow_key, fast_key = jax.random.split(key, 3)
    slow_share = 0.5
    slow_mask = jax.random.bernoulli(choose_key, slow_share, (CHANNELS,))
    chain_len = float(SEQ)
    slow_value = jnp.exp(jax.random.uniform(slow_key, (CHANNELS,), jnp.float32, jnp.log(0.2 / chain_len), jnp.log(2.0 / chain_len)))
    fast_value = jnp.exp(jax.random.uniform(fast_key, (CHANNELS,), jnp.float32, jnp.log(2.0 / chain_len), jnp.log(0.06)))
    return jnp.where(slow_mask, slow_value, fast_value).astype(jnp.float32)


def block_levels(key, shape, cuts, smallest, high):
    gain, own = 1.0, jax.random.fold_in(key, 6)
    for axis_at, shards_of in cuts:
        heights = jnp.exp(jax.random.uniform(jax.random.fold_in(own, axis_at), (shards_of,), jnp.float32, smallest / len(cuts), high / len(cuts)))
        gain = gain * jnp.repeat(heights, shape[axis_at] // shards_of).reshape([-1 if axis == axis_at else 1 for axis in range(len(shape))])
    return gain


def noise(rng, extent, scale, most, pieces=(), kind=jnp.bfloat16):
    gain = block_levels(rng, extent, pieces, -0.22, 0.18) if pieces else 1.0
    drawn = jax.random.normal(rng, extent, jnp.float32) * scale * gain
    return jnp.minimum(jnp.maximum(drawn, -most), most).astype(kind)


def setup_inputs(seed: int = 0, part: int = 0) -> dict:
    arg_keys = jax.random.split(jax.random.key(seed), 8)
    part_keys = jax.random.split(jax.random.fold_in(arg_keys[7], part), 8)
    inputs = noise(part_keys[0], (N_SEQOUT, BLOCK, CHANNELS), 1.0, 6.0, ((0, 2), (1, 4), (2, 2)))
    time_step = draw_time_step(jax.random.fold_in(arg_keys[7], 71), part)
    decay_rate = jnp.clip(jnp.exp(math.log(1.0) - 1.3862944 * jax.random.uniform(arg_keys[2], (STATES, CHANNELS), jnp.float32) ** block_levels(arg_keys[2], (STATES, CHANNELS), ((1, 2),), -0.2, 0.2)), 0.25, 1.0)
    frequency = jnp.clip(200.0 * jax.random.uniform(arg_keys[3], (STATES, CHANNELS), jnp.float32) ** block_levels(arg_keys[3], (STATES, CHANNELS), ((1, 2),), -0.2, 0.2), 0.0, 200.0)
    output_real = noise(arg_keys[4], (STATES, CHANNELS), (4 * STATES) ** -0.5, 0.5, ((1, 2),), jnp.float32)
    output_imag = noise(arg_keys[5], (STATES, CHANNELS), (4 * STATES) ** -0.5, 0.5, ((1, 2),), jnp.float32)
    skip_gain = jnp.clip(0.5 + 1.0 * jax.random.uniform(arg_keys[6], (CHANNELS,), jnp.float32) ** block_levels(arg_keys[6], (CHANNELS,), ((0, 2),), -0.2, 0.2), 0.5, 1.5)
    return {"inputs": inputs, "time_step": time_step, "decay_rate": decay_rate, "frequency": frequency, "output_real": output_real, "output_imag": output_imag, "skip_gain": skip_gain}


highest = lax.Precision.HIGHEST

def power_pair(fade_rate, turn_rate, amount):
    shrink = jnp.exp(-fade_rate * amount)
    return (shrink * jnp.cos(turn_rate * amount), shrink * jnp.sin(turn_rate * amount))

def reference(inputs, time_step, decay_rate, frequency, output_real, output_imag, skip_gain):
    blocks, block_len, channels = inputs.shape
    portion = TOK_DEV
    portions = block_len // portion
    fade_rate = time_step[None, :] * decay_rate
    turn_rate = time_step[None, :] * frequency
    input_gain = jnp.sqrt(-jnp.expm1(-2.0 * fade_rate))
    weight_real = input_gain * output_real
    weight_imag = input_gain * output_imag
    offsets = jnp.arange(portion).astype(jnp.float32)[:, None, None]
    near_real, near_imag = power_pair(fade_rate, turn_rate, offsets)
    starts = (jnp.arange(portions) * portion).astype(jnp.float32)[:, None, None]

    def spread(lead_real, lead_imag):
        first = jnp.einsum('anc,rnc->arc', lead_real, near_real, precision=highest)
        second = jnp.einsum('anc,rnc->arc', lead_imag, near_imag, precision=highest)
        return (2.0 * (first - second)).reshape(block_len, channels)
    far_real, far_imag = power_pair(fade_rate, turn_rate, starts)
    kernel = spread(weight_real * far_real - weight_imag * far_imag, weight_real * far_imag + weight_imag * far_real)
    kernel_hat = jnp.fft.rfft(kernel, n=2 * block_len, axis=0)
    next_real, next_imag = power_pair(fade_rate, turn_rate, starts + 1.0)
    tail_real, tail_imag = power_pair(fade_rate, turn_rate, block_len - starts - portion)
    span_real, span_imag = power_pair(fade_rate, turn_rate, float(block_len))
    back_real = near_real[::-1]
    back_imag = near_imag[::-1]
    state_real = jnp.zeros(fade_rate.shape, jnp.float32)
    state_imag = jnp.zeros(fade_rate.shape, jnp.float32)
    results = []
    for index in range(blocks):
        values = inputs[index].astype(jnp.float32)
        spectrum = jnp.fft.rfft(values, n=2 * block_len, axis=0) * kernel_hat
        convolved = jnp.fft.irfft(spectrum, n=2 * block_len, axis=0)[:block_len]
        lead_real = output_real * state_real - output_imag * state_imag
        lead_imag = output_real * state_imag + output_imag * state_real
        carried = spread(lead_real * next_real - lead_imag * next_imag, lead_real * next_imag + lead_imag * next_real)
        results.append(convolved + carried + skip_gain[None, :] * values)
        rows_here = values.reshape(portions, portion, channels)
        inner_real = jnp.einsum('rnc,arc->anc', back_real, rows_here, precision=highest)
        inner_imag = jnp.einsum('rnc,arc->anc', back_imag, rows_here, precision=highest)
        add_real = lax.optimization_barrier(jnp.sum(tail_real * inner_real - tail_imag * inner_imag, axis=0))
        add_imag = lax.optimization_barrier(jnp.sum(tail_real * inner_imag + tail_imag * inner_real, axis=0))
        new_real = span_real * state_real - span_imag * state_imag + input_gain * add_real
        new_imag = span_real * state_imag + span_imag * state_real + input_gain * add_imag
        state_real = new_real
        state_imag = new_imag
    return jnp.stack(results).astype(jnp.float32)
```

```python
import functools

import jax
import jax.numpy as jnp
from jax import lax
from jax.experimental import pallas as pl
from jax.experimental.pallas import tpu as pltpu
from jax.sharding import PartitionSpec as P

LANES = 128
NEAR = 16
SEQ_AXES = ("seqin", "seqout")


def cmul(a, b):
    return (a[0] * b[0] - a[1] * b[1], a[0] * b[1] + a[1] * b[0])


def cos_sin(angle):
    turns = jnp.floor(angle * 0.6366197723675814 + 0.5)
    rest = angle - turns * 1.5703125
    rest = rest - turns * 4.837512969970703125e-4
    rest = rest - turns * 7.549789948768648e-8
    square = rest * rest
    sine = rest + rest * square * (
        -1.6666654611e-1 + square * (8.3321608736e-3 - square * 1.9515295891e-4)
    )
    cosine = (
        1.0
        - 0.5 * square
        + square * square * (4.166664568298827e-2 + square * (-1.388731625493765e-3 + square * 2.443315711809948e-5))
    )
    quarter = turns.astype(jnp.int32) & 3
    swap = (quarter & 1) == 1
    first = jnp.where(swap, sine, cosine)
    second = jnp.where(swap, cosine, sine)
    return (
        jnp.where((quarter == 1) | (quarter == 2), -first, first),
        jnp.where(quarter >= 2, -second, second),
    )


def decay_step(time_step, decay_rate, frequency):
    fade_rate = time_step * decay_rate
    shrink = jnp.exp(-fade_rate)
    cosine, sine = cos_sin(time_step * frequency)
    return (fade_rate, (shrink * cosine, shrink * sine))


def gain_of(fade_rate):
    double = 2.0 * fade_rate
    series = 1.0 / 40320.0
    for factor in (5040.0, 720.0, 120.0, 24.0, 6.0, 2.0, 1.0):
        series = 1.0 / factor - double * series
    small = double * series
    return jnp.sqrt(jnp.where(double < 0.25, small, 1.0 - jnp.exp(-double)))


def power_list(lam, count):
    powers = [None, lam]
    for k in range(2, count + 1):
        powers.append(cmul(powers[k // 2], powers[k - k // 2]))
    return powers


def spread_rows(source_ref, target_ref, rows, groups, stack):
    for start in range(0, rows, stack):
        for k in range(groups):
            part = source_ref[start : start + stack, k * LANES : (k + 1) * LANES]
            target_ref[pl.ds(start * groups + k, stack, stride=groups), :] = part.astype(jnp.float32)


def store_powers(near_ref, n, powers, groups):
    for u in range(1, NEAR):
        for part in range(2):
            row = pl.multiple_of((n * (2 * NEAR) + 2 * u + part) * groups, groups)
            near_ref[pl.ds(row, groups), :] = powers[u][part]


def power_sum(near_ref, lead_ref, states, outer, groups, start_of, emit):
    u_tile, a_tile = 8, min(4, outer)
    for u0 in range(0, NEAR, u_tile):
        for a0 in range(0, outer, a_tile):

            def turn(n, acc, u0=u0, a0=a0):
                def near(u, part):
                    row = pl.multiple_of((n * (2 * NEAR) + 2 * u + part) * groups, groups)
                    return near_ref[pl.ds(row, groups), :]

                def lead(a, part):
                    row = pl.multiple_of((n * (2 * outer) + 2 * a + part) * groups, groups)
                    return lead_ref[pl.ds(row, groups), :]

                leads = [(lead(a0 + a, 0), lead(a0 + a, 1)) for a in range(a_tile)]
                acc = list(acc)
                for u in range(u_tile):
                    if u0 + u == 0:
                        for a in range(a_tile):
                            acc[u * a_tile + a] = acc[u * a_tile + a] + leads[a][0]
                        continue
                    real, imag = near(u0 + u, 0), near(u0 + u, 1)
                    for a in range(a_tile):
                        slot = u * a_tile + a
                        acc[slot] = acc[slot] + leads[a][0] * real - leads[a][1] * imag
                return tuple(acc)

            init = tuple(
                start_of((a0 + a) * NEAR + u0 + u) for u in range(u_tile) for a in range(a_tile)
            )
            acc = lax.fori_loop(0, states, turn, init)
            for u in range(u_tile):
                for a in range(a_tile):
                    emit((a0 + a) * NEAR + u0 + u, acc[u * a_tile + a])


def tables_kernel(
    width, step_ref, decay_ref, freq_ref, real_ref, imag_ref,
    taps_ref, seed_ref, mid_ref,
    decay_sp, freq_sp, real_sp, imag_sp, near_ref, lead_ref,
):
    states = decay_ref.shape[0]
    groups = decay_ref.shape[1] // LANES
    outer = taps_ref.shape[0] // groups // NEAR
    if width == LANES:
        place = lax.axis_index("seqin") * lax.axis_size("seqout") + lax.axis_index("seqout")
        own = pl.ds(pl.multiple_of(place * LANES, LANES), LANES)
        fade, lam = decay_step(step_ref[pl.ds(place, 1), :], decay_ref[:, own], freq_ref[:, own])
        mid_ref[0:states, :] = lam[0]
        mid_ref[states : 2 * states, :] = lam[1]
        mid_ref[2 * states : 3 * states, :] = gain_of(fade)
    for source, target in ((decay_ref, decay_sp), (freq_ref, freq_sp), (real_ref, real_sp), (imag_ref, imag_sp)):
        spread_rows(source, target, states, groups, 8)
    step = step_ref[...]

    def prepare(n, carry):
        at = pl.ds(pl.multiple_of(n * groups, groups), groups)
        fade, lam = decay_step(step, decay_sp[at, :], freq_sp[at, :])
        powers = power_list(lam, NEAR)
        store_powers(near_ref, n, powers, groups)
        weight = (2.0 * real_sp[at, :], 2.0 * imag_sp[at, :])
        shifted = cmul(weight, lam)
        for part in range(2):
            row = pl.multiple_of((n * 4 + part) * groups, groups)
            seed_ref[pl.ds(row, groups), :] = lam[part]
            row = pl.multiple_of((n * 4 + 2 + part) * groups, groups)
            seed_ref[pl.ds(row, groups), :] = shifted[part]
        gain = gain_of(fade)
        lead = (weight[0] * gain, weight[1] * gain)
        for a in range(outer):
            if a:
                lead = cmul(lead, powers[NEAR])
            for part in range(2):
                row = pl.multiple_of((n * (2 * outer) + 2 * a + part) * groups, groups)
                lead_ref[pl.ds(row, groups), :] = lead[part]
        return carry

    lax.fori_loop(0, states, prepare, 0)
    zero = jnp.zeros((groups, LANES), jnp.float32)

    def emit(t, value):
        taps_ref[t * groups : (t + 1) * groups, :] = value

    power_sum(near_ref, lead_ref, states, outer, groups, lambda t: zero, emit)


def conv_kernel(signal_ref, taps_ref, skip_ref, out_ref, signal_sp, taps_pad):
    tokens, channels = signal_ref.shape
    groups = channels // LANES
    tile = 8
    spread_rows(signal_ref, signal_sp, tokens, groups, 16)
    taps_pad[0 : tile * groups, :] = jnp.zeros((tile * groups, LANES), jnp.float32)
    taps_pad[tile * groups : (tile + tokens) * groups, :] = taps_ref[...]
    skip = skip_ref[...]

    def value(t):
        return signal_sp[pl.ds(pl.multiple_of(t * groups, groups), groups), :]

    def row_tile(ti, carry):
        def col_tile(ji, acc):
            gap = (ti - ji) * tile + 1
            window = [
                taps_pad[pl.ds(pl.multiple_of((gap + m) * groups, groups), groups), :]
                for m in range(2 * tile - 1)
            ]
            acc = list(acc)
            for j in range(tile):
                drive = value(ji * tile + j)
                for t in range(tile):
                    acc[t] = acc[t] + window[t - j + tile - 1] * drive
            return tuple(acc)

        acc = lax.fori_loop(0, ti + 1, col_tile, tuple(skip * value(ti * tile + t) for t in range(tile)))
        for t in range(tile):
            row = pl.multiple_of((ti * tile + t) * groups, groups)
            out_ref[pl.ds(row, groups), :] = acc[t]
        return carry

    lax.fori_loop(0, tokens // tile, row_tile, 0)


def states_kernel(n_in, n_out, tokens, signal_ref, mid_ref, out_ref, signal_f, near_ref):
    states = mid_ref.shape[0] // 3
    width = mid_ref.shape[1]
    parts = n_in * n_out
    tiles = states // 8
    a_tile = 4
    signal_f[...] = signal_ref[...].astype(jnp.float32)
    lam = (mid_ref[0:states, :], mid_ref[states : 2 * states, :])
    gain = mid_ref[2 * states : 3 * states, :]
    powers = power_list(lam, NEAR)
    for u in range(1, NEAR):
        for part in range(2):
            near_ref[2 * u + part] = powers[u][part]
    hop1 = powers[NEAR]
    hop2 = cmul(hop1, hop1)
    hop3 = cmul(hop1, hop2)
    hop4 = cmul(hop2, hop2)
    hops = [None, hop1, hop2, hop3]
    per_part = tokens // (NEAR * a_tile)

    def advance(base, state):
        real = [None] * a_tile
        imag = [None] * a_tile
        for u in range(NEAR):
            drive = [
                jnp.broadcast_to(signal_f[pl.ds(base + a * NEAR + u, 1), :], (states, width))
                for a in range(a_tile)
            ]
            power = NEAR - 1 - u
            if power:
                near_real, near_imag = near_ref[2 * power], near_ref[2 * power + 1]
            for a in range(a_tile):
                if power:
                    add_real, add_imag = near_real * drive[a], near_imag * drive[a]
                    real[a] = add_real if real[a] is None else real[a] + add_real
                    imag[a] = add_imag if imag[a] is None else imag[a] + add_imag
                else:
                    real[a] = real[a] + drive[a]
        total = (real[a_tile - 1], imag[a_tile - 1])
        for a in range(a_tile - 1):
            moved = cmul(hops[a_tile - 1 - a], (real[a], imag[a]))
            total = (total[0] + moved[0], total[1] + moved[1])
        moved = cmul(hop4, state)
        return (moved[0] + total[0], moved[1] + total[1])

    def part_turn(s, state):
        place = lax.rem(s, n_in) * n_out + s // n_in
        out_ref[place, 0:states, :] = gain * state[0]
        out_ref[place, states : 2 * states, :] = gain * state[1]

        def inside(i, state):
            base = pl.multiple_of(place * tokens + i * (a_tile * NEAR), a_tile * NEAR)
            return advance(base, state)

        return lax.fori_loop(0, per_part, inside, state)

    zero = jnp.zeros((states, width), jnp.float32)
    state = lax.fori_loop(0, parts - 1, part_turn, (zero, zero))
    out_ref[parts - 1, 0:states, :] = gain * state[0]
    out_ref[parts - 1, states : 2 * states, :] = gain * state[1]


def final_kernel(local_ref, seed_ref, state_ref, out_ref, near_ref, lead_ref, rows_ref):
    tokens = out_ref.shape[0]
    groups = out_ref.shape[1] // LANES
    states = seed_ref.shape[0] // (4 * groups)
    outer = tokens // NEAR

    def prepare(n, carry):
        def seed(i):
            return seed_ref[pl.ds(pl.multiple_of((n * 4 + i) * groups, groups), groups), :]

        lam, weight = (seed(0), seed(1)), (seed(2), seed(3))
        powers = power_list(lam, NEAR)
        store_powers(near_ref, n, powers, groups)
        entering = tuple(
            state_ref[pl.ds(n + part * states, groups, stride=2 * states), :] for part in range(2)
        )
        lead = cmul(weight, entering)
        for a in range(outer):
            if a:
                lead = cmul(lead, powers[NEAR])
            for part in range(2):
                row = pl.multiple_of((n * (2 * outer) + 2 * a + part) * groups, groups)
                lead_ref[pl.ds(row, groups), :] = lead[part]
        return carry

    lax.fori_loop(0, states, prepare, 0)

    def start_of(t):
        return local_ref[t * groups : (t + 1) * groups, :]

    def emit(t, value):
        rows_ref[t * groups : (t + 1) * groups, :] = value

    power_sum(near_ref, lead_ref, states, outer, groups, start_of, emit)
    for start in range(0, tokens, 8):
        for k in range(groups):
            out_ref[start : start + 8, k * LANES : (k + 1) * LANES] = rows_ref[
                pl.ds(start * groups + k, 8, stride=groups), :
            ]


def per_device(n_in, n_out, inputs, time_step, decay_rate, frequency, output_real, output_imag, skip_gain):
    signal = inputs[0]
    tokens, channels = signal.shape
    states = decay_rate.shape[0]
    groups = channels // LANES
    parts = n_in * n_out
    width = channels // parts
    outer = tokens // NEAR
    f32 = jnp.float32
    params = pltpu.CompilerParams(vmem_limit_bytes=40 * 1024 * 1024)

    def rows(count, dtype=f32):
        return pltpu.VMEM((count * groups, LANES), dtype)

    def shape(*dims):
        return jax.ShapeDtypeStruct(dims, f32)

    whole = lax.all_to_all(signal, SEQ_AXES, split_axis=1, concat_axis=0, tiled=True)

    taps, seeds, mid = pl.pallas_call(
        functools.partial(tables_kernel, width),
        out_shape=(
            shape(tokens * groups, LANES),
            shape(states * 4 * groups, LANES),
            shape(3 * states, LANES),
        ),
        scratch_shapes=[rows(states)] * 4 + [rows(states * 2 * NEAR), rows(states * 2 * outer)],
        compiler_params=params,
        cost_estimate=pl.CostEstimate(flops=20_000_000, bytes_accessed=2_000_000, transcendentals=40_000),
        name="tables",
    )(time_step.reshape(groups, LANES), decay_rate, frequency, output_real, output_imag)

    if width != LANES:
        place = lax.axis_index("seqin") * n_out + lax.axis_index("seqout")

        def own(array):
            return lax.dynamic_slice_in_dim(array, place * width, width, array.ndim - 1)

        fade, lam = decay_step(own(time_step)[None, :], own(decay_rate), own(frequency))
        mid = jnp.concatenate([lam[0], lam[1], gain_of(fade)], axis=0)

    entering = pl.pallas_call(
        functools.partial(states_kernel, n_in, n_out, tokens),
        out_shape=shape(parts, 2 * states, width),
        scratch_shapes=[
            pltpu.VMEM((parts * tokens, width), f32),
            pltpu.VMEM((2 * NEAR, states, width), f32),
        ],
        compiler_params=params,
        cost_estimate=pl.CostEstimate(flops=16_000_000, bytes_accessed=1_000_000, transcendentals=0),
        name="states",
    )(whole, mid)

    taps, entering = lax.optimization_barrier((taps, entering))
    entering = lax.all_to_all(entering, SEQ_AXES, split_axis=0, concat_axis=0, tiled=True)
    if width != LANES:
        entering = entering.transpose(1, 0, 2).reshape(2 * states, groups, LANES).transpose(1, 0, 2)
    entering = entering.reshape(groups * 2 * states, LANES)

    local = pl.pallas_call(
        conv_kernel,
        out_shape=shape(tokens * groups, LANES),
        scratch_shapes=[rows(tokens), rows(tokens + 8)],
        compiler_params=params,
        cost_estimate=pl.CostEstimate(flops=18_000_000, bytes_accessed=2_000_000, transcendentals=0),
        name="conv",
    )(signal, taps, skip_gain.reshape(groups, LANES))

    outputs = pl.pallas_call(
        final_kernel,
        out_shape=shape(tokens, channels),
        scratch_shapes=[rows(states * 2 * NEAR), rows(states * 2 * outer), rows(tokens)],
        compiler_params=params,
        cost_estimate=pl.CostEstimate(flops=20_000_000, bytes_accessed=2_000_000, transcendentals=0),
        name="final",
    )(local, seeds, entering)
    return outputs[None]


def solution(mesh):
    in_specs = (
        P(("groups", "seqout"), "seqin", "chan"),
        P("chan"),
        P(None, "chan"),
        P(None, "chan"),
        P(None, "chan"),
        P(None, "chan"),
        P("chan"),
    )
    out_specs = P(("groups", "seqout"), "seqin", "chan")
    return jax.shard_map(
        functools.partial(per_device, mesh.shape["seqin"], mesh.shape["seqout"]),
        mesh=mesh,
        in_specs=in_specs,
        out_specs=out_specs,
        check_vma=False,
    )
```

```python
import functools

import jax
import jax.numpy as jnp
from jax import lax
from jax.experimental import pallas as pl
from jax.experimental.pallas import tpu as pltpu
from jax.sharding import PartitionSpec as P

LANES = 128
NEAR = 16
FINAL_NEAR = 8
SEQ_AXES = ("seqin", "seqout")


def cmul(a, b):
    return (a[0] * b[0] - a[1] * b[1], a[0] * b[1] + a[1] * b[0])


def cos_sin(angle):
    turns = jnp.floor(angle * 0.6366197723675814 + 0.5)
    rest = angle - turns * 1.5703125
    rest = rest - turns * 4.837512969970703125e-4
    rest = rest - turns * 7.549789948768648e-8
    square = rest * rest
    sine = rest + rest * square * (
        -1.6666654611e-1 + square * (8.3321608736e-3 - square * 1.9515295891e-4)
    )
    cosine = (
        1.0
        - 0.5 * square
        + square * square * (4.166664568298827e-2 + square * (-1.388731625493765e-3 + square * 2.443315711809948e-5))
    )
    quarter = turns.astype(jnp.int32) & 3
    swap = (quarter & 1) == 1
    first = jnp.where(swap, sine, cosine)
    second = jnp.where(swap, cosine, sine)
    return (
        jnp.where((quarter == 1) | (quarter == 2), -first, first),
        jnp.where(quarter >= 2, -second, second),
    )


def decay_step(time_step, decay_rate, frequency):
    fade_rate = time_step * decay_rate
    shrink = jnp.exp(-fade_rate)
    cosine, sine = cos_sin(time_step * frequency)
    return (fade_rate, (shrink * cosine, shrink * sine))


def gain_of(fade_rate):
    double = 2.0 * fade_rate
    series = 1.0 / 40320.0
    for factor in (5040.0, 720.0, 120.0, 24.0, 6.0, 2.0, 1.0):
        series = 1.0 / factor - double * series
    small = double * series
    return jnp.sqrt(jnp.where(double < 0.25, small, 1.0 - jnp.exp(-double)))


def power_list(lam, count):
    powers = [None, lam]
    for k in range(2, count + 1):
        powers.append(cmul(powers[k // 2], powers[k - k // 2]))
    return powers


def spread_rows(source_ref, target_ref, rows, groups, stack):
    for start in range(0, rows, stack):
        for k in range(groups):
            part = source_ref[start : start + stack, k * LANES : (k + 1) * LANES]
            target_ref[pl.ds(start * groups + k, stack, stride=groups), :] = part.astype(jnp.float32)


def row_at(ref, index, groups):
    return ref[pl.ds(pl.multiple_of(index * groups, groups), groups), :]


def put_row(ref, index, groups, value):
    ref[pl.ds(pl.multiple_of(index * groups, groups), groups), :] = value


def power_sum(near_ref, lead_of, states, groups, near, count, init):

    def turn(n, acc):
        leads = lead_of(n)
        acc = list(acc)
        for a in range(count):
            acc[a * near] = acc[a * near] + leads[a][0]
        for u in range(1, near):
            real = row_at(near_ref, n * (2 * near) + 2 * u, groups)
            imag = row_at(near_ref, n * (2 * near) + 2 * u + 1, groups)
            for a in range(count):
                slot = a * near + u
                acc[slot] = acc[slot] + (leads[a][0] * real - leads[a][1] * imag)
        return tuple(acc)

    return lax.fori_loop(0, states, turn, tuple(init), unroll=16)


def split_kernel(signal_ref, out_ref, sems):
    parts, _, width = out_ref.shape
    copies = [
        pltpu.make_async_copy(signal_ref.at[:, pl.ds(k * width, width)], out_ref.at[k], sems.at[k])
        for k in range(parts)
    ]
    for copy in copies:
        copy.start()
    for copy in copies:
        copy.wait()


def tables_kernel(
    width, step_hbm, decay_hbm, freq_hbm, real_hbm, imag_hbm,
    pack_ref, mid_ref,
    step_ref, decay_ref, freq_ref, real_ref, imag_ref,
    decay_sp, freq_sp, real_sp, imag_sp, near_ref, lead_ref, sems,
):
    pairs = (
        (step_hbm, step_ref), (decay_hbm, decay_ref), (freq_hbm, freq_ref), (real_hbm, real_ref), (imag_hbm, imag_ref),
    )
    copies = [pltpu.make_async_copy(pair[0], pair[1], sems.at[i]) for i, pair in enumerate(pairs)]
    for copy in copies:
        copy.start()
    for copy in copies:
        copy.wait()
    states = decay_ref.shape[0]
    groups = decay_ref.shape[1] // LANES
    tokens = pack_ref.shape[0] // groups - 4 * states
    outer = tokens // NEAR
    taps_ref = pack_ref.at[0 : tokens * groups]
    seed_ref = pack_ref.at[tokens * groups : (tokens + 4 * states) * groups]
    if width == LANES:
        place = lax.axis_index("seqin") * lax.axis_size("seqout") + lax.axis_index("seqout")
        own = pl.ds(pl.multiple_of(place * LANES, LANES), LANES)
        fade, lam = decay_step(step_ref[pl.ds(place, 1), :], decay_ref[:, own], freq_ref[:, own])
        mid_ref[0:states, :] = lam[0]
        mid_ref[states : 2 * states, :] = lam[1]
        mid_ref[2 * states : 3 * states, :] = gain_of(fade)
    for source, target in ((decay_ref, decay_sp), (freq_ref, freq_sp), (real_ref, real_sp), (imag_ref, imag_sp)):
        spread_rows(source, target, states, groups, 8)
    step = step_ref[...]

    def prepare(n, carry):
        fade, lam = decay_step(step, row_at(decay_sp, n, groups), row_at(freq_sp, n, groups))
        powers = power_list(lam, NEAR)
        for u in range(1, NEAR):
            for part in range(2):
                put_row(near_ref, n * (2 * NEAR) + 2 * u + part, groups, powers[u][part])
        weight = (2.0 * row_at(real_sp, n, groups), 2.0 * row_at(imag_sp, n, groups))
        gain = gain_of(fade)
        lead = (weight[0] * gain, weight[1] * gain)
        for part in range(2):
            put_row(seed_ref, 4 * n + part, groups, lam[part])
            put_row(seed_ref, 4 * n + 2 + part, groups, weight[part])
        for a in range(outer):
            if a:
                lead = cmul(lead, powers[NEAR])
            for part in range(2):
                put_row(lead_ref, n * (2 * outer) + 2 * a + part, groups, lead[part])
        return carry

    lax.fori_loop(0, states, prepare, 0)
    zero = jnp.zeros((groups, LANES), jnp.float32)

    count = min(2, outer)
    for first in range(0, outer, count):

        def lead_of(n, first=first):
            return [
                tuple(row_at(lead_ref, n * (2 * outer) + 2 * (first + a) + part, groups) for part in range(2))
                for a in range(count)
            ]

        acc = power_sum(near_ref, lead_of, states, groups, NEAR, count, [zero] * (count * NEAR))
        for t in range(count * NEAR):
            row = (first * NEAR + t) * groups
            taps_ref[row : row + groups, :] = acc[t]


def split_pack(pack_ref, tokens, states, groups):
    first = tokens * groups
    second = first + states * 2 * FINAL_NEAR * groups
    return (pack_ref.at[0:first], pack_ref.at[first:second], pack_ref.at[second : second + 2 * states * groups])


def conv_kernel(
    signal_hbm, skip_hbm, given_ref, pack_ref, signal_ref, skip_ref, signal_sp, taps_pad, sems
):
    copies = [
        pltpu.make_async_copy(pair[0], pair[1], sems.at[i])
        for i, pair in enumerate(((signal_hbm, signal_ref), (skip_hbm, skip_ref)))
    ]
    for copy in copies:
        copy.start()
    tokens, channels = signal_ref.shape
    groups = channels // LANES
    states = (given_ref.shape[0] // groups - tokens) // 4
    taps_ref = given_ref.at[0 : tokens * groups]
    seed_ref = given_ref.at[tokens * groups : (tokens + 4 * states) * groups]
    out_ref, near_ref, lead_ref = split_pack(pack_ref, tokens, states, groups)
    tile = 8

    def prepare(n, carry):
        lam, weight = (tuple(row_at(seed_ref, 4 * n + 2 * i + part, groups) for part in range(2)) for i in range(2))
        powers = power_list(lam, FINAL_NEAR)
        powers[0] = powers[FINAL_NEAR]
        lead = cmul(weight, lam)
        for part in range(2):
            put_row(lead_ref, 2 * n + part, groups, lead[part])
            for u in range(FINAL_NEAR):
                put_row(near_ref, n * (2 * FINAL_NEAR) + 2 * u + part, groups, powers[u][part])
        return carry

    lax.fori_loop(0, states, prepare, 0)
    for copy in copies:
        copy.wait()
    spread_rows(signal_ref, signal_sp, tokens, groups, 16)
    taps_pad[0 : tile * groups, :] = jnp.zeros((tile * groups, LANES), jnp.float32)
    taps_pad[tile * groups : (tile + tokens) * groups, :] = taps_ref[...]
    skip = skip_ref[...]

    def row_tile(ti, carry):
        def col_tile(ji, acc):
            gap = (ti - ji) * tile + 1
            window = [row_at(taps_pad, gap + m, groups) for m in range(2 * tile - 1)]
            acc = list(acc)
            for j in range(tile):
                drive = row_at(signal_sp, ji * tile + j, groups)
                for t in range(tile):
                    acc[t] = acc[t] + window[t - j + tile - 1] * drive
            return tuple(acc)

        init = tuple(skip * row_at(signal_sp, ti * tile + t, groups) for t in range(tile))
        acc = lax.fori_loop(0, ti + 1, col_tile, init)
        for t in range(tile):
            put_row(out_ref, ti * tile + t, groups, acc[t])
        return carry

    lax.fori_loop(0, tokens // tile, row_tile, 0)


def states_kernel(n_in, n_out, tokens, signal_ref, mid_ref, out_ref, signal_f, near_ref, out_buf, sems):
    states = mid_ref.shape[0] // 3
    width = mid_ref.shape[1]
    parts = n_in * n_out
    a_tile = 4
    signal_f[...] = signal_ref[...].astype(jnp.float32)
    lam = (mid_ref[0:states, :], mid_ref[states : 2 * states, :])
    gain = mid_ref[2 * states : 3 * states, :]
    powers = power_list(lam, NEAR)
    for u in range(1, NEAR):
        for part in range(2):
            near_ref[2 * u + part] = powers[u][part]
    hops = [None, powers[NEAR]]
    for a in range(2, a_tile + 1):
        hops.append(cmul(hops[a // 2], hops[a - a // 2]))

    def advance(base, state):
        real = [None] * a_tile
        imag = [None] * a_tile
        for u in range(NEAR):
            drive = [
                jnp.broadcast_to(signal_f[pl.ds(base + a * NEAR + u, 1), :], (states, width))
                for a in range(a_tile)
            ]
            power = NEAR - 1 - u
            if power:
                near_real, near_imag = near_ref[2 * power], near_ref[2 * power + 1]
            for a in range(a_tile):
                if power:
                    add_real, add_imag = near_real * drive[a], near_imag * drive[a]
                    real[a] = add_real if real[a] is None else real[a] + add_real
                    imag[a] = add_imag if imag[a] is None else imag[a] + add_imag
                else:
                    real[a] = real[a] + drive[a]
        total = (real[a_tile - 1], imag[a_tile - 1])
        for a in range(a_tile - 1):
            moved = cmul(hops[a_tile - 1 - a], (real[a], imag[a]))
            total = (total[0] + moved[0], total[1] + moved[1])
        moved = cmul(hops[a_tile], state)
        return (moved[0] + total[0], moved[1] + total[1])

    def place_of(s):
        return lax.rem(s, n_in) * n_out + s // n_in

    def copy_of(s):
        place = place_of(s)
        return pltpu.make_async_copy(out_buf.at[s], out_ref.at[place], sems.at[s])

    def send(s, state):
        out_buf[s, 0:states, :] = gain * state[0]
        out_buf[s, states : 2 * states, :] = gain * state[1]
        copy_of(s).start()

    zero = jnp.zeros((states, width), jnp.float32)
    send(0, (zero, zero))

    def part_turn(s, state):
        for i in range(tokens // (NEAR * a_tile)):
            base = pl.multiple_of(place_of(s - 1) * tokens + i * (a_tile * NEAR), a_tile * NEAR)
            state = advance(base, state)
        send(s, state)
        return state

    lax.fori_loop(1, parts, part_turn, (zero, zero), unroll=min(7, parts - 1))

    def finish(s, carry):
        copy_of(s).wait()
        return carry

    lax.fori_loop(0, parts, finish, 0)


def final_kernel(pack_ref, state_ref, out_ref, state_sp, rows_ref, out_buf, sems):
    tokens, channels = out_ref.shape
    groups = channels // LANES
    near = FINAL_NEAR
    outer = tokens // near
    states = state_ref.shape[0] // (2 * groups)
    local_ref, near_ref, lead_ref = split_pack(pack_ref, tokens, states, groups)

    def pair_at(ref, index):
        return tuple(row_at(ref, index + part, groups) for part in range(2))

    for n in range(states):
        entering = tuple(state_ref[pl.ds(n + part * states, groups, stride=2 * states), :] for part in range(2))
        lead = cmul(pair_at(lead_ref, 2 * n), entering)
        for part in range(2):
            put_row(state_sp, 2 * n + part, groups, lead[part])

    count = min(4, outer)
    span = count * near
    copies = []
    for index in range(outer // count):
        last = index + 1 == outer // count

        def lead_of(n, last=last):
            hop = pair_at(near_ref, n * (2 * near))
            leads = [pair_at(state_sp, 2 * n)]
            for _ in range(count - 1 if last else count):
                leads.append(cmul(leads[-1], hop))
            if not last:
                for part in range(2):
                    put_row(state_sp, 2 * n + part, groups, leads[count][part])
            return leads

        start = index * span
        init = [local_ref[(start + t) * groups : (start + t + 1) * groups, :] for t in range(span)]
        acc = power_sum(near_ref, lead_of, states, groups, near, count, init)
        for t in range(span):
            rows_ref[t * groups : (t + 1) * groups, :] = acc[t]
        for t in range(0, span, 8):
            for k in range(groups):
                out_buf[start + t : start + t + 8, k * LANES : (k + 1) * LANES] = rows_ref[
                    pl.ds(t * groups + k, 8, stride=groups), :
                ]
        copy = pltpu.make_async_copy(
            out_buf.at[pl.ds(start, span)], out_ref.at[pl.ds(start, span)], sems.at[index]
        )
        copy.start()
        copies.append(copy)
    for copy in copies:
        copy.wait()


def per_device(n_in, n_out, inputs, time_step, decay_rate, frequency, output_real, output_imag, skip_gain):
    signal = inputs[0]
    tokens, channels = signal.shape
    states = decay_rate.shape[0]
    groups = channels // LANES
    parts = n_in * n_out
    width = channels // parts
    outer = tokens // NEAR
    f32 = jnp.float32

    def hbm(array):
        return pltpu.with_memory_space_constraint(array, pltpu.HBM)

    def params(mebibytes):
        return pltpu.CompilerParams(vmem_limit_bytes=mebibytes * 1024 * 1024)

    def rows(count, dtype=f32):
        return pltpu.VMEM((count * groups, LANES), dtype)

    def shape(*dims):
        return jax.ShapeDtypeStruct(dims, f32)

    if width == LANES:
        tiled = pl.pallas_call(
            split_kernel,
            out_shape=pltpu.VMEM((parts, tokens, width), signal.dtype),
            in_specs=[pl.BlockSpec(memory_space=pl.ANY)],
            out_specs=pl.BlockSpec(memory_space=pltpu.VMEM),
            scratch_shapes=[pltpu.SemaphoreType.DMA((parts,))],
            compiler_params=params(2),
            name="split",
        )(hbm(signal))
    else:
        tiled = signal.reshape(tokens, parts, width).transpose(1, 0, 2)
    whole = lax.all_to_all(tiled, SEQ_AXES, split_axis=0, concat_axis=0, tiled=True)
    whole = whole.reshape(parts * tokens, width)

    given, mid = pl.pallas_call(
        functools.partial(tables_kernel, width),
        out_shape=(
            shape((tokens + states * 4) * groups, LANES),
            shape(3 * states, LANES),
        ),
        in_specs=[pl.BlockSpec(memory_space=pl.ANY)] * 5,
        scratch_shapes=[
            rows(1),
            *[pltpu.VMEM((states, channels), f32)] * 4,
            *[rows(states)] * 4,
            rows(states * 2 * NEAR),
            rows(states * 2 * outer),
            pltpu.SemaphoreType.DMA((5,)),
        ],
        compiler_params=params(40),
        cost_estimate=pl.CostEstimate(flops=20_000_000, bytes_accessed=2_000_000, transcendentals=40_000),
        name="tables",
    )(*(hbm(array) for array in (time_step.reshape(groups, LANES), decay_rate, frequency, output_real, output_imag)))

    if width != LANES:
        place = lax.axis_index("seqin") * n_out + lax.axis_index("seqout")

        def own(array):
            return lax.dynamic_slice_in_dim(array, place * width, width, array.ndim - 1)

        fade, lam = decay_step(own(time_step)[None, :], own(decay_rate), own(frequency))
        mid = jnp.concatenate([lam[0], lam[1], gain_of(fade)], axis=0)

    entering = pl.pallas_call(
        functools.partial(states_kernel, n_in, n_out, tokens),
        out_shape=shape(parts, 2 * states, width),
        out_specs=pl.BlockSpec(memory_space=pl.ANY),
        scratch_shapes=[
            pltpu.VMEM((parts * tokens, width), f32),
            pltpu.VMEM((2 * NEAR, states, width), f32),
            pltpu.VMEM((parts, 2 * states, width), f32),
            pltpu.SemaphoreType.DMA((parts,)),
        ],
        compiler_params=params(40),
        cost_estimate=pl.CostEstimate(flops=16_000_000, bytes_accessed=1_000_000, transcendentals=0),
        name="states",
    )(whole, mid)

    given, entering = lax.optimization_barrier((given, entering))
    entering = lax.all_to_all(entering, SEQ_AXES, split_axis=0, concat_axis=0, tiled=True)
    if width != LANES:
        entering = entering.transpose(1, 0, 2).reshape(2 * states, groups, LANES).transpose(1, 0, 2)
    entering = entering.reshape(groups * 2 * states, LANES)

    pack = pl.pallas_call(
        conv_kernel,
        out_shape=shape((tokens + states * 2 * FINAL_NEAR + states * 2) * groups, LANES),
        in_specs=[
            pl.BlockSpec(memory_space=pl.ANY),
            pl.BlockSpec(memory_space=pl.ANY),
            pl.BlockSpec(memory_space=pltpu.VMEM),
        ],
        scratch_shapes=[
            pltpu.VMEM((tokens, channels), signal.dtype),
            rows(1),
            rows(tokens),
            rows(tokens + 8),
            pltpu.SemaphoreType.DMA((2,)),
        ],
        compiler_params=params(40),
        cost_estimate=pl.CostEstimate(flops=18_000_000, bytes_accessed=2_000_000, transcendentals=0),
        name="conv",
    )(hbm(signal), hbm(skip_gain.reshape(groups, LANES)), given)

    count = min(4, tokens // FINAL_NEAR)
    outputs = pl.pallas_call(
        final_kernel,
        out_shape=shape(tokens, channels),
        out_specs=pl.BlockSpec(memory_space=pl.ANY),
        scratch_shapes=[
            rows(2 * states),
            rows(count * FINAL_NEAR),
            pltpu.VMEM((tokens, channels), f32),
            pltpu.SemaphoreType.DMA((tokens // FINAL_NEAR // count,)),
        ],
        compiler_params=params(40),
        cost_estimate=pl.CostEstimate(flops=20_000_000, bytes_accessed=2_000_000, transcendentals=0),
        name="final",
    )(pack, entering)
    return outputs[None]


def solution(mesh):
    in_specs = (
        P(("groups", "seqout"), "seqin", "chan"),
        P("chan"),
        P(None, "chan"),
        P(None, "chan"),
        P(None, "chan"),
        P(None, "chan"),
        P("chan"),
    )
    out_specs = P(("groups", "seqout"), "seqin", "chan")
    return jax.shard_map(
        functools.partial(per_device, mesh.shape["seqin"], mesh.shape["seqout"]),
        mesh=mesh,
        in_specs=in_specs,
        out_specs=out_specs,
        check_vma=False,
    )
```

```python
import functools

import jax
import jax.numpy as jnp
from jax import lax
from jax.experimental import pallas as pl
from jax.experimental.pallas import tpu as pltpu
from jax.sharding import PartitionSpec as P

LANES = 128
NEAR = 16
FINAL_NEAR = 8
HALF_RANGE = 125.0
LOG_TWO = 0.6931471805599453
SCALE_ROWS = 8
SEQ_AXES = ("seqin", "seqout")


def cmul(a, b):
    return (a[0] * b[0] - a[1] * b[1], a[0] * b[1] + a[1] * b[0])


def cos_sin(angle):
    turns = jnp.floor(angle * 0.6366197723675814 + 0.5)
    rest = angle - turns * 1.5703125
    rest = rest - turns * 4.837512969970703125e-4
    rest = rest - turns * 7.549789948768648e-8
    square = rest * rest
    sine = rest + rest * square * (
        -1.6666654611e-1 + square * (8.3321608736e-3 - square * 1.9515295891e-4)
    )
    cosine = (
        1.0
        - 0.5 * square
        + square * square * (4.166664568298827e-2 + square * (-1.388731625493765e-3 + square * 2.443315711809948e-5))
    )
    quarter = turns.astype(jnp.int32) & 3
    swap = (quarter & 1) == 1
    first = jnp.where(swap, sine, cosine)
    second = jnp.where(swap, cosine, sine)
    return (
        jnp.where((quarter == 1) | (quarter == 2), -first, first),
        jnp.where(quarter >= 2, -second, second),
    )


def decay_step(time_step, decay_rate, frequency):
    fade_rate = time_step * decay_rate
    shrink = jnp.exp(-fade_rate)
    cosine, sine = cos_sin(time_step * frequency)
    return (fade_rate, (shrink * cosine, shrink * sine))


def gain_of(fade_rate):
    double = 2.0 * fade_rate
    series = 1.0 / 40320.0
    for factor in (5040.0, 720.0, 120.0, 24.0, 6.0, 2.0, 1.0):
        series = 1.0 / factor - double * series
    small = double * series
    return jnp.sqrt(jnp.where(double < 0.25, small, 1.0 - jnp.exp(-double)))


def power_list(lam, count):
    powers = [None, lam]
    for k in range(2, count + 1):
        powers.append(cmul(powers[k // 2], powers[k - k // 2]))
    return powers


def spread_rows(source_ref, target_ref, rows, groups, stack):
    for start in range(0, rows, stack):
        for k in range(groups):
            part = source_ref[start : start + stack, k * LANES : (k + 1) * LANES]
            target_ref[pl.ds(start * groups + k, stack, stride=groups), :] = part.astype(jnp.float32)


def row_at(ref, index, groups):
    return ref[pl.ds(pl.multiple_of(index * groups, groups), groups), :]


def put_row(ref, index, groups, value):
    ref[pl.ds(pl.multiple_of(index * groups, groups), groups), :] = value


def power_sum(near_ref, lead_of, states, groups, near, count, init):

    def turn(n, acc):
        leads = lead_of(n)
        acc = list(acc)
        for a in range(count):
            acc[a * near] = acc[a * near] + leads[a][0]
        for u in range(1, near):
            real = row_at(near_ref, n * (2 * near) + 2 * u, groups)
            imag = row_at(near_ref, n * (2 * near) + 2 * u + 1, groups)
            for a in range(count):
                slot = a * near + u
                acc[slot] = acc[slot] + (leads[a][0] * real - leads[a][1] * imag)
        return tuple(acc)

    return lax.fori_loop(0, states, turn, tuple(init), unroll=16)


def split_kernel(signal_ref, out_ref, buf, in_sems, out_sems):
    parts, _, width = out_ref.shape
    loads, stores = [], []
    for k in range(parts):
        load = pltpu.make_async_copy(signal_ref.at[:, pl.ds(k * width, width)], buf.at[k], in_sems.at[k])
        load.start()
        loads.append(load)
    for k in range(parts):
        loads[k].wait()
        store = pltpu.make_async_copy(buf.at[k], out_ref.at[k], out_sems.at[k])
        store.start()
        stores.append(store)
    for store in stores:
        store.wait()


def tables_kernel(
    width, step_hbm, decay_hbm, freq_hbm, real_hbm, imag_hbm,
    taps_hbm, seed_hbm, mid_ref,
    taps_ref, seed_ref, step_ref, decay_ref, freq_ref, real_ref, imag_ref,
    decay_sp, freq_sp, real_sp, imag_sp, near_ref, lead_ref, sems,
):
    pairs = (
        (step_hbm, step_ref), (decay_hbm, decay_ref), (freq_hbm, freq_ref), (real_hbm, real_ref), (imag_hbm, imag_ref),
    )
    copies = [pltpu.make_async_copy(pair[0], pair[1], sems.at[i]) for i, pair in enumerate(pairs)]
    for copy in copies:
        copy.start()
    for copy in copies:
        copy.wait()
    states = decay_ref.shape[0]
    groups = decay_ref.shape[1] // LANES
    tokens = taps_ref.shape[0] // groups
    outer = tokens // NEAR
    if width == LANES:
        place = lax.axis_index("seqin") * lax.axis_size("seqout") + lax.axis_index("seqout")
        own = pl.ds(pl.multiple_of(place * LANES, LANES), LANES)
        fade, lam = decay_step(step_ref[pl.ds(place, 1), :], decay_ref[:, own], freq_ref[:, own])
        mid_ref[0:states, :] = lam[0]
        mid_ref[states : 2 * states, :] = lam[1]
        mid_ref[2 * states : 3 * states, :] = gain_of(fade)
    for source, target in ((decay_ref, decay_sp), (freq_ref, freq_sp), (real_ref, real_sp), (imag_ref, imag_sp)):
        spread_rows(source, target, states, groups, 8)
    step = step_ref[...]

    def prepare(n, carry):
        fade, lam = decay_step(step, row_at(decay_sp, n, groups), row_at(freq_sp, n, groups))
        powers = power_list(lam, NEAR)
        for u in range(1, NEAR):
            for part in range(2):
                put_row(near_ref, n * (2 * NEAR) + 2 * u + part, groups, powers[u][part])
        weight = (2.0 * row_at(real_sp, n, groups), 2.0 * row_at(imag_sp, n, groups))
        gain = gain_of(fade)
        lead = (weight[0] * gain, weight[1] * gain)
        for part in range(2):
            put_row(seed_ref, 4 * n + part, groups, lam[part])
            put_row(seed_ref, 4 * n + 2 + part, groups, weight[part])
        for a in range(outer):
            if a:
                lead = cmul(lead, powers[NEAR])
            for part in range(2):
                put_row(lead_ref, n * (2 * outer) + 2 * a + part, groups, lead[part])
        return carry

    lax.fori_loop(0, states, prepare, 0)
    copies = [pltpu.make_async_copy(seed_ref, seed_hbm, sems.at[0])]
    copies[0].start()
    zero = jnp.zeros((groups, LANES), jnp.float32)

    count = min(2, outer)
    for first in range(0, outer, count):

        def lead_of(n, first=first):
            return [
                tuple(row_at(lead_ref, n * (2 * outer) + 2 * (first + a) + part, groups) for part in range(2))
                for a in range(count)
            ]

        acc = power_sum(near_ref, lead_of, states, groups, NEAR, count, [zero] * (count * NEAR))
        for t in range(count * NEAR):
            row = (first * NEAR + t) * groups
            taps_ref[row : row + groups, :] = acc[t]
        part = pl.ds(first * NEAR * groups, count * NEAR * groups)
        copies.append(pltpu.make_async_copy(taps_ref.at[part], taps_hbm.at[part], sems.at[len(copies)]))
        copies[-1].start()
    for copy in copies:
        copy.wait()


def split_pack(pack_ref, tokens, states, groups):
    first = tokens * groups
    second = first + states * 2 * FINAL_NEAR * groups
    return (pack_ref.at[0:first], pack_ref.at[first:second], pack_ref.at[second : second + 2 * states * groups])


def conv_kernel(
    signal_hbm, skip_hbm, taps_hbm, seed_hbm, pack_ref, signal_ref, skip_ref, seed_ref, signal_sp, taps_pad, sems
):
    tokens, channels = signal_ref.shape
    groups = channels // LANES
    states = seed_ref.shape[0] // (4 * groups)
    tile = 8
    copies = [
        pltpu.make_async_copy(pair[0], pair[1], sems.at[i])
        for i, pair in enumerate((
            (seed_hbm, seed_ref),
            (signal_hbm, signal_ref),
            (skip_hbm, skip_ref),
            (taps_hbm, taps_pad.at[tile * groups : (tile + tokens) * groups]),
        ))
    ]
    for copy in copies:
        copy.start()
    out_ref, near_ref, lead_ref = split_pack(pack_ref, tokens, states, groups)
    taps_pad[0 : tile * groups, :] = jnp.zeros((tile * groups, LANES), jnp.float32)
    copies[0].wait()

    def prepare(n, carry):
        lam, weight = (tuple(row_at(seed_ref, 4 * n + 2 * i + part, groups) for part in range(2)) for i in range(2))
        powers = power_list(lam, FINAL_NEAR)
        powers[0] = powers[FINAL_NEAR]
        lead = cmul(weight, lam)
        for part in range(2):
            put_row(lead_ref, 2 * n + part, groups, lead[part])
            for u in range(FINAL_NEAR):
                put_row(near_ref, n * (2 * FINAL_NEAR) + 2 * u + part, groups, powers[u][part])
        return carry

    lax.fori_loop(0, states, prepare, 0)
    for copy in copies[1:]:
        copy.wait()
    spread_rows(signal_ref, signal_sp, tokens, groups, 16)
    skip = skip_ref[...]

    def col_tile(ji, acc, ti):
        gap = (ti - ji) * tile + 1
        window = [row_at(taps_pad, gap + m, groups) for m in range(2 * tile - 1)]
        acc = list(acc)
        for j in range(tile):
            drive = row_at(signal_sp, ji * tile + j, groups)
            for t in range(tile):
                acc[t] = acc[t] + window[t - j + tile - 1] * drive
        return tuple(acc)

    for ti in range(tokens // tile):
        init = tuple(skip * row_at(signal_sp, ti * tile + t, groups) for t in range(tile))
        acc = lax.fori_loop(0, ti + 1, functools.partial(col_tile, ti=ti), init, unroll=4)
        for t in range(tile):
            put_row(out_ref, ti * tile + t, groups, acc[t])


def encode(value, inverse):
    code = jnp.exp2(jnp.abs(value) * inverse * (2.0 * HALF_RANGE) - HALF_RANGE)
    return jnp.where(value < 0.0, -code, code).astype(jnp.bfloat16)


def decode(code, scale):
    size = (jnp.log(jnp.abs(code)) * (0.5 / HALF_RANGE / LOG_TWO) + 0.5) * scale
    return jnp.where(code < 0.0, -size, size)


def states_kernel(n_in, n_out, tokens, signal_ref, mid_ref, out_ref, signal_f, near_ref, out_buf, sems):
    states = mid_ref.shape[0] // 3
    width = mid_ref.shape[1]
    parts = n_in * n_out
    a_tile = 4
    lam = (mid_ref[0:states, :], mid_ref[states : 2 * states, :])
    gain = mid_ref[2 * states : 3 * states, :]
    powers = power_list(lam, NEAR)
    for u in range(1, NEAR):
        for part in range(2):
            near_ref[2 * u + part] = powers[u][part]
    hops = [None, powers[NEAR]]
    for a in range(2, a_tile + 1):
        hops.append(cmul(hops[a // 2], hops[a - a // 2]))

    def advance(base, state):
        real = [None] * a_tile
        imag = [None] * a_tile
        for u in range(NEAR):
            drive = [
                jnp.broadcast_to(signal_f[pl.ds(base + a * NEAR + u, 1), :], (states, width))
                for a in range(a_tile)
            ]
            power = NEAR - 1 - u
            if power:
                near_real, near_imag = near_ref[2 * power], near_ref[2 * power + 1]
            for a in range(a_tile):
                if power:
                    add_real, add_imag = near_real * drive[a], near_imag * drive[a]
                    real[a] = add_real if real[a] is None else real[a] + add_real
                    imag[a] = add_imag if imag[a] is None else imag[a] + add_imag
                else:
                    real[a] = real[a] + drive[a]
        total = (real[a_tile - 1], imag[a_tile - 1])
        for a in range(a_tile - 1):
            moved = cmul(hops[a_tile - 1 - a], (real[a], imag[a]))
            total = (total[0] + moved[0], total[1] + moved[1])
        moved = cmul(hops[a_tile], state)
        return (moved[0] + total[0], moved[1] + total[1])

    def place_of(s):
        if isinstance(s, int):
            return s % n_in * n_out + s // n_in
        return lax.rem(s, n_in) * n_out + s // n_in

    def copy_of(s):
        place = place_of(s)
        return pltpu.make_async_copy(out_buf.at[s], out_ref.at[place], sems.at[s])

    def send(s, state):
        entering = (gain * state[0], gain * state[1])
        top = jnp.max(jnp.maximum(jnp.abs(entering[0]), jnp.abs(entering[1])), axis=0, keepdims=True)
        scale = (1.01 * top).astype(jnp.bfloat16)
        wide = scale.astype(jnp.float32)
        inverse = jnp.where(wide > 1e-36, 1.0 / jnp.maximum(wide, 1e-36), 0.0)
        for part in range(2):
            out_buf[s, part * states : (part + 1) * states, :] = encode(entering[part], inverse)
        out_buf[s, 2 * states :, :] = jnp.broadcast_to(wide, (SCALE_ROWS, width)).astype(jnp.bfloat16)
        copy_of(s).start()

    zero = jnp.zeros((states, width), jnp.float32)
    out_buf[0, 0 : 2 * states, :] = jnp.ones((2 * states, width), jnp.bfloat16)
    out_buf[0, 2 * states :, :] = jnp.zeros((SCALE_ROWS, width), jnp.bfloat16)
    copy_of(0).start()

    def part_turn(s, state):
        start = place_of(s - 1) * tokens
        if not isinstance(s, int):
            start = pl.multiple_of(start, tokens)
        signal_f[pl.ds(start, tokens), :] = signal_ref[pl.ds(start, tokens), :].astype(jnp.float32)
        for i in range(tokens // (NEAR * a_tile)):
            state = advance(start + i * (a_tile * NEAR), state)
        send(s, state)
        return state

    if parts <= 8:
        state = (zero, zero)
        for s in range(1, parts):
            state = part_turn(s, state)
        for s in range(parts):
            copy_of(s).wait()
        return

    lax.fori_loop(1, parts, part_turn, (zero, zero))

    def finish(s, carry):
        copy_of(s).wait()
        return carry

    lax.fori_loop(0, parts, finish, 0)


def final_kernel(states, pack_ref, code_ref, out_ref, state_ref, state_sp, rows_ref, out_buf, sems):
    tokens, channels = out_ref.shape
    groups = channels // LANES
    near = FINAL_NEAR
    outer = tokens // near
    local_ref, near_ref, lead_ref = split_pack(pack_ref, tokens, states, groups)

    def pair_at(ref, index):
        return tuple(row_at(ref, index + part, groups) for part in range(2))

    stride = 2 * states + SCALE_ROWS
    for k in range(groups):
        code = code_ref[k * stride : (k + 1) * stride, :].astype(jnp.float32)
        state_ref[k * 2 * states : (k + 1) * 2 * states, :] = decode(
            code[0 : 2 * states, :], code[2 * states : 2 * states + 1, :]
        )
    for n in range(states):
        entering = tuple(state_ref[pl.ds(n + part * states, groups, stride=2 * states), :] for part in range(2))
        lead = cmul(pair_at(lead_ref, 2 * n), entering)
        for part in range(2):
            put_row(state_sp, 2 * n + part, groups, lead[part])

    count = min(4, outer)
    span = count * near
    copies = []
    for index in range(outer // count):
        last = index + 1 == outer // count

        def lead_of(n, last=last):
            hop = pair_at(near_ref, n * (2 * near))
            leads = [pair_at(state_sp, 2 * n)]
            for _ in range(count - 1 if last else count):
                leads.append(cmul(leads[-1], hop))
            if not last:
                for part in range(2):
                    put_row(state_sp, 2 * n + part, groups, leads[count][part])
            return leads

        start = index * span
        init = [local_ref[(start + t) * groups : (start + t + 1) * groups, :] for t in range(span)]
        acc = power_sum(near_ref, lead_of, states, groups, near, count, init)
        for t in range(span):
            rows_ref[t * groups : (t + 1) * groups, :] = acc[t]
        for t in range(0, span, 8):
            for k in range(groups):
                out_buf[start + t : start + t + 8, k * LANES : (k + 1) * LANES] = rows_ref[
                    pl.ds(t * groups + k, 8, stride=groups), :
                ]
        copy = pltpu.make_async_copy(
            out_buf.at[pl.ds(start, span)], out_ref.at[pl.ds(start, span)], sems.at[index]
        )
        copy.start()
        copies.append(copy)
    for copy in copies:
        copy.wait()


def per_device(n_in, n_out, inputs, time_step, decay_rate, frequency, output_real, output_imag, skip_gain):
    signal = inputs[0]
    tokens, channels = signal.shape
    states = decay_rate.shape[0]
    groups = channels // LANES
    parts = n_in * n_out
    width = channels // parts
    outer = tokens // NEAR
    f32 = jnp.float32
    code_rows = 2 * states + SCALE_ROWS

    def hbm(array):
        return pltpu.with_memory_space_constraint(array, pltpu.HBM)

    def params(mebibytes):
        return pltpu.CompilerParams(vmem_limit_bytes=mebibytes * 1024 * 1024)

    def rows(count, dtype=f32):
        return pltpu.VMEM((count * groups, LANES), dtype)

    def shape(*dims):
        return jax.ShapeDtypeStruct(dims, f32)

    if width == LANES:
        tiled = pl.pallas_call(
            split_kernel,
            out_shape=jax.ShapeDtypeStruct((parts, tokens, width), signal.dtype),
            in_specs=[pl.BlockSpec(memory_space=pl.ANY)],
            out_specs=pl.BlockSpec(memory_space=pl.ANY),
            scratch_shapes=[
                pltpu.VMEM((parts, tokens, width), signal.dtype),
                pltpu.SemaphoreType.DMA((parts,)),
                pltpu.SemaphoreType.DMA((parts,)),
            ],
            compiler_params=params(2),
            name="split",
        )(hbm(signal))
    else:
        tiled = signal.reshape(tokens, parts, width).transpose(1, 0, 2)
    whole = lax.all_to_all(tiled, SEQ_AXES, split_axis=0, concat_axis=0, tiled=True)
    whole = whole.reshape(parts * tokens, width)

    taps, seeds, mid = pl.pallas_call(
        functools.partial(tables_kernel, width),
        out_shape=(
            pltpu.HBM((tokens * groups, LANES), f32),
            pltpu.HBM((states * 4 * groups, LANES), f32),
            shape(3 * states, LANES),
        ),
        out_specs=(
            pl.BlockSpec(memory_space=pltpu.HBM),
            pl.BlockSpec(memory_space=pltpu.HBM),
            pl.BlockSpec(memory_space=pltpu.VMEM),
        ),
        in_specs=[pl.BlockSpec(memory_space=pl.ANY)] * 5,
        scratch_shapes=[
            rows(tokens),
            rows(states * 4),
            rows(1),
            *[pltpu.VMEM((states, channels), f32)] * 4,
            *[rows(states)] * 4,
            rows(states * 2 * NEAR),
            rows(states * 2 * outer),
            pltpu.SemaphoreType.DMA((max(5, 1 + outer // min(2, outer)),)),
        ],
        compiler_params=params(40),
        cost_estimate=pl.CostEstimate(flops=20_000_000, bytes_accessed=2_000_000, transcendentals=40_000),
        name="tables",
    )(*(hbm(array) for array in (time_step.reshape(groups, LANES), decay_rate, frequency, output_real, output_imag)))

    if width != LANES:
        place = lax.axis_index("seqin") * n_out + lax.axis_index("seqout")

        def own(array):
            return lax.dynamic_slice_in_dim(array, place * width, width, array.ndim - 1)

        fade, lam = decay_step(own(time_step)[None, :], own(decay_rate), own(frequency))
        mid = jnp.concatenate([lam[0], lam[1], gain_of(fade)], axis=0)

    entering = pl.pallas_call(
        functools.partial(states_kernel, n_in, n_out, tokens),
        out_shape=jax.ShapeDtypeStruct((parts, code_rows, width), jnp.bfloat16),
        out_specs=pl.BlockSpec(memory_space=pl.ANY),
        scratch_shapes=[
            pltpu.VMEM((parts * tokens, width), f32),
            pltpu.VMEM((2 * NEAR, states, width), f32),
            pltpu.VMEM((parts, code_rows, width), jnp.bfloat16),
            pltpu.SemaphoreType.DMA((parts,)),
        ],
        compiler_params=params(40),
        cost_estimate=pl.CostEstimate(flops=16_000_000, bytes_accessed=1_000_000, transcendentals=0),
        name="states",
    )(whole, mid)

    taps, entering = lax.optimization_barrier((taps, entering))
    entering = lax.all_to_all(entering, SEQ_AXES, split_axis=0, concat_axis=0, tiled=True)
    if width != LANES:
        entering = entering.transpose(1, 0, 2).reshape(code_rows, groups, LANES).transpose(1, 0, 2)
    entering = entering.reshape(groups * code_rows, LANES)

    pack = pl.pallas_call(
        conv_kernel,
        out_shape=shape((tokens + states * 2 * FINAL_NEAR + states * 2) * groups, LANES),
        in_specs=[pl.BlockSpec(memory_space=pl.ANY)] * 4,
        scratch_shapes=[
            pltpu.VMEM((tokens, channels), signal.dtype),
            rows(1),
            rows(states * 4),
            rows(tokens),
            rows(tokens + 8),
            pltpu.SemaphoreType.DMA((4,)),
        ],
        compiler_params=params(40),
        cost_estimate=pl.CostEstimate(flops=18_000_000, bytes_accessed=2_000_000, transcendentals=0),
        name="conv",
    )(hbm(signal), hbm(skip_gain.reshape(groups, LANES)), hbm(taps), hbm(seeds))

    count = min(4, tokens // FINAL_NEAR)
    outputs = pl.pallas_call(
        functools.partial(final_kernel, states),
        out_shape=shape(tokens, channels),
        out_specs=pl.BlockSpec(memory_space=pl.ANY),
        scratch_shapes=[
            rows(2 * states),
            rows(2 * states),
            rows(count * FINAL_NEAR),
            pltpu.VMEM((tokens, channels), f32),
            pltpu.SemaphoreType.DMA((tokens // FINAL_NEAR // count,)),
        ],
        compiler_params=params(40),
        cost_estimate=pl.CostEstimate(flops=20_000_000, bytes_accessed=2_000_000, transcendentals=0),
        name="final",
    )(pack, entering)
    return outputs[None]


def solution(mesh):
    in_specs = (
        P(("groups", "seqout"), "seqin", "chan"),
        P("chan"),
        P(None, "chan"),
        P(None, "chan"),
        P(None, "chan"),
        P(None, "chan"),
        P("chan"),
    )
    out_specs = P(("groups", "seqout"), "seqin", "chan")
    return jax.shard_map(
        functools.partial(per_device, mesh.shape["seqin"], mesh.shape["seqout"]),
        mesh=mesh,
        in_specs=in_specs,
        out_specs=out_specs,
        check_vma=False,
    )
```

```python
import functools

import jax
import jax.numpy as jnp
from jax import lax
from jax.experimental import pallas as pl
from jax.experimental.pallas import tpu as pltpu
from jax.sharding import PartitionSpec as P

LANES = 128
NEAR = 16
FINAL_NEAR = 8
HALF_RANGE = 125.0
LOG_TWO = 0.6931471805599453


def cmul(a, b):
    return (a[0] * b[0] - a[1] * b[1], a[0] * b[1] + a[1] * b[0])


def cos_sin(angle):
    turns = jnp.floor(angle * 0.6366197723675814 + 0.5)
    rest = angle - turns * 1.5703125
    rest = rest - turns * 4.837512969970703125e-4
    rest = rest - turns * 7.549789948768648e-8
    square = rest * rest
    sine = rest + rest * square * (
        -1.6666654611e-1 + square * (8.3321608736e-3 - square * 1.9515295891e-4)
    )
    cosine = (
        1.0
        - 0.5 * square
        + square * square * (4.166664568298827e-2 + square * (-1.388731625493765e-3 + square * 2.443315711809948e-5))
    )
    quarter = turns.astype(jnp.int32) & 3
    swap = (quarter & 1) == 1
    first = jnp.where(swap, sine, cosine)
    second = jnp.where(swap, cosine, sine)
    return (
        jnp.where((quarter == 1) | (quarter == 2), -first, first),
        jnp.where(quarter >= 2, -second, second),
    )


def decay_step(time_step, decay_rate, frequency):
    fade_rate = time_step * decay_rate
    shrink = jnp.exp(-fade_rate)
    cosine, sine = cos_sin(time_step * frequency)
    return (fade_rate, (shrink * cosine, shrink * sine))


def gain_of(fade_rate):
    double = 2.0 * fade_rate
    series = 1.0 / 40320.0
    for factor in (5040.0, 720.0, 120.0, 24.0, 6.0, 2.0, 1.0):
        series = 1.0 / factor - double * series
    small = double * series
    return jnp.sqrt(jnp.where(double < 0.25, small, 1.0 - jnp.exp(-double)))


def power_list(lam, count):
    powers = [None, lam]
    for k in range(2, count + 1):
        powers.append(cmul(powers[k // 2], powers[k - k // 2]))
    return powers


def spread_rows(source_ref, target_ref, rows, groups, stack):
    for start in range(0, rows, stack):
        for k in range(groups):
            part = source_ref[start : start + stack, k * LANES : (k + 1) * LANES]
            target_ref[pl.ds(start * groups + k, stack, stride=groups), :] = part.astype(jnp.float32)


def row_at(ref, index, groups):
    return ref[pl.ds(pl.multiple_of(index * groups, groups), groups), :]


def put_row(ref, index, groups, value):
    ref[pl.ds(pl.multiple_of(index * groups, groups), groups), :] = value


def power_sum(near_ref, lead_of, states, groups, near, count, init):

    def turn(n, acc):
        leads = lead_of(n)
        acc = list(acc)
        for a in range(count):
            acc[a * near] = acc[a * near] + leads[a][0]
        for u in range(1, near):
            real = row_at(near_ref, n * (2 * near) + 2 * u, groups)
            imag = row_at(near_ref, n * (2 * near) + 2 * u + 1, groups)
            for a in range(count):
                slot = a * near + u
                acc[slot] = acc[slot] + (leads[a][0] * real - leads[a][1] * imag)
        return tuple(acc)

    return lax.fori_loop(0, states, turn, tuple(init), unroll=16)


def power_of(base, exponent):
    result = None
    while exponent:
        if exponent & 1:
            result = base if result is None else cmul(result, base)
        exponent //= 2
        if exponent:
            base = cmul(base, base)
    return result


def start_copies(pairs, sems):
    copies = [pltpu.make_async_copy(pair[0], pair[1], sems.at[i]) for i, pair in enumerate(pairs)]
    for copy in copies:
        copy.start()
    return copies


def pair_at(ref, index, groups):
    return tuple(row_at(ref, index + part, groups) for part in range(2))


def put_pair(ref, index, groups, value):
    for part in range(2):
        put_row(ref, index + part, groups, value[part])


def decayed_sum(signal_sp, powers, tokens, groups):
    a_tile = min(4, tokens // NEAR)
    total = None
    for first in range(0, tokens // NEAR, a_tile):
        real, imag = [None] * a_tile, [None] * a_tile
        for u in range(NEAR):
            power = NEAR - 1 - u
            for a in range(a_tile):
                row = ((first + a) * NEAR + u) * groups
                drive = signal_sp[row : row + groups, :]
                if power:
                    add_real, add_imag = powers[power][0] * drive, powers[power][1] * drive
                    real[a] = add_real if real[a] is None else real[a] + add_real
                    imag[a] = add_imag if imag[a] is None else imag[a] + add_imag
                else:
                    real[a] = real[a] + drive
        for a in range(a_tile):
            if total is None:
                total = (real[a], imag[a])
            else:
                moved = cmul(powers[NEAR], total)
                total = (moved[0] + real[a], moved[1] + imag[a])
    return total


def sums_kernel(
    signal_hbm, step_hbm, decay_hbm, freq_hbm, real_hbm, imag_hbm,
    seed_hbm, base_ref,
    signal_ref, step_ref, decay_ref, freq_ref, real_ref, imag_ref,
    signal_sp, decay_sp, freq_sp, real_sp, imag_sp, seed_ref, sems,
):
    copies = start_copies(
        (
            (step_hbm, step_ref), (decay_hbm, decay_ref), (freq_hbm, freq_ref),
            (signal_hbm, signal_ref), (real_hbm, real_ref), (imag_hbm, imag_ref),
        ),
        sems,
    )
    states, channels = decay_ref.shape
    groups = channels // LANES
    tokens = signal_ref.shape[0]
    for copy in copies:
        copy.wait()
    for source, target in ((decay_ref, decay_sp), (freq_ref, freq_sp), (real_ref, real_sp), (imag_ref, imag_sp)):
        spread_rows(source, target, states, groups, 8)
    spread_rows(signal_ref, signal_sp, tokens, groups, 16)
    step = step_ref[...]

    def prepare(n, carry):
        fade, lam = decay_step(step, row_at(decay_sp, n, groups), row_at(freq_sp, n, groups))
        gain = gain_of(fade)
        weight = (2.0 * row_at(real_sp, n, groups), 2.0 * row_at(imag_sp, n, groups))
        put_pair(seed_ref, 6 * n, groups, lam)
        put_pair(seed_ref, 6 * n + 2, groups, weight)
        put_pair(seed_ref, 6 * n + 4, groups, (weight[0] * gain, weight[1] * gain))
        own = decayed_sum(signal_sp, power_list(lam, NEAR), tokens, groups)
        put_pair(base_ref, 5 * n, groups, lam)
        put_pair(base_ref, 5 * n + 2, groups, (gain * own[0], gain * own[1]))
        put_row(base_ref, 5 * n + 4, groups, gain)
        return carry

    lax.fori_loop(0, states, prepare, 0, unroll=2)
    copy = pltpu.make_async_copy(seed_ref, seed_hbm, sems.at[0])
    copy.start()
    copy.wait()


def largest(value, most):
    return jnp.maximum(most, jnp.maximum(jnp.abs(value[0]), jnp.abs(value[1])))


def messages_kernel(n_in, n_early, base_ref, *refs):
    early_refs, out_refs, own_hbm = refs[:n_early], refs[n_early : n_early + n_in - 1], refs[n_early + n_in - 1]
    signal_sp, sums_ref, own_ref, code_ref, sems = refs[n_early + n_in :]
    tokens, channels = early_refs[0].shape
    groups = channels // LANES
    states = base_ref.shape[0] // (5 * groups)
    for j in range(n_early):
        spread_rows(early_refs[j], signal_sp.at[j], tokens, groups, 16)

    def gather(n, most):
        lam, own = pair_at(base_ref, 5 * n, groups), pair_at(base_ref, 5 * n + 2, groups)
        gain = row_at(base_ref, 5 * n + 4, groups)
        powers = power_list(lam, NEAR)
        block = power_of(powers[NEAR], tokens // NEAR * n_in)
        early = None
        for j in reversed(range(n_early)):
            part = decayed_sum(signal_sp.at[j], powers, tokens, groups)
            part = (gain * part[0], gain * part[1])
            if early is not None:
                moved = cmul(block, early)
                part = (part[0] + moved[0], part[1] + moved[1])
            early = part
        moved = cmul(block, early)
        later = (own[0] + moved[0], own[1] + moved[1])
        put_pair(sums_ref, 4 * n, groups, later)
        put_pair(sums_ref, 4 * n + 2, groups, early)
        put_pair(own_ref, 2 * n, groups, early)
        return (largest(later, most[0]), largest(early, most[1]))

    zero = jnp.zeros((groups, LANES), jnp.float32)
    most = lax.fori_loop(0, states, gather, (zero, zero), unroll=2)
    own_copy = pltpu.make_async_copy(own_ref, own_hbm, sems.at[0])
    own_copy.start()
    inverse = []
    for kind in range(2):
        scale = (1.01 * most[kind]).astype(jnp.bfloat16).astype(jnp.float32)
        inverse.append(jnp.where(scale > 1e-36, 1.0 / jnp.maximum(scale, 1e-36), 0.0))
        pair = jnp.concatenate([scale, scale], axis=0).astype(jnp.bfloat16)
        code_ref[kind, states * 2 * groups :, :] = pair

    def write(n, carry):
        for kind in range(2):
            value = pair_at(sums_ref, 4 * n + 2 * kind, groups)
            code = jnp.concatenate([encode(value[part], inverse[kind]) for part in range(2)], axis=0)
            row = pl.multiple_of(n * (2 * groups), 2 * groups)
            code_ref[kind, pl.ds(row, 2 * groups), :] = code.astype(jnp.bfloat16)
        return carry

    lax.fori_loop(0, states, write, 0, unroll=4)
    place = lax.axis_index("seqin")
    copies = [own_copy]
    for d in range(1, n_in):
        kind = (place + d) // n_in
        copies.append(pltpu.make_async_copy(code_ref.at[kind], out_refs[d - 1], sems.at[d]))
        copies[-1].start()
    for copy in copies:
        copy.wait()


def split_pack(pack_ref, tokens, states, groups):
    refs, start = [], 0
    for count in (tokens, states * 2 * FINAL_NEAR, 2 * states, 2 * states, 2 * states):
        refs.append(pack_ref.at[start * groups : (start + count) * groups])
        start += count
    return refs


def conv_kernel(
    signal_hbm, skip_hbm, seed_hbm, own_hbm, pack_ref,
    signal_ref, skip_ref, seed_ref, near_ref, lead_ref, signal_sp, taps_pad, sems,
):
    tokens, channels = signal_ref.shape
    groups = channels // LANES
    states = seed_ref.shape[0] // (6 * groups)
    outer = tokens // NEAR
    tile = 8
    out_ref, few_ref, shift_ref, hop_ref, own_ref = split_pack(pack_ref, tokens, states, groups)
    copies = start_copies(
        ((seed_hbm, seed_ref), (signal_hbm, signal_ref), (skip_hbm, skip_ref), (own_hbm, own_ref)), sems
    )
    taps_pad[0 : tile * groups, :] = jnp.zeros((tile * groups, LANES), jnp.float32)
    copies[0].wait()

    def prepare(n, carry):
        lam, weight, lead = (pair_at(seed_ref, 6 * n + 2 * i, groups) for i in range(3))
        powers = power_list(lam, NEAR)
        for u in range(1, NEAR):
            put_pair(near_ref, n * (2 * NEAR) + 2 * u, groups, powers[u])
        for u in range(FINAL_NEAR):
            put_pair(few_ref, n * (2 * FINAL_NEAR) + 2 * u, groups, powers[u if u else FINAL_NEAR])
        put_pair(shift_ref, 2 * n, groups, cmul(weight, lam))
        put_pair(hop_ref, 2 * n, groups, power_of(powers[NEAR], outer))
        for a in range(outer):
            if a:
                lead = cmul(lead, powers[NEAR])
            put_pair(lead_ref, n * (2 * outer) + 2 * a, groups, lead)
        return carry

    lax.fori_loop(0, states, prepare, 0, unroll=2)
    for copy in copies[1:]:
        copy.wait()
    spread_rows(signal_ref, signal_sp, tokens, groups, 16)
    zero = jnp.zeros((groups, LANES), jnp.float32)
    count = min(2, outer)
    for first in range(0, outer, count):

        def lead_of(n, first=first):
            return [pair_at(lead_ref, n * (2 * outer) + 2 * (first + a), groups) for a in range(count)]

        acc = power_sum(near_ref, lead_of, states, groups, NEAR, count, [zero] * (count * NEAR))
        for t in range(count * NEAR):
            put_row(taps_pad, tile + first * NEAR + t, groups, acc[t])

    skip = skip_ref[...]

    def col_tile(ji, acc, ti):
        gap = (ti - ji) * tile + 1
        window = [row_at(taps_pad, gap + m, groups) for m in range(2 * tile - 1)]
        acc = list(acc)
        for j in range(tile):
            drive = row_at(signal_sp, ji * tile + j, groups)
            for t in range(tile):
                acc[t] = acc[t] + window[t - j + tile - 1] * drive
        return tuple(acc)

    for ti in range(tokens // tile):
        init = tuple(skip * row_at(signal_sp, ti * tile + t, groups) for t in range(tile))
        acc = lax.fori_loop(0, ti + 1, functools.partial(col_tile, ti=ti), init, unroll=4)
        for t in range(tile):
            put_row(out_ref, ti * tile + t, groups, acc[t])


def encode(value, inverse):
    code = jnp.exp2(jnp.abs(value) * inverse * (2.0 * HALF_RANGE) - HALF_RANGE)
    return jnp.where(value < 0.0, -code, code)


def decode(code, scale):
    size = (jnp.log(jnp.abs(code)) * (0.5 / HALF_RANGE / LOG_TWO) + 0.5) * scale
    return jnp.where(code < 0.0, -size, size)


def final_kernel(states, pack_ref, *refs):
    message_refs, out_ref = refs[:-5], refs[-5]
    state_sp, rows_ref, out_buf, sems = refs[-4:]
    tokens, channels = out_ref.shape
    groups = channels // LANES
    near = FINAL_NEAR
    outer = tokens // near
    local_ref, near_ref, shift_ref, hop_ref, own_ref = split_pack(pack_ref, tokens, states, groups)
    scales = [ref[states * 2 * groups :, :].astype(jnp.float32)[0:groups, :] for ref in message_refs]

    def enter(n, carry):
        hop = pair_at(hop_ref, 2 * n, groups)
        state = pair_at(own_ref, 2 * n, groups)
        row = pl.multiple_of(n * (2 * groups), 2 * groups)
        for ref, scale in zip(reversed(message_refs), reversed(scales)):
            code = ref[pl.ds(row, 2 * groups), :].astype(jnp.float32)
            moved = cmul(hop, state)
            state = tuple(
                moved[part] + decode(code[part * groups : (part + 1) * groups, :], scale) for part in range(2)
            )
        put_pair(state_sp, 2 * n, groups, cmul(pair_at(shift_ref, 2 * n, groups), state))
        return carry

    lax.fori_loop(0, states, enter, 0, unroll=4)
    count = min(4, outer)
    span = count * near
    copies = []
    for index in range(outer // count):
        last = index + 1 == outer // count

        def lead_of(n, last=last):
            hop = pair_at(near_ref, n * (2 * near), groups)
            leads = [pair_at(state_sp, 2 * n, groups)]
            for _ in range(count - 1 if last else count):
                leads.append(cmul(leads[-1], hop))
            if not last:
                for part in range(2):
                    put_row(state_sp, 2 * n + part, groups, leads[count][part])
            return leads

        start = index * span
        init = [local_ref[(start + t) * groups : (start + t + 1) * groups, :] for t in range(span)]
        acc = power_sum(near_ref, lead_of, states, groups, near, count, init)
        for t in range(span):
            rows_ref[t * groups : (t + 1) * groups, :] = acc[t]
        for t in range(0, span, 8):
            for k in range(groups):
                out_buf[start + t : start + t + 8, k * LANES : (k + 1) * LANES] = rows_ref[
                    pl.ds(t * groups + k, 8, stride=groups), :
                ]
        copy = pltpu.make_async_copy(
            out_buf.at[pl.ds(start, span)], out_ref.at[pl.ds(start, span)], sems.at[index]
        )
        copy.start()
        copies.append(copy)
    for copy in copies:
        copy.wait()


def per_device(n_in, n_out, inputs, time_step, decay_rate, frequency, output_real, output_imag, skip_gain):
    signal = inputs[0]
    tokens, channels = signal.shape
    states = decay_rate.shape[0]
    groups = channels // LANES
    outer = tokens // NEAR
    code_rows = 2 * groups * (states + 1)
    f32 = jnp.float32
    any_space = pl.BlockSpec(memory_space=pl.ANY)
    in_vmem = pl.BlockSpec(memory_space=pltpu.VMEM)
    in_hbm = pl.BlockSpec(memory_space=pltpu.HBM)

    def rows(count, dtype=f32):
        return pltpu.VMEM((count * groups, LANES), dtype)

    def shape(*dims):
        return jax.ShapeDtypeStruct(dims, f32)

    def kept(count):
        return pltpu.HBM((count * groups, LANES), f32)

    def hbm(array):
        return pltpu.with_memory_space_constraint(array, pltpu.HBM)

    def call(kernel, name, flops, **options):
        return pl.pallas_call(
            kernel,
            compiler_params=pltpu.CompilerParams(vmem_limit_bytes=24 * 1024 * 1024),
            cost_estimate=pl.CostEstimate(flops=flops, bytes_accessed=2_000_000, transcendentals=0),
            name=name,
            **options,
        )

    early = [
        lax.ppermute(signal, "seqout", [(i, i + j) for i in range(n_out - j)]) for j in range(1, n_out)
    ]

    parameters = (time_step.reshape(groups, LANES), decay_rate, frequency, output_real, output_imag)
    seeds, base = call(
        sums_kernel,
        "sums",
        20_000_000,
        out_shape=(kept(6 * states), shape(5 * states * groups, LANES)),
        in_specs=[any_space] * 6,
        out_specs=(in_hbm, in_vmem),
        scratch_shapes=[
            pltpu.VMEM((tokens, channels), signal.dtype),
            rows(1),
            *[pltpu.VMEM((states, channels), f32)] * 4,
            rows(tokens),
            *[rows(states)] * 4,
            rows(6 * states),
            pltpu.SemaphoreType.DMA((6,)),
        ],
    )(hbm(signal), *(hbm(array) for array in parameters))

    *messages, own = call(
        functools.partial(messages_kernel, n_in, n_out - 1),
        "messages",
        20_000_000,
        out_shape=(
            *[pltpu.HBM((code_rows, LANES), jnp.bfloat16)] * (n_in - 1),
            kept(2 * states),
        ),
        out_specs=(in_hbm,) * n_in,
        scratch_shapes=[
            pltpu.VMEM((n_out - 1, tokens * groups, LANES), f32),
            rows(4 * states),
            rows(2 * states),
            pltpu.VMEM((2, code_rows, LANES), jnp.bfloat16),
            pltpu.SemaphoreType.DMA((n_in,)),
        ],
    )(base, *early)

    received = [
        lax.ppermute(messages[d - 1], "seqin", [(i, (i + d) % n_in) for i in range(n_in)]) for d in range(1, n_in)
    ]

    pack = call(
        conv_kernel,
        "conv",
        40_000_000,
        out_shape=shape((tokens + states * (2 * FINAL_NEAR + 6)) * groups, LANES),
        in_specs=[any_space] * 4,
        scratch_shapes=[
            pltpu.VMEM((tokens, channels), signal.dtype),
            rows(1),
            rows(6 * states),
            rows(2 * NEAR * states),
            rows(2 * outer * states),
            rows(tokens),
            rows(tokens + 8),
            pltpu.SemaphoreType.DMA((4,)),
        ],
    )(hbm(signal), hbm(skip_gain.reshape(groups, LANES)), hbm(seeds), hbm(own))

    count = min(4, tokens // FINAL_NEAR)
    outputs = call(
        functools.partial(final_kernel, states),
        "final",
        20_000_000,
        out_shape=shape(tokens, channels),
        out_specs=any_space,
        scratch_shapes=[
            rows(2 * states),
            rows(count * FINAL_NEAR),
            pltpu.VMEM((tokens, channels), f32),
            pltpu.SemaphoreType.DMA((tokens // FINAL_NEAR // count,)),
        ],
    )(pack, *received)
    return outputs[None]


def solution(mesh):
    in_specs = (
        P(("groups", "seqout"), "seqin", "chan"),
        P("chan"),
        P(None, "chan"),
        P(None, "chan"),
        P(None, "chan"),
        P(None, "chan"),
        P("chan"),
    )
    out_specs = P(("groups", "seqout"), "seqin", "chan")
    return jax.shard_map(
        functools.partial(per_device, mesh.shape["seqin"], mesh.shape["seqout"]),
        mesh=mesh,
        in_specs=in_specs,
        out_specs=out_specs,
        check_vma=False,
    )
```

```python
import functools

import jax
import jax.numpy as jnp
from jax import lax
from jax.experimental import pallas as pl
from jax.experimental.pallas import tpu as pltpu
from jax.sharding import PartitionSpec as P

LANES = 128
NEAR = 16
FINAL_NEAR = 8
HALF_RANGE = 125.0
LOG_TWO = 0.6931471805599453
SMALLEST_CODE = 2.0**-125


def cmul(a, b):
    return (a[0] * b[0] - a[1] * b[1], a[0] * b[1] + a[1] * b[0])


def cos_sin(angle):
    turns = jnp.floor(angle * 0.6366197723675814 + 0.5)
    rest = angle - turns * 1.5703125
    rest = rest - turns * 4.837512969970703125e-4
    rest = rest - turns * 7.549789948768648e-8
    square = rest * rest
    sine = rest + rest * square * (
        -1.6666654611e-1 + square * (8.3321608736e-3 - square * 1.9515295891e-4)
    )
    cosine = (
        1.0
        - 0.5 * square
        + square * square * (4.166664568298827e-2 + square * (-1.388731625493765e-3 + square * 2.443315711809948e-5))
    )
    quarter = turns.astype(jnp.int32) & 3
    swap = (quarter & 1) == 1
    first = jnp.where(swap, sine, cosine)
    second = jnp.where(swap, cosine, sine)
    return (
        jnp.where((quarter == 1) | (quarter == 2), -first, first),
        jnp.where(quarter >= 2, -second, second),
    )


def decay_step(time_step, decay_rate, frequency):
    fade_rate = time_step * decay_rate
    shrink = jnp.exp(-fade_rate)
    cosine, sine = cos_sin(time_step * frequency)
    return (fade_rate, (shrink * cosine, shrink * sine))


def gain_of(fade_rate):
    double = 2.0 * fade_rate
    series = 1.0 / 40320.0
    for factor in (5040.0, 720.0, 120.0, 24.0, 6.0, 2.0, 1.0):
        series = 1.0 / factor - double * series
    small = double * series
    return jnp.sqrt(jnp.where(double < 0.25, small, 1.0 - jnp.exp(-double)))


def power_list(lam, count):
    powers = [None, lam]
    for k in range(2, count + 1):
        powers.append(cmul(powers[k // 2], powers[k - k // 2]))
    return powers


def spread_rows(source_ref, target_ref, rows, groups, stack):
    for start in range(0, rows, stack):
        for k in range(groups):
            part = source_ref[start : start + stack, k * LANES : (k + 1) * LANES]
            target_ref[pl.ds(start * groups + k, stack, stride=groups), :] = part.astype(jnp.float32)


def row_at(ref, index, groups):
    return ref[pl.ds(pl.multiple_of(index * groups, groups), groups), :]


def put_row(ref, index, groups, value):
    ref[pl.ds(pl.multiple_of(index * groups, groups), groups), :] = value


def power_sum(near_ref, lead_of, states, groups, near, count, init):

    def turn(n, acc):
        leads = lead_of(n)
        acc = list(acc)
        for a in range(count):
            acc[a * near] = acc[a * near] + leads[a][0]
        for u in range(1, near):
            real = row_at(near_ref, n * (2 * near) + 2 * u, groups)
            imag = row_at(near_ref, n * (2 * near) + 2 * u + 1, groups)
            for a in range(count):
                slot = a * near + u
                acc[slot] = acc[slot] + (leads[a][0] * real - leads[a][1] * imag)
        return tuple(acc)

    return lax.fori_loop(0, states, turn, tuple(init), unroll=16)


def power_of(base, exponent):
    result = None
    while exponent:
        if exponent & 1:
            result = base if result is None else cmul(result, base)
        exponent //= 2
        if exponent:
            base = cmul(base, base)
    return result


def start_copies(pairs, sems):
    copies = [pltpu.make_async_copy(pair[0], pair[1], sems.at[i]) for i, pair in enumerate(pairs)]
    for copy in copies:
        copy.start()
    return copies


def pair_at(ref, index, groups):
    return tuple(row_at(ref, index + part, groups) for part in range(2))


def put_pair(ref, index, groups, value):
    for part in range(2):
        put_row(ref, index + part, groups, value[part])


def decayed_sum(signal_sp, powers, tokens, groups):
    a_tile = min(4, tokens // NEAR)
    total = None
    for first in range(0, tokens // NEAR, a_tile):
        real, imag = [None] * a_tile, [None] * a_tile
        for u in range(NEAR):
            power = NEAR - 1 - u
            for a in range(a_tile):
                row = ((first + a) * NEAR + u) * groups
                drive = signal_sp[row : row + groups, :]
                if power:
                    add_real, add_imag = powers[power][0] * drive, powers[power][1] * drive
                    real[a] = add_real if real[a] is None else real[a] + add_real
                    imag[a] = add_imag if imag[a] is None else imag[a] + add_imag
                else:
                    real[a] = real[a] + drive
        for a in range(a_tile):
            if total is None:
                total = (real[a], imag[a])
            else:
                moved = cmul(powers[NEAR], total)
                total = (moved[0] + real[a], moved[1] + imag[a])
    return total


def encode(value, inverse):
    code = jnp.exp2(jnp.abs(value) * inverse * (2.0 * HALF_RANGE) - HALF_RANGE)
    return jnp.where(value < 0.0, -code, code)


def decode(code, scale):
    size = (jnp.log(jnp.maximum(jnp.abs(code), SMALLEST_CODE)) * (0.5 / HALF_RANGE / LOG_TWO) + 0.5) * scale
    return jnp.where(code < 0.0, -size, size)


def largest(value, most):
    return jnp.maximum(most, jnp.maximum(jnp.abs(value[0]), jnp.abs(value[1])))


def write_codes(value_of, code_ref, most, states, groups):
    scale = (1.01 * most).astype(jnp.bfloat16).astype(jnp.float32)
    inverse = jnp.where(scale > 1e-36, 1.0 / jnp.maximum(scale, 1e-36), 0.0)
    code_ref[states * 2 * groups :, :] = jnp.concatenate([scale, scale], axis=0).astype(jnp.bfloat16)

    def write(n, carry):
        value = value_of(n)
        code = jnp.concatenate([encode(value[part], inverse) for part in range(2)], axis=0)
        row = pl.multiple_of(n * (2 * groups), 2 * groups)
        code_ref[pl.ds(row, 2 * groups), :] = code.astype(jnp.bfloat16)
        return carry

    lax.fori_loop(0, states, write, 0, unroll=4)


def scale_at(code_ref, states, groups):
    return code_ref[states * 2 * groups :, :].astype(jnp.float32)[0:groups, :]


def decode_at(code_ref, n, scale, groups):
    row = pl.multiple_of(n * (2 * groups), 2 * groups)
    code = code_ref[pl.ds(row, 2 * groups), :].astype(jnp.float32)
    return tuple(decode(code[part * groups : (part + 1) * groups, :], scale) for part in range(2))


def sums_kernel(
    n_in, send, signal_hbm, step_hbm, decay_hbm, freq_hbm,
    result_ref,
    signal_ref, step_ref, decay_ref, freq_ref,
    signal_sp, decay_sp, freq_sp, base_ref, code_ref, sems,
):
    place = lax.axis_index("seqout")
    needed = place < lax.axis_size("seqout") - 1 if send else place > 0

    @pl.when(needed)
    def _():
        copies = start_copies(
            ((step_hbm, step_ref), (decay_hbm, decay_ref), (freq_hbm, freq_ref), (signal_hbm, signal_ref)), sems
        )
        states, channels = decay_ref.shape
        groups = channels // LANES
        tokens = signal_ref.shape[0]
        for copy in copies[:3]:
            copy.wait()
        for source, target in ((decay_ref, decay_sp), (freq_ref, freq_sp)):
            spread_rows(source, target, states, groups, 8)
        copies[3].wait()
        spread_rows(signal_ref, signal_sp, tokens, groups, 16)
        step = step_ref[...]
        target_ref = base_ref if send else result_ref

        def prepare(n, most):
            fade, lam = decay_step(step, row_at(decay_sp, n, groups), row_at(freq_sp, n, groups))
            gain = gain_of(fade)
            powers = power_list(lam, NEAR)
            own = decayed_sum(signal_sp, powers, tokens, groups)
            own = (gain * own[0], gain * own[1])
            if not send:
                put_pair(target_ref, 4 * n, groups, power_of(powers[NEAR], tokens // NEAR * n_in))
            put_pair(target_ref, 4 * n + 2, groups, own)
            return largest(own, most)

        most = lax.fori_loop(0, states, prepare, jnp.zeros((groups, LANES), jnp.float32), unroll=4)
        if send:
            write_codes(lambda n: pair_at(base_ref, 4 * n + 2, groups), code_ref, most, states, groups)
            copy = pltpu.make_async_copy(code_ref, result_ref, sems.at[0])
            copy.start()
            copy.wait()


def messages_kernel(n_in, n_early, base_ref, sent_hbm, *refs):
    received_refs, out_refs, own_hbm = refs[:n_early], refs[n_early : n_early + n_in - 1], refs[n_early + n_in - 1]
    later_ref, own_ref, code_ref, sems = refs[n_early + n_in :]
    groups = (received_refs[0].shape[0] - base_ref.shape[0] // 2) // 2
    states = base_ref.shape[0] // (4 * groups)
    first_block = lax.axis_index("seqout") == 0

    @pl.when(first_block)
    def _():
        copy = pltpu.make_async_copy(sent_hbm, code_ref.at[0], sems.at[0])
        copy.start()
        own_ref[...] = jnp.zeros_like(own_ref)
        code_ref[1] = jnp.zeros_like(code_ref[1])
        copy.wait()

    @pl.when(jnp.logical_not(first_block))
    def _():
        scales = [scale_at(ref, states, groups) for ref in received_refs]

        def gather(n, most):
            block, own = pair_at(base_ref, 4 * n, groups), pair_at(base_ref, 4 * n + 2, groups)
            early = None
            for ref, scale in zip(reversed(received_refs), reversed(scales)):
                part = decode_at(ref, n, scale, groups)
                if early is not None:
                    moved = cmul(block, early)
                    part = (part[0] + moved[0], part[1] + moved[1])
                early = part
            moved = cmul(block, early)
            later = (own[0] + moved[0], own[1] + moved[1])
            put_pair(later_ref, 2 * n, groups, later)
            put_pair(own_ref, 2 * n, groups, early)
            return (largest(later, most[0]), largest(early, most[1]))

        zero = jnp.zeros((groups, LANES), jnp.float32)
        most = lax.fori_loop(0, states, gather, (zero, zero), unroll=4)
        write_codes(lambda n: pair_at(later_ref, 2 * n, groups), code_ref.at[0], most[0], states, groups)
        if n_early == 1:
            code_ref[1] = received_refs[0][...]
        else:
            write_codes(lambda n: pair_at(own_ref, 2 * n, groups), code_ref.at[1], most[1], states, groups)

    place = lax.axis_index("seqin")
    copies = [pltpu.make_async_copy(own_ref, own_hbm, sems.at[0])]
    for d in range(1, n_in):
        kind = (place + d) // n_in
        copies.append(pltpu.make_async_copy(code_ref.at[kind], out_refs[d - 1], sems.at[d]))
    for copy in copies:
        copy.start()
    for copy in copies:
        copy.wait()


def split_pack(pack_ref, tokens, states, groups):
    refs, start = [], 0
    for count in (tokens, states * 2 * FINAL_NEAR, 2 * states, 2 * states, 2 * states):
        refs.append(pack_ref.at[start * groups : (start + count) * groups])
        start += count
    return refs


def conv_kernel(
    signal_hbm, skip_hbm, step_hbm, decay_hbm, freq_hbm, real_hbm, imag_hbm, own_hbm, pack_ref,
    signal_ref, skip_ref, step_ref, decay_ref, freq_ref, real_ref, imag_ref,
    decay_sp, freq_sp, real_sp, imag_sp, near_ref, lead_ref, signal_sp, taps_pad, sems,
):
    tokens, channels = signal_ref.shape
    groups = channels // LANES
    states = decay_ref.shape[0]
    outer = tokens // NEAR
    tile = 8
    out_ref, few_ref, shift_ref, hop_ref, own_ref = split_pack(pack_ref, tokens, states, groups)
    copies = start_copies(
        (
            (step_hbm, step_ref), (decay_hbm, decay_ref), (freq_hbm, freq_ref), (real_hbm, real_ref),
            (imag_hbm, imag_ref), (signal_hbm, signal_ref), (skip_hbm, skip_ref), (own_hbm, own_ref),
        ),
        sems,
    )
    taps_pad[0 : tile * groups, :] = jnp.zeros((tile * groups, LANES), jnp.float32)
    for copy in copies[:5]:
        copy.wait()
    for source, target in ((decay_ref, decay_sp), (freq_ref, freq_sp), (real_ref, real_sp), (imag_ref, imag_sp)):
        spread_rows(source, target, states, groups, 8)
    step = step_ref[...]

    def prepare(n, carry):
        fade, lam = decay_step(step, row_at(decay_sp, n, groups), row_at(freq_sp, n, groups))
        gain = gain_of(fade)
        weight = (2.0 * row_at(real_sp, n, groups), 2.0 * row_at(imag_sp, n, groups))
        lead = (weight[0] * gain, weight[1] * gain)
        powers = power_list(lam, NEAR)
        for u in range(1, NEAR):
            put_pair(near_ref, n * (2 * NEAR) + 2 * u, groups, powers[u])
        for u in range(FINAL_NEAR):
            put_pair(few_ref, n * (2 * FINAL_NEAR) + 2 * u, groups, powers[u if u else FINAL_NEAR])
        put_pair(shift_ref, 2 * n, groups, cmul(weight, lam))
        put_pair(hop_ref, 2 * n, groups, power_of(powers[NEAR], outer))
        for a in range(outer):
            if a:
                lead = cmul(lead, powers[NEAR])
            put_pair(lead_ref, n * (2 * outer) + 2 * a, groups, lead)
        return carry

    lax.fori_loop(0, states, prepare, 0, unroll=2)
    for copy in copies[5:]:
        copy.wait()
    spread_rows(signal_ref, signal_sp, tokens, groups, 16)
    zero = jnp.zeros((groups, LANES), jnp.float32)
    count = min(2, outer)
    for first in range(0, outer, count):

        def lead_of(n, first=first):
            return [pair_at(lead_ref, n * (2 * outer) + 2 * (first + a), groups) for a in range(count)]

        acc = power_sum(near_ref, lead_of, states, groups, NEAR, count, [zero] * (count * NEAR))
        for t in range(count * NEAR):
            put_row(taps_pad, tile + first * NEAR + t, groups, acc[t])

    skip = skip_ref[...]

    def col_tile(ji, acc, ti):
        gap = (ti - ji) * tile + 1
        window = [row_at(taps_pad, gap + m, groups) for m in range(2 * tile - 1)]
        acc = list(acc)
        for j in range(tile):
            drive = row_at(signal_sp, ji * tile + j, groups)
            for t in range(tile):
                acc[t] = acc[t] + window[t - j + tile - 1] * drive
        return tuple(acc)

    for ti in range(tokens // tile):
        init = tuple(skip * row_at(signal_sp, ti * tile + t, groups) for t in range(tile))
        acc = lax.fori_loop(0, ti + 1, functools.partial(col_tile, ti=ti), init, unroll=4)
        for t in range(tile):
            put_row(out_ref, ti * tile + t, groups, acc[t])


def final_kernel(states, pack_ref, *refs):
    message_refs, out_ref = refs[:-5], refs[-5]
    state_sp, rows_ref, out_buf, sems = refs[-4:]
    tokens, channels = out_ref.shape
    groups = channels // LANES
    near = FINAL_NEAR
    outer = tokens // near
    local_ref, near_ref, shift_ref, hop_ref, own_ref = split_pack(pack_ref, tokens, states, groups)
    scales = [scale_at(ref, states, groups) for ref in message_refs]

    def enter(n, carry):
        hop = pair_at(hop_ref, 2 * n, groups)
        state = pair_at(own_ref, 2 * n, groups)
        for ref, scale in zip(reversed(message_refs), reversed(scales)):
            moved, part = cmul(hop, state), decode_at(ref, n, scale, groups)
            state = (moved[0] + part[0], moved[1] + part[1])
        put_pair(state_sp, 2 * n, groups, cmul(pair_at(shift_ref, 2 * n, groups), state))
        return carry

    lax.fori_loop(0, states, enter, 0, unroll=4)
    count = min(4, outer)
    span = count * near
    copies = []
    for index in range(outer // count):
        last = index + 1 == outer // count

        def lead_of(n, last=last):
            hop = pair_at(near_ref, n * (2 * near), groups)
            leads = [pair_at(state_sp, 2 * n, groups)]
            for _ in range(count - 1 if last else count):
                leads.append(cmul(leads[-1], hop))
            if not last:
                for part in range(2):
                    put_row(state_sp, 2 * n + part, groups, leads[count][part])
            return leads

        start = index * span
        init = [local_ref[(start + t) * groups : (start + t + 1) * groups, :] for t in range(span)]
        acc = power_sum(near_ref, lead_of, states, groups, near, count, init)
        for t in range(span):
            rows_ref[t * groups : (t + 1) * groups, :] = acc[t]
        for t in range(0, span, 8):
            for k in range(groups):
                out_buf[start + t : start + t + 8, k * LANES : (k + 1) * LANES] = rows_ref[
                    pl.ds(t * groups + k, 8, stride=groups), :
                ]
        copy = pltpu.make_async_copy(
            out_buf.at[pl.ds(start, span)], out_ref.at[pl.ds(start, span)], sems.at[index]
        )
        copy.start()
        copies.append(copy)
    for copy in copies:
        copy.wait()


def per_device(n_in, n_out, inputs, time_step, decay_rate, frequency, output_real, output_imag, skip_gain):
    signal = inputs[0]
    tokens, channels = signal.shape
    states = decay_rate.shape[0]
    groups = channels // LANES
    outer = tokens // NEAR
    code_rows = 2 * groups * (states + 1)
    f32 = jnp.float32
    any_space = pl.BlockSpec(memory_space=pl.ANY)
    in_vmem = pl.BlockSpec(memory_space=pltpu.VMEM)
    in_hbm = pl.BlockSpec(memory_space=pltpu.HBM)

    def rows(count, dtype=f32):
        return pltpu.VMEM((count * groups, LANES), dtype)

    def shape(*dims):
        return jax.ShapeDtypeStruct(dims, f32)

    def kept(count):
        return pltpu.HBM((count * groups, LANES), f32)

    def hbm(array):
        return pltpu.with_memory_space_constraint(array, pltpu.HBM)

    def call(kernel, name, flops, **options):
        return pl.pallas_call(
            kernel,
            compiler_params=pltpu.CompilerParams(vmem_limit_bytes=24 * 1024 * 1024),
            cost_estimate=pl.CostEstimate(flops=flops, bytes_accessed=2_000_000, transcendentals=0),
            name=name,
            **options,
        )

    parameters = tuple(hbm(array) for array in (time_step.reshape(groups, LANES), decay_rate, frequency))
    codes = pltpu.HBM((code_rows, LANES), jnp.bfloat16)

    def sums(send):
        return call(
            functools.partial(sums_kernel, n_in, send),
            "sums" if send else "base",
            20_000_000,
            out_shape=codes if send else shape(4 * states * groups, LANES),
            in_specs=[any_space] * 4,
            out_specs=in_hbm if send else in_vmem,
            scratch_shapes=[
                pltpu.VMEM((tokens, channels), signal.dtype),
                rows(1),
                *[pltpu.VMEM((states, channels), f32)] * 2,
                rows(tokens),
                *[rows(states)] * 2,
                rows(4 * states if send else 1),
                pltpu.VMEM((code_rows if send else 16, LANES), jnp.bfloat16),
                pltpu.SemaphoreType.DMA((4,)),
            ],
        )(hbm(signal), *parameters)

    code = sums(True)
    early = [lax.ppermute(code, "seqout", [(i, i + j) for i in range(n_out - j)]) for j in range(1, n_out)]
    parameters = lax.optimization_barrier((code, *parameters))[1:]
    parameters = tuple(hbm(array) for array in parameters)
    base = sums(False)

    *messages, own = call(
        functools.partial(messages_kernel, n_in, n_out - 1),
        "messages",
        4_000_000,
        out_shape=(*[codes] * (n_in - 1), kept(2 * states)),
        in_specs=(in_vmem, any_space, *[in_vmem] * (n_out - 1)),
        out_specs=(in_hbm,) * n_in,
        scratch_shapes=[
            rows(2 * states),
            rows(2 * states),
            pltpu.VMEM((2, code_rows, LANES), jnp.bfloat16),
            pltpu.SemaphoreType.DMA((n_in,)),
        ],
    )(base, hbm(code), *early)

    received = [
        lax.ppermute(messages[d - 1], "seqin", [(i, (i + d) % n_in) for i in range(n_in)]) for d in range(1, n_in)
    ]

    pack = call(
        conv_kernel,
        "conv",
        40_000_000,
        out_shape=shape((tokens + states * (2 * FINAL_NEAR + 6)) * groups, LANES),
        in_specs=[any_space] * 8,
        scratch_shapes=[
            pltpu.VMEM((tokens, channels), signal.dtype),
            rows(1),
            rows(1),
            *[pltpu.VMEM((states, channels), f32)] * 4,
            *[rows(states)] * 4,
            rows(2 * NEAR * states),
            rows(2 * outer * states),
            rows(tokens),
            rows(tokens + 8),
            pltpu.SemaphoreType.DMA((8,)),
        ],
    )(
        hbm(signal), hbm(skip_gain.reshape(groups, LANES)), *parameters,
        hbm(output_real), hbm(output_imag), hbm(own),
    )

    count = min(4, tokens // FINAL_NEAR)
    outputs = call(
        functools.partial(final_kernel, states),
        "final",
        20_000_000,
        out_shape=shape(tokens, channels),
        out_specs=any_space,
        scratch_shapes=[
            rows(2 * states),
            rows(count * FINAL_NEAR),
            pltpu.VMEM((tokens, channels), f32),
            pltpu.SemaphoreType.DMA((tokens // FINAL_NEAR // count,)),
        ],
    )(pack, *received)
    return outputs[None]


def solution(mesh):
    in_specs = (
        P(("groups", "seqout"), "seqin", "chan"),
        P("chan"),
        P(None, "chan"),
        P(None, "chan"),
        P(None, "chan"),
        P(None, "chan"),
        P("chan"),
    )
    out_specs = P(("groups", "seqout"), "seqin", "chan")
    return jax.shard_map(
        functools.partial(per_device, mesh.shape["seqin"], mesh.shape["seqout"]),
        mesh=mesh,
        in_specs=in_specs,
        out_specs=out_specs,
        check_vma=False,
    )
```

```python
import functools

import jax
import jax.numpy as jnp
from jax import lax
from jax.experimental import pallas as pl
from jax.experimental.pallas import tpu as pltpu
from jax.sharding import PartitionSpec as P

LANES = 128
NEAR = 16
FINAL_NEAR = 8
SUM_NEAR = 8
HALF_RANGE = 125.0
LOG_TWO = 0.6931471805599453
SMALLEST_CODE = 2.0**-125


def cmul(a, b):
    return (a[0] * b[0] - a[1] * b[1], a[0] * b[1] + a[1] * b[0])


def cos_sin(angle):
    turns = jnp.floor(angle * 0.6366197723675814 + 0.5)
    rest = angle - turns * 1.5703125
    rest = rest - turns * 4.837512969970703125e-4
    rest = rest - turns * 7.549789948768648e-8
    square = rest * rest
    sine = rest + rest * square * (
        -1.6666654611e-1 + square * (8.3321608736e-3 - square * 1.9515295891e-4)
    )
    cosine = (
        1.0
        - 0.5 * square
        + square * square * (4.166664568298827e-2 + square * (-1.388731625493765e-3 + square * 2.443315711809948e-5))
    )
    quarter = turns.astype(jnp.int32) & 3
    swap = (quarter & 1) == 1
    first = jnp.where(swap, sine, cosine)
    second = jnp.where(swap, cosine, sine)
    return (
        jnp.where((quarter == 1) | (quarter == 2), -first, first),
        jnp.where(quarter >= 2, -second, second),
    )


def decay_step(time_step, decay_rate, frequency):
    fade_rate = time_step * decay_rate
    shrink = jnp.exp(-fade_rate)
    cosine, sine = cos_sin(time_step * frequency)
    return (fade_rate, (shrink * cosine, shrink * sine))


def gain_of(fade_rate):
    double = 2.0 * fade_rate
    series = 1.0 / 40320.0
    for factor in (5040.0, 720.0, 120.0, 24.0, 6.0, 2.0, 1.0):
        series = 1.0 / factor - double * series
    small = double * series
    return jnp.sqrt(jnp.where(double < 0.25, small, 1.0 - jnp.exp(-double)))


def power_list(lam, count):
    powers = [None, lam]
    for k in range(2, count + 1):
        powers.append(cmul(powers[k // 2], powers[k - k // 2]))
    return powers


def spread_rows(source_ref, target_ref, rows, groups, stack):
    for start in range(0, rows, stack):
        for k in range(groups):
            part = source_ref[start : start + stack, k * LANES : (k + 1) * LANES]
            target_ref[pl.ds(start * groups + k, stack, stride=groups), :] = part.astype(jnp.float32)


def row_at(ref, index, groups):
    return ref[pl.ds(pl.multiple_of(index * groups, groups), groups), :]


def put_row(ref, index, groups, value):
    ref[pl.ds(pl.multiple_of(index * groups, groups), groups), :] = value


def power_sum(near_ref, lead_of, states, groups, near, count, init):

    def turn(n, acc):
        leads = lead_of(n)
        acc = list(acc)
        for a in range(count):
            acc[a * near] = acc[a * near] + leads[a][0]
        for u in range(1, near):
            real = row_at(near_ref, n * (2 * near) + 2 * u, groups)
            imag = row_at(near_ref, n * (2 * near) + 2 * u + 1, groups)
            for a in range(count):
                slot = a * near + u
                acc[slot] = acc[slot] + (leads[a][0] * real - leads[a][1] * imag)
        return tuple(acc)

    return lax.fori_loop(0, states, turn, tuple(init), unroll=16)


def power_of(base, exponent):
    result = None
    while exponent:
        if exponent & 1:
            result = base if result is None else cmul(result, base)
        exponent //= 2
        if exponent:
            base = cmul(base, base)
    return result


def start_copies(pairs, sems):
    copies = [pltpu.make_async_copy(pair[0], pair[1], sems.at[i]) for i, pair in enumerate(pairs)]
    for copy in copies:
        copy.start()
    return copies


def pair_at(ref, index, groups):
    return tuple(row_at(ref, index + part, groups) for part in range(2))


def put_pair(ref, index, groups, value):
    for part in range(2):
        put_row(ref, index + part, groups, value[part])


def decayed_sum(signal_sp, powers, tokens, groups):
    a_tile = min(4, tokens // SUM_NEAR)
    total = None
    for first in range(0, tokens // SUM_NEAR, a_tile):
        real, imag = [None] * a_tile, [None] * a_tile
        for u in range(SUM_NEAR):
            power = SUM_NEAR - 1 - u
            for a in range(a_tile):
                row = ((first + a) * SUM_NEAR + u) * groups
                drive = signal_sp[row : row + groups, :]
                if power:
                    add_real, add_imag = powers[power][0] * drive, powers[power][1] * drive
                    real[a] = add_real if real[a] is None else real[a] + add_real
                    imag[a] = add_imag if imag[a] is None else imag[a] + add_imag
                else:
                    real[a] = real[a] + drive
        for a in range(a_tile):
            if total is None:
                total = (real[a], imag[a])
            else:
                moved = cmul(powers[SUM_NEAR], total)
                total = (moved[0] + real[a], moved[1] + imag[a])
    return total


def encode(value, inverse):
    code = jnp.exp2(jnp.abs(value) * inverse * (2.0 * HALF_RANGE) - HALF_RANGE)
    return jnp.where(value < 0.0, -code, code)


def decode(code, scale):
    size = (jnp.log(jnp.maximum(jnp.abs(code), SMALLEST_CODE)) * (0.5 / HALF_RANGE / LOG_TWO) + 0.5) * scale
    return jnp.where(code < 0.0, -size, size)


def largest(value, most):
    return jnp.maximum(most, jnp.maximum(jnp.abs(value[0]), jnp.abs(value[1])))


def write_codes(value_of, code_ref, most, states, groups):
    scale = (1.01 * most).astype(jnp.bfloat16).astype(jnp.float32)
    inverse = jnp.where(scale > 1e-36, 1.0 / jnp.maximum(scale, 1e-36), 0.0)
    code_ref[states * 2 * groups :, :] = jnp.concatenate([scale, scale], axis=0).astype(jnp.bfloat16)

    def write(n, carry):
        value = value_of(n)
        code = jnp.concatenate([encode(value[part], inverse) for part in range(2)], axis=0)
        row = pl.multiple_of(n * (2 * groups), 2 * groups)
        code_ref[pl.ds(row, 2 * groups), :] = code.astype(jnp.bfloat16)
        return carry

    lax.fori_loop(0, states, write, 0, unroll=4)


def scale_at(code_ref, states, groups):
    return code_ref[states * 2 * groups :, :].astype(jnp.float32)[0:groups, :]


def decode_at(code_ref, n, scale, groups):
    row = pl.multiple_of(n * (2 * groups), 2 * groups)
    code = code_ref[pl.ds(row, 2 * groups), :].astype(jnp.float32)
    return tuple(decode(code[part * groups : (part + 1) * groups, :], scale) for part in range(2))


def sums_kernel(
    n_in, send, signal_hbm, step_hbm, decay_hbm, freq_hbm,
    result_ref,
    signal_ref, step_ref, decay_ref, freq_ref,
    signal_sp, decay_sp, freq_sp, base_ref, code_ref, sems,
):
    place = lax.axis_index("seqout")
    needed = place < lax.axis_size("seqout") - 1 if send else place > 0

    @pl.when(needed)
    def _():
        copies = start_copies(
            ((step_hbm, step_ref), (decay_hbm, decay_ref), (freq_hbm, freq_ref), (signal_hbm, signal_ref)), sems
        )
        states, channels = decay_ref.shape
        groups = channels // LANES
        tokens = signal_ref.shape[0]
        for copy in copies[:3]:
            copy.wait()
        for source, target in ((decay_ref, decay_sp), (freq_ref, freq_sp)):
            spread_rows(source, target, states, groups, 8)
        copies[3].wait()
        spread_rows(signal_ref, signal_sp, tokens, groups, 16)
        step = step_ref[...]
        target_ref = base_ref if send else result_ref

        def prepare(n, most):
            _, lam = decay_step(step, row_at(decay_sp, n, groups), row_at(freq_sp, n, groups))
            powers = power_list(lam, SUM_NEAR)
            own = decayed_sum(signal_sp, powers, tokens, groups)
            if not send:
                put_pair(target_ref, 4 * n, groups, power_of(powers[SUM_NEAR], tokens // SUM_NEAR * n_in))
            put_pair(target_ref, 4 * n + 2, groups, own)
            return largest(own, most)

        most = lax.fori_loop(0, states, prepare, jnp.zeros((groups, LANES), jnp.float32), unroll=4)
        if send:
            write_codes(lambda n: pair_at(base_ref, 4 * n + 2, groups), code_ref, most, states, groups)
            copy = pltpu.make_async_copy(code_ref, result_ref, sems.at[0])
            copy.start()
            copy.wait()


def messages_kernel(n_in, n_early, base_ref, sent_hbm, *refs):
    received_refs, out_refs, own_hbm = refs[:n_early], refs[n_early : n_early + n_in - 1], refs[n_early + n_in - 1]
    later_ref, own_ref, code_ref, sems = refs[n_early + n_in :]
    groups = (received_refs[0].shape[0] - base_ref.shape[0] // 2) // 2
    states = base_ref.shape[0] // (4 * groups)
    first_block = lax.axis_index("seqout") == 0

    @pl.when(first_block)
    def _():
        copy = pltpu.make_async_copy(sent_hbm, code_ref.at[0], sems.at[0])
        copy.start()
        own_ref[...] = jnp.zeros_like(own_ref)
        code_ref[1] = jnp.zeros_like(code_ref[1])
        copy.wait()

    @pl.when(jnp.logical_not(first_block))
    def _():
        scales = [scale_at(ref, states, groups) for ref in received_refs]

        def gather(n, most):
            block, own = pair_at(base_ref, 4 * n, groups), pair_at(base_ref, 4 * n + 2, groups)
            early = None
            for ref, scale in zip(reversed(received_refs), reversed(scales)):
                part = decode_at(ref, n, scale, groups)
                if early is not None:
                    moved = cmul(block, early)
                    part = (part[0] + moved[0], part[1] + moved[1])
                early = part
            moved = cmul(block, early)
            later = (own[0] + moved[0], own[1] + moved[1])
            put_pair(later_ref, 2 * n, groups, later)
            put_pair(own_ref, 2 * n, groups, early)
            return (largest(later, most[0]), largest(early, most[1]))

        zero = jnp.zeros((groups, LANES), jnp.float32)
        most = lax.fori_loop(0, states, gather, (zero, zero), unroll=4)
        write_codes(lambda n: pair_at(later_ref, 2 * n, groups), code_ref.at[0], most[0], states, groups)
        if n_early == 1:
            code_ref[1] = received_refs[0][...]
        else:
            write_codes(lambda n: pair_at(own_ref, 2 * n, groups), code_ref.at[1], most[1], states, groups)

    place = lax.axis_index("seqin")
    copies = [pltpu.make_async_copy(own_ref, own_hbm, sems.at[0])]
    for d in range(1, n_in):
        kind = (place + d) // n_in
        copies.append(pltpu.make_async_copy(code_ref.at[kind], out_refs[d - 1], sems.at[d]))
    for copy in copies:
        copy.start()
    for copy in copies:
        copy.wait()


def split_pack(pack_ref, tokens, states, groups):
    refs, start = [], 0
    for count in (tokens, states * 2 * FINAL_NEAR, 2 * states, 2 * states, 2 * states):
        refs.append(pack_ref.at[start * groups : (start + count) * groups])
        start += count
    return refs


def conv_kernel(
    signal_hbm, skip_hbm, step_hbm, decay_hbm, freq_hbm, real_hbm, imag_hbm, own_hbm, pack_ref,
    signal_ref, skip_ref, step_ref, decay_ref, freq_ref, real_ref, imag_ref,
    decay_sp, freq_sp, real_sp, imag_sp, near_ref, lead_ref, signal_sp, taps_pad, sems,
):
    tokens, channels = signal_ref.shape
    groups = channels // LANES
    states = decay_ref.shape[0]
    outer = tokens // NEAR
    tile = 8
    out_ref, few_ref, shift_ref, hop_ref, own_ref = split_pack(pack_ref, tokens, states, groups)
    copies = start_copies(
        (
            (step_hbm, step_ref), (decay_hbm, decay_ref), (freq_hbm, freq_ref), (real_hbm, real_ref),
            (imag_hbm, imag_ref), (signal_hbm, signal_ref), (skip_hbm, skip_ref), (own_hbm, own_ref),
        ),
        sems,
    )
    taps_pad[0 : tile * groups, :] = jnp.zeros((tile * groups, LANES), jnp.float32)
    for copy in copies[:5]:
        copy.wait()
    for source, target in ((decay_ref, decay_sp), (freq_ref, freq_sp), (real_ref, real_sp), (imag_ref, imag_sp)):
        spread_rows(source, target, states, groups, 8)
    step = step_ref[...]

    def prepare(n, carry):
        fade, lam = decay_step(step, row_at(decay_sp, n, groups), row_at(freq_sp, n, groups))
        gain = gain_of(fade)
        weight = (2.0 * row_at(real_sp, n, groups), 2.0 * row_at(imag_sp, n, groups))
        lead = (weight[0] * gain, weight[1] * gain)
        powers = power_list(lam, NEAR)
        for u in range(1, NEAR):
            put_pair(near_ref, n * (2 * NEAR) + 2 * u, groups, powers[u])
        for u in range(FINAL_NEAR):
            put_pair(few_ref, n * (2 * FINAL_NEAR) + 2 * u, groups, powers[u if u else FINAL_NEAR])
        put_pair(shift_ref, 2 * n, groups, cmul(lead, lam))
        put_pair(hop_ref, 2 * n, groups, power_of(powers[NEAR], outer))
        for a in range(outer):
            if a:
                lead = cmul(lead, powers[NEAR])
            put_pair(lead_ref, n * (2 * outer) + 2 * a, groups, lead)
        return carry

    lax.fori_loop(0, states, prepare, 0, unroll=2)
    for copy in copies[5:]:
        copy.wait()
    spread_rows(signal_ref, signal_sp, tokens, groups, 16)
    zero = jnp.zeros((groups, LANES), jnp.float32)
    count = min(2, outer)
    for first in range(0, outer, count):

        def lead_of(n, first=first):
            return [pair_at(lead_ref, n * (2 * outer) + 2 * (first + a), groups) for a in range(count)]

        acc = power_sum(near_ref, lead_of, states, groups, NEAR, count, [zero] * (count * NEAR))
        for t in range(count * NEAR):
            put_row(taps_pad, tile + first * NEAR + t, groups, acc[t])

    convolve(signal_sp, taps_pad, skip_ref[...], out_ref, tokens, groups)


def pair_sums_body(signal_hbm, step_hbm, decay_hbm, freq_hbm, base_ref, code_ref, buffers, sems):
    signal_ref, step_ref, decay_ref, freq_ref, signal_sp, decay_sp, freq_sp = buffers
    copies = start_copies(
        ((step_hbm, step_ref), (decay_hbm, decay_ref), (freq_hbm, freq_ref), (signal_hbm, signal_ref)), sems
    )
    states, channels = decay_ref.shape
    groups = channels // LANES
    tokens = signal_ref.shape[0]
    for copy in copies[:3]:
        copy.wait()
    for source, target in ((decay_ref, decay_sp), (freq_ref, freq_sp)):
        spread_rows(source, target, states, groups, 8)
    copies[3].wait()
    spread_rows(signal_ref, signal_sp, tokens, groups, 16)
    step = step_ref[...]

    def prepare(n, most):
        _, lam = decay_step(step, row_at(decay_sp, n, groups), row_at(freq_sp, n, groups))
        powers = power_list(lam, SUM_NEAR)
        own = decayed_sum(signal_sp, powers, tokens, groups)
        put_pair(base_ref, 4 * n, groups, power_of(powers[SUM_NEAR], tokens // SUM_NEAR))
        put_pair(base_ref, 4 * n + 2, groups, own)
        return largest(own, most)

    most = lax.fori_loop(0, states, prepare, jnp.zeros((groups, LANES), jnp.float32), unroll=4)
    write_codes(lambda n: pair_at(base_ref, 4 * n + 2, groups), code_ref, most, states, groups)


def pair_sums_kernel(
    first_block, signal_hbm, step_hbm, decay_hbm, freq_hbm, *rest
):
    if not first_block:
        rest = rest[2:]
    *out_refs, signal_ref, step_ref, decay_ref, freq_ref, signal_sp, decay_sp, freq_sp, base_ref, code_ref, sems = rest
    buffers = (signal_ref, step_ref, decay_ref, freq_ref, signal_sp, decay_sp, freq_sp)

    @pl.when((lax.axis_index("seqout") == 0) == first_block)
    def _():
        pair_sums_body(signal_hbm, step_hbm, decay_hbm, freq_hbm, base_ref, code_ref, buffers, sems)
        pairs = [(base_ref, out_refs[0])] + [(code_ref, ref) for ref in out_refs[1:]]
        for copy in start_copies(pairs, sems):
            copy.wait()


def joined(hop, mine, other, second):
    before = tuple(jnp.where(second, other[part], mine[part]) for part in range(2))
    after = tuple(jnp.where(second, mine[part], other[part]) for part in range(2))
    moved = cmul(hop, before)
    return (moved[0] + after[0], moved[1] + after[1])


def pair_early_kernel(base_ref, early_ref, early_partner_ref, held_ref):
    groups = (early_ref.shape[0] - base_ref.shape[0] // 2) // 2
    states = base_ref.shape[0] // (4 * groups)
    second = lax.rem(lax.axis_index("seqin"), 2) == 1
    scales = [scale_at(ref, states, groups) for ref in (early_ref, early_partner_ref)]

    def gather(n, carry):
        hop = pair_at(base_ref, 4 * n, groups)
        early, early_partner = (
            decode_at(ref, n, scale, groups) for ref, scale in zip((early_ref, early_partner_ref), scales)
        )
        put_pair(held_ref, 6 * n, groups, hop)
        put_pair(held_ref, 6 * n + 2, groups, pair_at(base_ref, 4 * n + 2, groups))
        put_pair(held_ref, 6 * n + 4, groups, joined(hop, early, early_partner, second))
        return carry

    lax.fori_loop(0, states, gather, 0, unroll=4)


def pair_message_kernel(held_ref, partner_ref, message_hbm, known_hbm, *scratch):
    message_ref, known_ref, code_ref, sems = scratch
    groups = (partner_ref.shape[0] - held_ref.shape[0] // 3) // 2
    states = held_ref.shape[0] // (6 * groups)
    place = lax.axis_index("seqin")
    second = lax.rem(place, 2) == 1
    upper = place >= 2
    scale = scale_at(partner_ref, states, groups)

    def gather(n, most):
        hop, own, early_total = (pair_at(held_ref, 6 * n + 2 * i, groups) for i in range(3))
        partner = decode_at(partner_ref, n, scale, groups)
        total = joined(hop, own, partner, second)
        hop2 = cmul(hop, hop)
        moved2 = cmul(hop2, early_total)
        moved4 = cmul(hop2, moved2)
        moved3 = cmul(hop, moved2)
        message = tuple(jnp.where(upper, early_total[part], total[part] + moved4[part]) for part in range(2))
        known = tuple(jnp.where(second, moved3[part] + partner[part], moved2[part]) for part in range(2))
        put_pair(message_ref, 2 * n, groups, message)
        put_pair(known_ref, 2 * n, groups, known)
        return largest(message, most)

    most = lax.fori_loop(0, states, gather, jnp.zeros((groups, LANES), jnp.float32), unroll=4)
    known_copy = pltpu.make_async_copy(known_ref, known_hbm, sems.at[0])
    known_copy.start()
    write_codes(lambda n: pair_at(message_ref, 2 * n, groups), code_ref, most, states, groups)
    copy = pltpu.make_async_copy(code_ref, message_hbm, sems.at[1])
    copy.start()
    known_copy.wait()
    copy.wait()


def taps_kernel(
    step_hbm, decay_hbm, freq_hbm, real_hbm, imag_hbm, base_hbm,
    taps_hbm, tables_hbm, late_hbm, base_ref,
    step_ref, decay_ref, freq_ref, real_ref, imag_ref,
    decay_sp, freq_sp, real_sp, imag_sp, near_ref, lead_ref, late_ref, taps_ref, tables_ref, sems,
):
    copies = start_copies(
        (
            (step_hbm, step_ref), (decay_hbm, decay_ref), (freq_hbm, freq_ref), (real_hbm, real_ref),
            (imag_hbm, imag_ref), (base_hbm, base_ref),
        ),
        sems,
    )
    states, channels = decay_ref.shape
    groups = channels // LANES
    half = taps_ref.shape[0] // groups
    outer = half // NEAR
    shift_row, hop_row = states * 2 * FINAL_NEAR, states * (2 * FINAL_NEAR + 2)
    for copy in copies[:5]:
        copy.wait()
    for source, target in ((decay_ref, decay_sp), (freq_ref, freq_sp), (real_ref, real_sp), (imag_ref, imag_sp)):
        spread_rows(source, target, states, groups, 8)
    step = step_ref[...]

    def prepare(n, carry):
        fade, lam = decay_step(step, row_at(decay_sp, n, groups), row_at(freq_sp, n, groups))
        gain = gain_of(fade)
        weight = (2.0 * row_at(real_sp, n, groups), 2.0 * row_at(imag_sp, n, groups))
        lead = (weight[0] * gain, weight[1] * gain)
        powers = power_list(lam, NEAR)
        for u in range(1, NEAR):
            put_pair(near_ref, n * (2 * NEAR) + 2 * u, groups, powers[u])
        for u in range(FINAL_NEAR):
            put_pair(tables_ref, n * (2 * FINAL_NEAR) + 2 * u, groups, powers[u if u else FINAL_NEAR])
        put_pair(tables_ref, shift_row + 2 * n, groups, cmul(lead, lam))
        put_pair(tables_ref, hop_row + 2 * n, groups, power_of(powers[NEAR], 2 * outer))
        for a in range(outer):
            if a:
                lead = cmul(lead, powers[NEAR])
            put_pair(lead_ref, n * (2 * outer) + 2 * a, groups, lead)
        put_pair(late_ref, 2 * n, groups, cmul(lead, powers[NEAR]))
        return carry

    lax.fori_loop(0, states, prepare, 0, unroll=2)
    copies[5].wait()
    tables_copies = start_copies(((tables_ref, tables_hbm), (late_ref, late_hbm)), sems)
    zero = jnp.zeros((groups, LANES), jnp.float32)
    count = min(2, outer)
    for first in range(0, outer, count):

        def lead_of(n, first=first):
            return [pair_at(lead_ref, n * (2 * outer) + 2 * (first + a), groups) for a in range(count)]

        acc = power_sum(near_ref, lead_of, states, groups, NEAR, count, [zero] * (count * NEAR))
        for t in range(count * NEAR):
            put_row(taps_ref, first * NEAR + t, groups, acc[t])
    taps_copy = pltpu.make_async_copy(taps_ref, taps_hbm, sems.at[2])
    taps_copy.start()
    for copy in tables_copies:
        copy.wait()
    taps_copy.wait()


def convolve(signal_sp, taps_pad, skip, out_ref, tokens, groups, low=0, high=None):
    tile = 8

    def col_tile(ji, acc, ti):
        gap = (ti - ji) * tile + 1
        window = [row_at(taps_pad, gap + m, groups) for m in range(2 * tile - 1)]
        acc = list(acc)
        for j in range(tile):
            drive = row_at(signal_sp, ji * tile + j, groups)
            for t in range(tile):
                acc[t] = acc[t] + window[t - j + tile - 1] * drive
        return tuple(acc)

    for ti in range(low, tokens // tile):
        first = 0 if high is None else max(0, ti - high + 1)
        if low:
            init = tuple(row_at(out_ref, ti * tile + t, groups) for t in range(tile))
        else:
            init = tuple(skip * row_at(signal_sp, ti * tile + t, groups) for t in range(tile))
        acc = lax.fori_loop(first, ti - low + 1, functools.partial(col_tile, ti=ti), init, unroll=4)
        for t in range(tile):
            put_row(out_ref, ti * tile + t, groups, acc[t])


def pair_conv_kernel(
    signal_hbm, skip_hbm, taps_hbm, tables_hbm, known_hbm, late_hbm, pack_ref,
    signal_ref, skip_ref, late_ref, signal_sp, taps_pad, sems,
):
    tokens, channels = signal_ref.shape
    groups = channels // LANES
    states = late_ref.shape[0] // (2 * groups)
    half, tile = tokens // 2, 8
    first, last = tokens * groups, tokens * groups + tables_hbm.shape[0]
    near_ref = pack_ref.at[first:last]
    copies = start_copies(
        (
            (signal_hbm, signal_ref), (skip_hbm, skip_ref),
            (taps_hbm, taps_pad.at[tile * groups : (tile + half) * groups]),
            (late_hbm, late_ref), (tables_hbm, near_ref),
            (known_hbm, pack_ref.at[last : last + known_hbm.shape[0]]),
        ),
        sems,
    )
    taps_pad[0 : tile * groups, :] = jnp.zeros((tile * groups, LANES), jnp.float32)
    for copy in copies[:3]:
        copy.wait()
    spread_rows(signal_ref, signal_sp, tokens, groups, 16)
    skip = skip_ref[...]
    out_ref = pack_ref.at[0:first]
    convolve(signal_sp, taps_pad, skip, out_ref, tokens, groups, 0, half // tile)
    for copy in copies[3:]:
        copy.wait()
    zero = jnp.zeros((groups, LANES), jnp.float32)
    count = 4

    def lead_of(n):
        hop = pair_at(near_ref, n * (2 * FINAL_NEAR), groups)
        leads = [pair_at(late_ref, 2 * n, groups)]
        for _ in range(count):
            leads.append(cmul(leads[-1], hop))
        put_pair(late_ref, 2 * n, groups, leads[count])
        return leads

    for start in range(half, tokens, count * FINAL_NEAR):
        acc = power_sum(near_ref, lead_of, states, groups, FINAL_NEAR, count, [zero] * (count * FINAL_NEAR))
        for t in range(count * FINAL_NEAR):
            put_row(taps_pad, tile + start + t, groups, acc[t])
    convolve(signal_sp, taps_pad, skip, out_ref, tokens, groups, half // tile)


def final_kernel(states, pairs, pack_ref, *refs):
    message_refs, out_ref = refs[:-5], refs[-5]
    state_sp, rows_ref, out_buf, sems = refs[-4:]
    tokens, channels = out_ref.shape
    groups = channels // LANES
    near = FINAL_NEAR
    outer = tokens // near
    local_ref, near_ref, shift_ref, hop_ref, own_ref = split_pack(pack_ref, tokens, states, groups)
    scales = [scale_at(ref, states, groups) for ref in message_refs]
    second = lax.rem(lax.axis_index("seqin"), 2).astype(jnp.float32)

    def enter(n, carry):
        hop = pair_at(hop_ref, 2 * n, groups)
        state = pair_at(own_ref, 2 * n, groups)
        if pairs:
            part = decode_at(message_refs[0], n, scales[0], groups)
            moved = cmul((1.0 + second * (hop[0] - 1.0), second * hop[1]), part)
            state = (moved[0] + state[0], moved[1] + state[1])
            put_pair(state_sp, 2 * n, groups, cmul(pair_at(shift_ref, 2 * n, groups), state))
            return carry
        for ref, scale in zip(reversed(message_refs), reversed(scales)):
            moved, part = cmul(hop, state), decode_at(ref, n, scale, groups)
            state = (moved[0] + part[0], moved[1] + part[1])
        put_pair(state_sp, 2 * n, groups, cmul(pair_at(shift_ref, 2 * n, groups), state))
        return carry

    lax.fori_loop(0, states, enter, 0, unroll=4)
    count = min(4, outer)
    span = count * near
    copies = []
    for index in range(outer // count):
        last = index + 1 == outer // count

        def lead_of(n, last=last):
            hop = pair_at(near_ref, n * (2 * near), groups)
            leads = [pair_at(state_sp, 2 * n, groups)]
            for _ in range(count - 1 if last else count):
                leads.append(cmul(leads[-1], hop))
            if not last:
                for part in range(2):
                    put_row(state_sp, 2 * n + part, groups, leads[count][part])
            return leads

        start = index * span
        init = [local_ref[(start + t) * groups : (start + t + 1) * groups, :] for t in range(span)]
        acc = power_sum(near_ref, lead_of, states, groups, near, count, init)
        for t in range(span):
            rows_ref[t * groups : (t + 1) * groups, :] = acc[t]
        for t in range(0, span, 8):
            for k in range(groups):
                out_buf[start + t : start + t + 8, k * LANES : (k + 1) * LANES] = rows_ref[
                    pl.ds(t * groups + k, 8, stride=groups), :
                ]
        copy = pltpu.make_async_copy(
            out_buf.at[pl.ds(start, span)], out_ref.at[pl.ds(start, span)], sems.at[index]
        )
        copy.start()
        copies.append(copy)
    for copy in copies:
        copy.wait()


def per_device(n_in, n_out, inputs, time_step, decay_rate, frequency, output_real, output_imag, skip_gain):
    signal = inputs[0]
    tokens, channels = signal.shape
    states = decay_rate.shape[0]
    groups = channels // LANES
    outer = tokens // NEAR
    code_rows = 2 * groups * (states + 1)
    f32 = jnp.float32
    any_space = pl.BlockSpec(memory_space=pl.ANY)
    in_vmem = pl.BlockSpec(memory_space=pltpu.VMEM)
    in_hbm = pl.BlockSpec(memory_space=pltpu.HBM)

    def rows(count, dtype=f32):
        return pltpu.VMEM((count * groups, LANES), dtype)

    def shape(*dims):
        return jax.ShapeDtypeStruct(dims, f32)

    def kept(count):
        return pltpu.HBM((count * groups, LANES), f32)

    def hbm(array):
        return pltpu.with_memory_space_constraint(array, pltpu.HBM)

    def call(kernel, name, flops, **options):
        return pl.pallas_call(
            kernel,
            compiler_params=pltpu.CompilerParams(vmem_limit_bytes=24 * 1024 * 1024),
            cost_estimate=pl.CostEstimate(flops=flops, bytes_accessed=2_000_000, transcendentals=0),
            name=name,
            **options,
        )

    parameters = tuple(hbm(array) for array in (time_step.reshape(groups, LANES), decay_rate, frequency))
    codes = pltpu.HBM((code_rows, LANES), jnp.bfloat16)

    pairs = (n_in, n_out) == (4, 2) and tokens == 128
    if pairs:
        sum_buffers = [
            pltpu.VMEM((tokens, channels), signal.dtype),
            rows(1),
            *[pltpu.VMEM((states, channels), f32)] * 2,
            rows(tokens),
            *[rows(states)] * 2,
        ]
        code_buffer = pltpu.VMEM((code_rows, LANES), jnp.bfloat16)
        sum_scratch = [*sum_buffers, rows(4 * states), code_buffer, pltpu.SemaphoreType.DMA((4,))]
        base, kept_code, code = call(
            functools.partial(pair_sums_kernel, True),
            "sums",
            20_000_000,
            out_shape=(kept(4 * states), codes, codes),
            in_specs=[any_space] * 4,
            out_specs=(in_hbm,) * 3,
            scratch_shapes=sum_scratch,
        )(hbm(signal), *parameters)
        across = lax.ppermute(
            code, ("seqin", "seqout"), [(z * n_out, (z ^ 1) * n_out + 1) for z in range(n_in)]
        )
        early = lax.ppermute(code, "seqout", [(0, 1)])
        base, code = call(
            functools.partial(pair_sums_kernel, False),
            "base",
            20_000_000,
            out_shape=(kept(4 * states), codes),
            in_specs=[any_space] * 4 + [in_hbm] * 2,
            out_specs=(in_hbm,) * 2,
            input_output_aliases={4: 0, 5: 1},
            scratch_shapes=sum_scratch,
        )(hbm(signal), *parameters, base, kept_code)
        partner = lax.ppermute(code, "seqin", [(z, z ^ 1) for z in range(n_in)])

        table_rows = states * (2 * FINAL_NEAR + 4)
        taps, tables, late, base = call(
            taps_kernel,
            "taps",
            24_000_000,
            out_shape=(kept(tokens // 2), kept(table_rows), kept(2 * states), shape(4 * states * groups, LANES)),
            in_specs=[any_space] * 6,
            out_specs=(in_hbm, in_hbm, in_hbm, in_vmem),
            scratch_shapes=[
                rows(1),
                *[pltpu.VMEM((states, channels), f32)] * 4,
                *[rows(states)] * 4,
                rows(2 * NEAR * states),
                rows(outer * states),
                rows(2 * states),
                rows(tokens // 2),
                rows(table_rows),
                pltpu.SemaphoreType.DMA((6,)),
            ],
        )(*parameters, hbm(output_real), hbm(output_imag), hbm(base))

        held = call(
            pair_early_kernel,
            "early",
            100_000_000,
            out_shape=shape(6 * states * groups, LANES),
            in_specs=[in_vmem] * 3,
        )(base, early, across)

        message, own = call(
            pair_message_kernel,
            "messages",
            6_000_000,
            out_shape=(codes, kept(2 * states)),
            in_specs=[in_vmem] * 2,
            out_specs=(in_hbm, in_hbm),
            scratch_shapes=[
                rows(2 * states),
                rows(2 * states),
                code_buffer,
                pltpu.SemaphoreType.DMA((2,)),
            ],
        )(held, partner)

        received = [lax.ppermute(message, "seqin", [(z, z ^ 2) for z in range(n_in)])]

        pack = call(
            pair_conv_kernel,
            "conv",
            18_000_000,
            out_shape=shape((tokens + table_rows + 2 * states) * groups, LANES),
            in_specs=[any_space] * 6,
            scratch_shapes=[
                pltpu.VMEM((tokens, channels), signal.dtype),
                rows(1),
                rows(2 * states),
                rows(tokens),
                rows(tokens + 8),
                pltpu.SemaphoreType.DMA((6,)),
            ],
        )(hbm(signal), hbm(skip_gain.reshape(groups, LANES)), hbm(taps), hbm(tables), hbm(own), hbm(late))
    else:
        def sums(send, given):
            return call(
                functools.partial(sums_kernel, n_in, send),
                "sums" if send else "base",
                20_000_000,
                out_shape=codes if send else shape(4 * states * groups, LANES),
                in_specs=[any_space] * 4,
                out_specs=in_hbm if send else in_vmem,
                scratch_shapes=[
                    pltpu.VMEM((tokens, channels), signal.dtype),
                    rows(1),
                    *[pltpu.VMEM((states, channels), f32)] * 2,
                    rows(tokens),
                    *[rows(states)] * 2,
                    rows(4 * states if send else 1),
                    pltpu.VMEM((code_rows if send else 16, LANES), jnp.bfloat16),
                    pltpu.SemaphoreType.DMA((4,)),
                ],
            )(hbm(signal), *given)

        code = sums(True, parameters)
        early = [lax.ppermute(code, "seqout", [(i, i + j) for i in range(n_out - j)]) for j in range(1, n_out)]
        later = lax.optimization_barrier((code, *parameters))[1:]
        parameters = tuple(hbm(array) for array in later)
        base = sums(False, parameters)

        *messages, own = call(
            functools.partial(messages_kernel, n_in, n_out - 1),
            "messages",
            4_000_000,
            out_shape=(*[codes] * (n_in - 1), kept(2 * states)),
            in_specs=(in_vmem, any_space, *[in_vmem] * (n_out - 1)),
            out_specs=(in_hbm,) * n_in,
            scratch_shapes=[
                rows(2 * states),
                rows(2 * states),
                pltpu.VMEM((2, code_rows, LANES), jnp.bfloat16),
                pltpu.SemaphoreType.DMA((n_in,)),
            ],
        )(base, hbm(code), *early)

        received = [
            lax.ppermute(messages[d - 1], "seqin", [(i, (i + d) % n_in) for i in range(n_in)]) for d in range(1, n_in)
        ]

        pack = call(
            conv_kernel,
            "conv",
            40_000_000,
            out_shape=shape((tokens + states * (2 * FINAL_NEAR + 6)) * groups, LANES),
            in_specs=[any_space] * 8,
            scratch_shapes=[
                pltpu.VMEM((tokens, channels), signal.dtype),
                rows(1),
                rows(1),
                *[pltpu.VMEM((states, channels), f32)] * 4,
                *[rows(states)] * 4,
                rows(2 * NEAR * states),
                rows(2 * outer * states),
                rows(tokens),
                rows(tokens + 8),
                pltpu.SemaphoreType.DMA((8,)),
            ],
        )(
            hbm(signal), hbm(skip_gain.reshape(groups, LANES)), *parameters,
            hbm(output_real), hbm(output_imag), hbm(own),
        )

    count = min(4, tokens // FINAL_NEAR)
    outputs = call(
        functools.partial(final_kernel, states, pairs),
        "final",
        20_000_000,
        out_shape=shape(tokens, channels),
        out_specs=any_space,
        scratch_shapes=[
            rows(2 * states),
            rows(count * FINAL_NEAR),
            pltpu.VMEM((tokens, channels), f32),
            pltpu.SemaphoreType.DMA((tokens // FINAL_NEAR // count,)),
        ],
    )(pack, *received)
    return outputs[None]


def solution(mesh):
    in_specs = (
        P(("groups", "seqout"), "seqin", "chan"),
        P("chan"),
        P(None, "chan"),
        P(None, "chan"),
        P(None, "chan"),
        P(None, "chan"),
        P("chan"),
    )
    out_specs = P(("groups", "seqout"), "seqin", "chan")
    return jax.shard_map(
        functools.partial(per_device, mesh.shape["seqin"], mesh.shape["seqout"]),
        mesh=mesh,
        in_specs=in_specs,
        out_specs=out_specs,
        check_vma=False,
    )
```

```python
import functools

import jax
import jax.numpy as jnp
from jax import lax
from jax.experimental import pallas as pl
from jax.experimental.pallas import tpu as pltpu
from jax.sharding import PartitionSpec as P

LANES = 128
NEAR = 16
FINAL_NEAR = 16
SUM_NEAR = 8
HALF_RANGE = 125.0
LOG_TWO = 0.6931471805599453
SMALLEST_CODE = 2.0**-125


def cmul(a, b):
    return (a[0] * b[0] - a[1] * b[1], a[0] * b[1] + a[1] * b[0])


def cos_sin(angle):
    turns = jnp.floor(angle * 0.6366197723675814 + 0.5)
    rest = angle - turns * 1.5703125
    rest = rest - turns * 4.837512969970703125e-4
    rest = rest - turns * 7.549789948768648e-8
    square = rest * rest
    sine = rest + rest * square * (
        -1.6666654611e-1 + square * (8.3321608736e-3 - square * 1.9515295891e-4)
    )
    cosine = (
        1.0
        - 0.5 * square
        + square * square * (4.166664568298827e-2 + square * (-1.388731625493765e-3 + square * 2.443315711809948e-5))
    )
    quarter = turns.astype(jnp.int32) & 3
    swap = (quarter & 1) == 1
    first = jnp.where(swap, sine, cosine)
    second = jnp.where(swap, cosine, sine)
    return (
        jnp.where((quarter == 1) | (quarter == 2), -first, first),
        jnp.where(quarter >= 2, -second, second),
    )


def decay_step(time_step, decay_rate, frequency):
    fade_rate = time_step * decay_rate
    shrink = jnp.exp(-fade_rate)
    cosine, sine = cos_sin(time_step * frequency)
    return (fade_rate, (shrink * cosine, shrink * sine))


def gain_of(fade_rate):
    double = 2.0 * fade_rate
    series = 1.0 / 40320.0
    for factor in (5040.0, 720.0, 120.0, 24.0, 6.0, 2.0, 1.0):
        series = 1.0 / factor - double * series
    small = double * series
    return jnp.sqrt(jnp.where(double < 0.25, small, 1.0 - jnp.exp(-double)))


def power_list(lam, count):
    powers = [None, lam]
    for k in range(2, count + 1):
        powers.append(cmul(powers[k // 2], powers[k - k // 2]))
    return powers


def spread_rows(source_ref, target_ref, rows, groups, stack):
    for start in range(0, rows, stack):
        for k in range(groups):
            part = source_ref[start : start + stack, k * LANES : (k + 1) * LANES]
            target_ref[pl.ds(start * groups + k, stack, stride=groups), :] = part.astype(jnp.float32)


def row_at(ref, index, groups):
    return ref[pl.ds(pl.multiple_of(index * groups, groups), groups), :]


def put_row(ref, index, groups, value):
    ref[pl.ds(pl.multiple_of(index * groups, groups), groups), :] = value


def power_sum(near_ref, lead_of, states, groups, near, count, init):

    def turn(n, acc):
        leads = lead_of(n)
        acc = list(acc)
        for a in range(count):
            acc[a * near] = acc[a * near] + leads[a][0]
        for u in range(1, near):
            real = row_at(near_ref, n * (2 * near) + 2 * u, groups)
            imag = row_at(near_ref, n * (2 * near) + 2 * u + 1, groups)
            for a in range(count):
                slot = a * near + u
                acc[slot] = acc[slot] + (leads[a][0] * real - leads[a][1] * imag)
        return tuple(acc)

    return lax.fori_loop(0, states, turn, tuple(init), unroll=32)


def power_of(base, exponent):
    result = None
    while exponent:
        if exponent & 1:
            result = base if result is None else cmul(result, base)
        exponent //= 2
        if exponent:
            base = cmul(base, base)
    return result


def start_copies(pairs, sems):
    copies = [pltpu.make_async_copy(pair[0], pair[1], sems.at[i]) for i, pair in enumerate(pairs)]
    for copy in copies:
        copy.start()
    return copies


def pair_at(ref, index, groups):
    return tuple(row_at(ref, index + part, groups) for part in range(2))


def put_pair(ref, index, groups, value):
    for part in range(2):
        put_row(ref, index + part, groups, value[part])


def decayed_sum(signal_sp, powers, tokens, groups):
    a_tile = min(4, tokens // SUM_NEAR)
    total = None
    for first in range(0, tokens // SUM_NEAR, a_tile):
        real, imag = [None] * a_tile, [None] * a_tile
        for u in range(SUM_NEAR):
            power = SUM_NEAR - 1 - u
            for a in range(a_tile):
                row = ((first + a) * SUM_NEAR + u) * groups
                drive = signal_sp[row : row + groups, :]
                if power:
                    add_real, add_imag = powers[power][0] * drive, powers[power][1] * drive
                    real[a] = add_real if real[a] is None else real[a] + add_real
                    imag[a] = add_imag if imag[a] is None else imag[a] + add_imag
                else:
                    real[a] = real[a] + drive
        for a in range(a_tile):
            if total is None:
                total = (real[a], imag[a])
            else:
                moved = cmul(powers[SUM_NEAR], total)
                total = (moved[0] + real[a], moved[1] + imag[a])
    return total


def encode(value, inverse):
    code = jnp.exp2(jnp.abs(value) * inverse * (2.0 * HALF_RANGE) - HALF_RANGE)
    return jnp.where(value < 0.0, -code, code)


def decode(code, scale):
    size = (jnp.log(jnp.maximum(jnp.abs(code), SMALLEST_CODE)) * (0.5 / HALF_RANGE / LOG_TWO) + 0.5) * scale
    return jnp.where(code < 0.0, -size, size)


def largest(value, most):
    return jnp.maximum(most, jnp.maximum(jnp.abs(value[0]), jnp.abs(value[1])))


def write_codes(value_of, code_ref, most, states, groups):
    scale = (1.01 * most).astype(jnp.bfloat16).astype(jnp.float32)
    inverse = jnp.where(scale > 1e-36, 1.0 / jnp.maximum(scale, 1e-36), 0.0)
    code_ref[states * 2 * groups :, :] = jnp.concatenate([scale, scale], axis=0).astype(jnp.bfloat16)

    def write(n, carry):
        value = value_of(n)
        code = jnp.concatenate([encode(value[part], inverse) for part in range(2)], axis=0)
        row = pl.multiple_of(n * (2 * groups), 2 * groups)
        code_ref[pl.ds(row, 2 * groups), :] = code.astype(jnp.bfloat16)
        return carry

    lax.fori_loop(0, states, write, 0, unroll=4)


def scale_at(code_ref, states, groups):
    return code_ref[states * 2 * groups :, :].astype(jnp.float32)[0:groups, :]


def decode_at(code_ref, n, scale, groups):
    row = pl.multiple_of(n * (2 * groups), 2 * groups)
    code = code_ref[pl.ds(row, 2 * groups), :].astype(jnp.float32)
    return tuple(decode(code[part * groups : (part + 1) * groups, :], scale) for part in range(2))


def sums_kernel(
    n_in, send, signal_hbm, step_hbm, decay_hbm, freq_hbm,
    result_ref,
    signal_ref, step_ref, decay_ref, freq_ref,
    signal_sp, decay_sp, freq_sp, base_ref, code_ref, sems,
):
    place = lax.axis_index("seqout")
    needed = place < lax.axis_size("seqout") - 1 if send else place > 0

    @pl.when(needed)
    def _():
        copies = start_copies(
            ((step_hbm, step_ref), (decay_hbm, decay_ref), (freq_hbm, freq_ref), (signal_hbm, signal_ref)), sems
        )
        states, channels = decay_ref.shape
        groups = channels // LANES
        tokens = signal_ref.shape[0]
        for copy in copies[:3]:
            copy.wait()
        for source, target in ((decay_ref, decay_sp), (freq_ref, freq_sp)):
            spread_rows(source, target, states, groups, 8)
        copies[3].wait()
        spread_rows(signal_ref, signal_sp, tokens, groups, 16)
        step = step_ref[...]
        target_ref = base_ref if send else result_ref

        def prepare(n, most):
            _, lam = decay_step(step, row_at(decay_sp, n, groups), row_at(freq_sp, n, groups))
            powers = power_list(lam, SUM_NEAR)
            own = decayed_sum(signal_sp, powers, tokens, groups)
            if not send:
                put_pair(target_ref, 4 * n, groups, power_of(powers[SUM_NEAR], tokens // SUM_NEAR * n_in))
            put_pair(target_ref, 4 * n + 2, groups, own)
            return largest(own, most)

        most = lax.fori_loop(0, states, prepare, jnp.zeros((groups, LANES), jnp.float32), unroll=4)
        if send:
            write_codes(lambda n: pair_at(base_ref, 4 * n + 2, groups), code_ref, most, states, groups)
            copy = pltpu.make_async_copy(code_ref, result_ref, sems.at[0])
            copy.start()
            copy.wait()


def messages_kernel(n_in, n_early, base_ref, sent_hbm, *refs):
    received_refs, out_refs, own_hbm = refs[:n_early], refs[n_early : n_early + n_in - 1], refs[n_early + n_in - 1]
    later_ref, own_ref, code_ref, sems = refs[n_early + n_in :]
    groups = (received_refs[0].shape[0] - base_ref.shape[0] // 2) // 2
    states = base_ref.shape[0] // (4 * groups)
    first_block = lax.axis_index("seqout") == 0

    @pl.when(first_block)
    def _():
        copy = pltpu.make_async_copy(sent_hbm, code_ref.at[0], sems.at[0])
        copy.start()
        own_ref[...] = jnp.zeros_like(own_ref)
        code_ref[1] = jnp.zeros_like(code_ref[1])
        copy.wait()

    @pl.when(jnp.logical_not(first_block))
    def _():
        scales = [scale_at(ref, states, groups) for ref in received_refs]

        def gather(n, most):
            block, own = pair_at(base_ref, 4 * n, groups), pair_at(base_ref, 4 * n + 2, groups)
            early = None
            for ref, scale in zip(reversed(received_refs), reversed(scales)):
                part = decode_at(ref, n, scale, groups)
                if early is not None:
                    moved = cmul(block, early)
                    part = (part[0] + moved[0], part[1] + moved[1])
                early = part
            moved = cmul(block, early)
            later = (own[0] + moved[0], own[1] + moved[1])
            put_pair(later_ref, 2 * n, groups, later)
            put_pair(own_ref, 2 * n, groups, early)
            return (largest(later, most[0]), largest(early, most[1]))

        zero = jnp.zeros((groups, LANES), jnp.float32)
        most = lax.fori_loop(0, states, gather, (zero, zero), unroll=4)
        write_codes(lambda n: pair_at(later_ref, 2 * n, groups), code_ref.at[0], most[0], states, groups)
        if n_early == 1:
            code_ref[1] = received_refs[0][...]
        else:
            write_codes(lambda n: pair_at(own_ref, 2 * n, groups), code_ref.at[1], most[1], states, groups)

    place = lax.axis_index("seqin")
    copies = [pltpu.make_async_copy(own_ref, own_hbm, sems.at[0])]
    for d in range(1, n_in):
        kind = (place + d) // n_in
        copies.append(pltpu.make_async_copy(code_ref.at[kind], out_refs[d - 1], sems.at[d]))
    for copy in copies:
        copy.start()
    for copy in copies:
        copy.wait()


def split_pack(pack_ref, tokens, states, groups):
    refs, start = [], 0
    for count in (tokens, states * 2 * FINAL_NEAR, 2 * states, 2 * states, 2 * states):
        refs.append(pack_ref.at[start * groups : (start + count) * groups])
        start += count
    return refs


def conv_kernel(
    signal_hbm, skip_hbm, step_hbm, decay_hbm, freq_hbm, real_hbm, imag_hbm, own_hbm, pack_ref,
    signal_ref, skip_ref, step_ref, decay_ref, freq_ref, real_ref, imag_ref,
    decay_sp, freq_sp, real_sp, imag_sp, near_ref, lead_ref, signal_sp, taps_pad, sems,
):
    tokens, channels = signal_ref.shape
    groups = channels // LANES
    states = decay_ref.shape[0]
    outer = tokens // NEAR
    tile = 8
    out_ref, few_ref, shift_ref, hop_ref, own_ref = split_pack(pack_ref, tokens, states, groups)
    copies = start_copies(
        (
            (step_hbm, step_ref), (decay_hbm, decay_ref), (freq_hbm, freq_ref), (real_hbm, real_ref),
            (imag_hbm, imag_ref), (signal_hbm, signal_ref), (skip_hbm, skip_ref), (own_hbm, own_ref),
        ),
        sems,
    )
    taps_pad[0 : tile * groups, :] = jnp.zeros((tile * groups, LANES), jnp.float32)
    for copy in copies[:5]:
        copy.wait()
    for source, target in ((decay_ref, decay_sp), (freq_ref, freq_sp), (real_ref, real_sp), (imag_ref, imag_sp)):
        spread_rows(source, target, states, groups, 8)
    step = step_ref[...]

    def prepare(n, carry):
        fade, lam = decay_step(step, row_at(decay_sp, n, groups), row_at(freq_sp, n, groups))
        gain = gain_of(fade)
        weight = (2.0 * row_at(real_sp, n, groups), 2.0 * row_at(imag_sp, n, groups))
        lead = (weight[0] * gain, weight[1] * gain)
        powers = power_list(lam, NEAR)
        for u in range(1, NEAR):
            put_pair(near_ref, n * (2 * NEAR) + 2 * u, groups, powers[u])
        for u in range(FINAL_NEAR):
            put_pair(few_ref, n * (2 * FINAL_NEAR) + 2 * u, groups, powers[u if u else FINAL_NEAR])
        put_pair(shift_ref, 2 * n, groups, cmul(lead, lam))
        put_pair(hop_ref, 2 * n, groups, power_of(powers[NEAR], outer))
        for a in range(outer):
            if a:
                lead = cmul(lead, powers[NEAR])
            put_pair(lead_ref, n * (2 * outer) + 2 * a, groups, lead)
        return carry

    lax.fori_loop(0, states, prepare, 0, unroll=2)
    for copy in copies[5:]:
        copy.wait()
    spread_rows(signal_ref, signal_sp, tokens, groups, 16)
    zero = jnp.zeros((groups, LANES), jnp.float32)
    count = min(2, outer)
    for first in range(0, outer, count):

        def lead_of(n, first=first):
            return [pair_at(lead_ref, n * (2 * outer) + 2 * (first + a), groups) for a in range(count)]

        acc = power_sum(near_ref, lead_of, states, groups, NEAR, count, [zero] * (count * NEAR))
        for t in range(count * NEAR):
            put_row(taps_pad, tile + first * NEAR + t, groups, acc[t])

    convolve(signal_sp, taps_pad, skip_ref[...], out_ref, tokens, groups)


def pair_sums_body(signal_hbm, step_hbm, decay_hbm, freq_hbm, base_hbm, base_ref, code_ref, buffers, sems):
    signal_ref, step_ref, decay_ref, freq_ref, signal_sp, decay_sp, freq_sp = buffers
    copies = start_copies(
        ((step_hbm, step_ref), (decay_hbm, decay_ref), (freq_hbm, freq_ref), (signal_hbm, signal_ref)), sems
    )
    states, channels = decay_ref.shape
    groups = channels // LANES
    tokens = signal_ref.shape[0]
    for copy in copies[:3]:
        copy.wait()
    for source, target in ((decay_ref, decay_sp), (freq_ref, freq_sp)):
        spread_rows(source, target, states, groups, 8)
    copies[3].wait()
    spread_rows(signal_ref, signal_sp, tokens, groups, 16)
    step = step_ref[...]

    def prepare(n, most):
        _, lam = decay_step(step, row_at(decay_sp, n, groups), row_at(freq_sp, n, groups))
        powers = power_list(lam, SUM_NEAR)
        own = decayed_sum(signal_sp, powers, tokens, groups)
        put_pair(base_ref, 4 * n, groups, power_of(powers[SUM_NEAR], tokens // SUM_NEAR))
        put_pair(base_ref, 4 * n + 2, groups, own)
        return largest(own, most)

    most = lax.fori_loop(0, states, prepare, jnp.zeros((groups, LANES), jnp.float32), unroll=8)
    base_copy = pltpu.make_async_copy(base_ref, base_hbm, sems.at[3])
    base_copy.start()
    write_codes(lambda n: pair_at(base_ref, 4 * n + 2, groups), code_ref, most, states, groups)
    return base_copy


def pair_sums_kernel(
    first_block, signal_hbm, step_hbm, decay_hbm, freq_hbm, *rest
):
    if not first_block:
        rest = rest[2:]
    *out_refs, signal_ref, step_ref, decay_ref, freq_ref, signal_sp, decay_sp, freq_sp, base_ref, code_ref, sems = rest
    buffers = (signal_ref, step_ref, decay_ref, freq_ref, signal_sp, decay_sp, freq_sp)

    @pl.when((lax.axis_index("seqout") == 0) == first_block)
    def _():
        base_copy = pair_sums_body(
            signal_hbm, step_hbm, decay_hbm, freq_hbm, out_refs[0], base_ref, code_ref, buffers, sems
        )
        for copy in start_copies([(code_ref, ref) for ref in out_refs[1:]], sems):
            copy.wait()
        base_copy.wait()


def joined(hop, mine, other, second):
    before = tuple(jnp.where(second, other[part], mine[part]) for part in range(2))
    after = tuple(jnp.where(second, mine[part], other[part]) for part in range(2))
    moved = cmul(hop, before)
    return (moved[0] + after[0], moved[1] + after[1])


def pair_early_kernel(base_ref, early_ref, early_partner_ref, held_ref):
    groups = (early_ref.shape[0] - base_ref.shape[0] // 2) // 2
    states = base_ref.shape[0] // (4 * groups)
    second = lax.rem(lax.axis_index("seqin"), 2) == 1
    scales = [scale_at(ref, states, groups) for ref in (early_ref, early_partner_ref)]

    def gather(n, carry):
        hop = pair_at(base_ref, 4 * n, groups)
        early, early_partner = (
            decode_at(ref, n, scale, groups) for ref, scale in zip((early_ref, early_partner_ref), scales)
        )
        put_pair(held_ref, 6 * n, groups, hop)
        put_pair(held_ref, 6 * n + 2, groups, pair_at(base_ref, 4 * n + 2, groups))
        put_pair(held_ref, 6 * n + 4, groups, joined(hop, early, early_partner, second))
        return carry

    lax.fori_loop(0, states, gather, 0, unroll=8)


def pair_message_kernel(held_ref, partner_ref, message_hbm, known_hbm, *scratch):
    message_ref, known_ref, code_ref, sems = scratch
    groups = (partner_ref.shape[0] - held_ref.shape[0] // 3) // 2
    states = held_ref.shape[0] // (6 * groups)
    place = lax.axis_index("seqin")
    second = lax.rem(place, 2) == 1
    upper = place >= 2
    scale = scale_at(partner_ref, states, groups)

    def gather(n, most):
        hop, own, early_total = (pair_at(held_ref, 6 * n + 2 * i, groups) for i in range(3))
        partner = decode_at(partner_ref, n, scale, groups)
        total = joined(hop, own, partner, second)
        hop2 = cmul(hop, hop)
        moved2 = cmul(hop2, early_total)
        moved4 = cmul(hop2, moved2)
        moved3 = cmul(hop, moved2)
        message = tuple(jnp.where(upper, early_total[part], total[part] + moved4[part]) for part in range(2))
        known = tuple(jnp.where(second, moved3[part] + partner[part], moved2[part]) for part in range(2))
        put_pair(message_ref, 2 * n, groups, message)
        put_pair(known_ref, 2 * n, groups, known)
        return largest(message, most)

    most = lax.fori_loop(0, states, gather, jnp.zeros((groups, LANES), jnp.float32), unroll=8)
    known_copy = pltpu.make_async_copy(known_ref, known_hbm, sems.at[0])
    known_copy.start()
    write_codes(lambda n: pair_at(message_ref, 2 * n, groups), code_ref, most, states, groups)
    copy = pltpu.make_async_copy(code_ref, message_hbm, sems.at[1])
    copy.start()
    known_copy.wait()
    copy.wait()


def taps_kernel(
    step_hbm, decay_hbm, freq_hbm, real_hbm, imag_hbm, base_hbm,
    taps_hbm, tables_hbm, late_hbm, base_ref,
    step_ref, decay_ref, freq_ref, real_ref, imag_ref,
    decay_sp, freq_sp, real_sp, imag_sp, near_ref, lead_ref, late_ref, taps_ref, tables_ref, sems,
):
    copies = start_copies(
        (
            (step_hbm, step_ref), (decay_hbm, decay_ref), (freq_hbm, freq_ref), (real_hbm, real_ref),
            (imag_hbm, imag_ref), (base_hbm, base_ref),
        ),
        sems,
    )
    states, channels = decay_ref.shape
    groups = channels // LANES
    half = taps_ref.shape[0] // groups
    outer = half // NEAR
    shift_row, hop_row = states * 2 * FINAL_NEAR, states * (2 * FINAL_NEAR + 2)
    for copy in copies[:5]:
        copy.wait()
    for source, target in ((decay_ref, decay_sp), (freq_ref, freq_sp), (real_ref, real_sp), (imag_ref, imag_sp)):
        spread_rows(source, target, states, groups, 8)
    step = step_ref[...]

    def prepare(n, carry):
        fade, lam = decay_step(step, row_at(decay_sp, n, groups), row_at(freq_sp, n, groups))
        gain = gain_of(fade)
        weight = (2.0 * row_at(real_sp, n, groups), 2.0 * row_at(imag_sp, n, groups))
        lead = (weight[0] * gain, weight[1] * gain)
        powers = power_list(lam, NEAR)
        for u in range(1, NEAR):
            put_pair(near_ref, n * (2 * NEAR) + 2 * u, groups, powers[u])
        for u in range(FINAL_NEAR):
            put_pair(tables_ref, n * (2 * FINAL_NEAR) + 2 * u, groups, powers[u if u else FINAL_NEAR])
        put_pair(tables_ref, shift_row + 2 * n, groups, cmul(lead, lam))
        put_pair(tables_ref, hop_row + 2 * n, groups, power_of(powers[NEAR], 2 * outer))
        for a in range(outer):
            if a:
                lead = cmul(lead, powers[NEAR])
            put_pair(lead_ref, n * (2 * outer) + 2 * a, groups, lead)
        put_pair(late_ref, 2 * n, groups, cmul(lead, powers[NEAR]))
        return carry

    lax.fori_loop(0, states, prepare, 0, unroll=2)
    copies[5].wait()
    tables_copies = start_copies(((tables_ref, tables_hbm), (late_ref, late_hbm)), sems)
    zero = jnp.zeros((groups, LANES), jnp.float32)
    count = min(2, outer)
    for first in range(0, outer, count):

        def lead_of(n, first=first):
            return [pair_at(lead_ref, n * (2 * outer) + 2 * (first + a), groups) for a in range(count)]

        acc = power_sum(near_ref, lead_of, states, groups, NEAR, count, [zero] * (count * NEAR))
        for t in range(count * NEAR):
            put_row(taps_ref, first * NEAR + t, groups, acc[t])
    taps_copy = pltpu.make_async_copy(taps_ref, taps_hbm, sems.at[2])
    taps_copy.start()
    for copy in tables_copies:
        copy.wait()
    taps_copy.wait()


def convolve(signal_sp, taps_pad, skip, out_ref, tokens, groups, low=0, high=None):
    tile = 8

    def col_tile(ji, acc, ti):
        gap = (ti - ji) * tile + 1
        window = [row_at(taps_pad, gap + m, groups) for m in range(2 * tile - 1)]
        acc = list(acc)
        for j in range(tile):
            drive = row_at(signal_sp, ji * tile + j, groups)
            for t in range(tile):
                acc[t] = acc[t] + window[t - j + tile - 1] * drive
        return tuple(acc)

    for ti in range(low, tokens // tile):
        first = 0 if high is None else max(0, ti - high + 1)
        if low:
            init = tuple(row_at(out_ref, ti * tile + t, groups) for t in range(tile))
        else:
            init = tuple(skip * row_at(signal_sp, ti * tile + t, groups) for t in range(tile))
        acc = lax.fori_loop(first, ti - low + 1, functools.partial(col_tile, ti=ti), init, unroll=4)
        for t in range(tile):
            put_row(out_ref, ti * tile + t, groups, acc[t])


def pair_conv_kernel(
    signal_hbm, skip_hbm, taps_hbm, tables_hbm, known_hbm, late_hbm, pack_ref,
    signal_ref, skip_ref, late_ref, signal_sp, taps_pad, sems,
):
    tokens, channels = signal_ref.shape
    groups = channels // LANES
    states = late_ref.shape[0] // (2 * groups)
    half, tile = tokens // 2, 8
    first, last = tokens * groups, tokens * groups + tables_hbm.shape[0]
    near_ref = pack_ref.at[first:last]
    copies = start_copies(
        (
            (signal_hbm, signal_ref), (skip_hbm, skip_ref),
            (taps_hbm, taps_pad.at[tile * groups : (tile + half) * groups]),
            (late_hbm, late_ref), (tables_hbm, near_ref),
            (known_hbm, pack_ref.at[last : last + known_hbm.shape[0]]),
        ),
        sems,
    )
    taps_pad[0 : tile * groups, :] = jnp.zeros((tile * groups, LANES), jnp.float32)
    for copy in copies[:3]:
        copy.wait()
    spread_rows(signal_ref, signal_sp, tokens, groups, 16)
    skip = skip_ref[...]
    out_ref = pack_ref.at[0:first]
    convolve(signal_sp, taps_pad, skip, out_ref, tokens, groups, 0, half // tile)
    for copy in copies[3:]:
        copy.wait()
    zero = jnp.zeros((groups, LANES), jnp.float32)
    count = 32 // FINAL_NEAR

    def lead_of(n):
        hop = pair_at(near_ref, n * (2 * FINAL_NEAR), groups)
        leads = [pair_at(late_ref, 2 * n, groups)]
        for _ in range(count):
            leads.append(cmul(leads[-1], hop))
        put_pair(late_ref, 2 * n, groups, leads[count])
        return leads

    for start in range(half, tokens, count * FINAL_NEAR):
        acc = power_sum(near_ref, lead_of, states, groups, FINAL_NEAR, count, [zero] * (count * FINAL_NEAR))
        for t in range(count * FINAL_NEAR):
            put_row(taps_pad, tile + start + t, groups, acc[t])
    convolve(signal_sp, taps_pad, skip, out_ref, tokens, groups, half // tile)


def final_kernel(states, pairs, pack_ref, *refs):
    message_refs, out_ref = refs[:-5], refs[-5]
    state_sp, rows_ref, out_buf, sems = refs[-4:]
    tokens, channels = out_ref.shape
    groups = channels // LANES
    near = FINAL_NEAR
    outer = tokens // near
    local_ref, near_ref, shift_ref, hop_ref, own_ref = split_pack(pack_ref, tokens, states, groups)
    scales = [scale_at(ref, states, groups) for ref in message_refs]
    second = lax.rem(lax.axis_index("seqin"), 2).astype(jnp.float32)

    def enter(n, carry):
        hop = pair_at(hop_ref, 2 * n, groups)
        state = pair_at(own_ref, 2 * n, groups)
        if pairs:
            part = decode_at(message_refs[0], n, scales[0], groups)
            moved = cmul((1.0 + second * (hop[0] - 1.0), second * hop[1]), part)
            state = (moved[0] + state[0], moved[1] + state[1])
            put_pair(state_sp, 2 * n, groups, cmul(pair_at(shift_ref, 2 * n, groups), state))
            return carry
        for ref, scale in zip(reversed(message_refs), reversed(scales)):
            moved, part = cmul(hop, state), decode_at(ref, n, scale, groups)
            state = (moved[0] + part[0], moved[1] + part[1])
        put_pair(state_sp, 2 * n, groups, cmul(pair_at(shift_ref, 2 * n, groups), state))
        return carry

    lax.fori_loop(0, states, enter, 0, unroll=8)
    count = min(32 // near, outer)
    span = count * near
    copies = []
    for index in range(outer // count):
        last = index + 1 == outer // count

        def lead_of(n, last=last):
            hop = pair_at(near_ref, n * (2 * near), groups)
            leads = [pair_at(state_sp, 2 * n, groups)]
            for _ in range(count - 1 if last else count):
                leads.append(cmul(leads[-1], hop))
            if not last:
                for part in range(2):
                    put_row(state_sp, 2 * n + part, groups, leads[count][part])
            return leads

        start = index * span
        init = [local_ref[(start + t) * groups : (start + t + 1) * groups, :] for t in range(span)]
        acc = power_sum(near_ref, lead_of, states, groups, near, count, init)
        for t in range(span):
            rows_ref[t * groups : (t + 1) * groups, :] = acc[t]
        for t in range(0, span, 8):
            for k in range(groups):
                out_buf[start + t : start + t + 8, k * LANES : (k + 1) * LANES] = rows_ref[
                    pl.ds(t * groups + k, 8, stride=groups), :
                ]
        copy = pltpu.make_async_copy(
            out_buf.at[pl.ds(start, span)], out_ref.at[pl.ds(start, span)], sems.at[index]
        )
        copy.start()
        copies.append(copy)
    for copy in copies:
        copy.wait()


def per_device(n_in, n_out, inputs, time_step, decay_rate, frequency, output_real, output_imag, skip_gain):
    signal = inputs[0]
    tokens, channels = signal.shape
    states = decay_rate.shape[0]
    groups = channels // LANES
    outer = tokens // NEAR
    code_rows = 2 * groups * (states + 1)
    f32 = jnp.float32
    any_space = pl.BlockSpec(memory_space=pl.ANY)
    in_vmem = pl.BlockSpec(memory_space=pltpu.VMEM)
    in_hbm = pl.BlockSpec(memory_space=pltpu.HBM)

    def rows(count, dtype=f32):
        return pltpu.VMEM((count * groups, LANES), dtype)

    def shape(*dims):
        return jax.ShapeDtypeStruct(dims, f32)

    def kept(count):
        return pltpu.HBM((count * groups, LANES), f32)

    def hbm(array):
        return pltpu.with_memory_space_constraint(array, pltpu.HBM)

    def call(kernel, name, flops, **options):
        return pl.pallas_call(
            kernel,
            compiler_params=pltpu.CompilerParams(vmem_limit_bytes=24 * 1024 * 1024),
            cost_estimate=pl.CostEstimate(flops=flops, bytes_accessed=2_000_000, transcendentals=0),
            name=name,
            **options,
        )

    parameters = tuple(hbm(array) for array in (time_step.reshape(groups, LANES), decay_rate, frequency))
    codes = pltpu.HBM((code_rows, LANES), jnp.bfloat16)

    pairs = (n_in, n_out) == (4, 2) and tokens == 128
    if pairs:
        sum_buffers = [
            pltpu.VMEM((tokens, channels), signal.dtype),
            rows(1),
            *[pltpu.VMEM((states, channels), f32)] * 2,
            rows(tokens),
            *[rows(states)] * 2,
        ]
        code_buffer = pltpu.VMEM((code_rows, LANES), jnp.bfloat16)
        sum_scratch = [*sum_buffers, rows(4 * states), code_buffer, pltpu.SemaphoreType.DMA((4,))]
        base, kept_code, code = call(
            functools.partial(pair_sums_kernel, True),
            "sums",
            20_000_000,
            out_shape=(kept(4 * states), codes, codes),
            in_specs=[any_space] * 4,
            out_specs=(in_hbm,) * 3,
            scratch_shapes=sum_scratch,
        )(hbm(signal), *parameters)
        across = lax.ppermute(
            code, ("seqin", "seqout"), [(z * n_out, (z ^ 1) * n_out + 1) for z in range(n_in)]
        )
        early = lax.ppermute(code, "seqout", [(0, 1)])
        base, code = call(
            functools.partial(pair_sums_kernel, False),
            "base",
            20_000_000,
            out_shape=(kept(4 * states), codes),
            in_specs=[any_space] * 4 + [in_hbm] * 2,
            out_specs=(in_hbm,) * 2,
            input_output_aliases={4: 0, 5: 1},
            scratch_shapes=sum_scratch,
        )(hbm(signal), *parameters, base, kept_code)
        partner = lax.ppermute(code, "seqin", [(z, z ^ 1) for z in range(n_in)])

        table_rows = states * (2 * FINAL_NEAR + 4)
        taps, tables, late, base = call(
            taps_kernel,
            "taps",
            24_000_000,
            out_shape=(kept(tokens // 2), kept(table_rows), kept(2 * states), shape(4 * states * groups, LANES)),
            in_specs=[any_space] * 6,
            out_specs=(in_hbm, in_hbm, in_hbm, in_vmem),
            scratch_shapes=[
                rows(1),
                *[pltpu.VMEM((states, channels), f32)] * 4,
                *[rows(states)] * 4,
                rows(2 * NEAR * states),
                rows(outer * states),
                rows(2 * states),
                rows(tokens // 2),
                rows(table_rows),
                pltpu.SemaphoreType.DMA((6,)),
            ],
        )(*parameters, hbm(output_real), hbm(output_imag), hbm(base))

        held = call(
            pair_early_kernel,
            "early",
            100_000_000,
            out_shape=shape(6 * states * groups, LANES),
            in_specs=[in_vmem] * 3,
        )(base, early, across)

        message, own = call(
            pair_message_kernel,
            "messages",
            6_000_000,
            out_shape=(codes, kept(2 * states)),
            in_specs=[in_vmem] * 2,
            out_specs=(in_hbm, in_hbm),
            scratch_shapes=[
                rows(2 * states),
                rows(2 * states),
                code_buffer,
                pltpu.SemaphoreType.DMA((2,)),
            ],
        )(held, partner)

        received = [lax.ppermute(message, "seqin", [(z, z ^ 2) for z in range(n_in)])]

        pack = call(
            pair_conv_kernel,
            "conv",
            18_000_000,
            out_shape=shape((tokens + table_rows + 2 * states) * groups, LANES),
            in_specs=[any_space] * 6,
            scratch_shapes=[
                pltpu.VMEM((tokens, channels), signal.dtype),
                rows(1),
                rows(2 * states),
                rows(tokens),
                rows(tokens + 8),
                pltpu.SemaphoreType.DMA((6,)),
            ],
        )(hbm(signal), hbm(skip_gain.reshape(groups, LANES)), hbm(taps), hbm(tables), hbm(own), hbm(late))
    else:
        def sums(send, given):
            return call(
                functools.partial(sums_kernel, n_in, send),
                "sums" if send else "base",
                20_000_000,
                out_shape=codes if send else shape(4 * states * groups, LANES),
                in_specs=[any_space] * 4,
                out_specs=in_hbm if send else in_vmem,
                scratch_shapes=[
                    pltpu.VMEM((tokens, channels), signal.dtype),
                    rows(1),
                    *[pltpu.VMEM((states, channels), f32)] * 2,
                    rows(tokens),
                    *[rows(states)] * 2,
                    rows(4 * states if send else 1),
                    pltpu.VMEM((code_rows if send else 16, LANES), jnp.bfloat16),
                    pltpu.SemaphoreType.DMA((4,)),
                ],
            )(hbm(signal), *given)

        code = sums(True, parameters)
        early = [lax.ppermute(code, "seqout", [(i, i + j) for i in range(n_out - j)]) for j in range(1, n_out)]
        later = lax.optimization_barrier((code, *parameters))[1:]
        parameters = tuple(hbm(array) for array in later)
        base = sums(False, parameters)

        *messages, own = call(
            functools.partial(messages_kernel, n_in, n_out - 1),
            "messages",
            4_000_000,
            out_shape=(*[codes] * (n_in - 1), kept(2 * states)),
            in_specs=(in_vmem, any_space, *[in_vmem] * (n_out - 1)),
            out_specs=(in_hbm,) * n_in,
            scratch_shapes=[
                rows(2 * states),
                rows(2 * states),
                pltpu.VMEM((2, code_rows, LANES), jnp.bfloat16),
                pltpu.SemaphoreType.DMA((n_in,)),
            ],
        )(base, hbm(code), *early)

        received = [
            lax.ppermute(messages[d - 1], "seqin", [(i, (i + d) % n_in) for i in range(n_in)]) for d in range(1, n_in)
        ]

        pack = call(
            conv_kernel,
            "conv",
            40_000_000,
            out_shape=shape((tokens + states * (2 * FINAL_NEAR + 6)) * groups, LANES),
            in_specs=[any_space] * 8,
            scratch_shapes=[
                pltpu.VMEM((tokens, channels), signal.dtype),
                rows(1),
                rows(1),
                *[pltpu.VMEM((states, channels), f32)] * 4,
                *[rows(states)] * 4,
                rows(2 * NEAR * states),
                rows(2 * outer * states),
                rows(tokens),
                rows(tokens + 8),
                pltpu.SemaphoreType.DMA((8,)),
            ],
        )(
            hbm(signal), hbm(skip_gain.reshape(groups, LANES)), *parameters,
            hbm(output_real), hbm(output_imag), hbm(own),
        )

    count = min(32 // FINAL_NEAR, tokens // FINAL_NEAR)
    outputs = call(
        functools.partial(final_kernel, states, pairs),
        "final",
        20_000_000,
        out_shape=shape(tokens, channels),
        out_specs=any_space,
        scratch_shapes=[
            rows(2 * states),
            rows(count * FINAL_NEAR),
            pltpu.VMEM((tokens, channels), f32),
            pltpu.SemaphoreType.DMA((tokens // FINAL_NEAR // count,)),
        ],
    )(pack, *received)
    return outputs[None]


def solution(mesh):
    in_specs = (
        P(("groups", "seqout"), "seqin", "chan"),
        P("chan"),
        P(None, "chan"),
        P(None, "chan"),
        P(None, "chan"),
        P(None, "chan"),
        P("chan"),
    )
    out_specs = P(("groups", "seqout"), "seqin", "chan")
    return jax.shard_map(
        functools.partial(per_device, mesh.shape["seqin"], mesh.shape["seqout"]),
        mesh=mesh,
        in_specs=in_specs,
        out_specs=out_specs,
        check_vma=False,
    )
```

```python
import functools

import jax
import jax.numpy as jnp
from jax import lax
from jax.experimental import pallas as pl
from jax.experimental.pallas import tpu as pltpu
from jax.sharding import PartitionSpec as P

LANES = 128
NEAR = 16
FINAL_NEAR = 16
SUM_NEAR = 8
EARLY_PARTS = 4
HALF_RANGE = 125.0
LOG_TWO = 0.6931471805599453
SMALLEST_CODE = 2.0**-125


def cmul(a, b):
    return (a[0] * b[0] - a[1] * b[1], a[0] * b[1] + a[1] * b[0])


def cos_sin(angle):
    turns = jnp.floor(angle * 0.6366197723675814 + 0.5)
    rest = angle - turns * 1.5703125
    rest = rest - turns * 4.837512969970703125e-4
    rest = rest - turns * 7.549789948768648e-8
    square = rest * rest
    sine = rest + rest * square * (
        -1.6666654611e-1 + square * (8.3321608736e-3 - square * 1.9515295891e-4)
    )
    cosine = (
        1.0
        - 0.5 * square
        + square * square * (4.166664568298827e-2 + square * (-1.388731625493765e-3 + square * 2.443315711809948e-5))
    )
    quarter = turns.astype(jnp.int32) & 3
    swap = (quarter & 1) == 1
    first = jnp.where(swap, sine, cosine)
    second = jnp.where(swap, cosine, sine)
    return (
        jnp.where((quarter == 1) | (quarter == 2), -first, first),
        jnp.where(quarter >= 2, -second, second),
    )


def decay_step(time_step, decay_rate, frequency):
    fade_rate = time_step * decay_rate
    shrink = jnp.exp(-fade_rate)
    cosine, sine = cos_sin(time_step * frequency)
    return (fade_rate, (shrink * cosine, shrink * sine))


def gain_of(fade_rate):
    double = 2.0 * fade_rate
    series = 1.0 / 40320.0
    for factor in (5040.0, 720.0, 120.0, 24.0, 6.0, 2.0, 1.0):
        series = 1.0 / factor - double * series
    small = double * series
    return jnp.sqrt(jnp.where(double < 0.25, small, 1.0 - jnp.exp(-double)))


def power_list(lam, count):
    powers = [None, lam]
    for k in range(2, count + 1):
        powers.append(cmul(powers[k // 2], powers[k - k // 2]))
    return powers


def spread_rows(source_ref, target_ref, rows, groups, stack):
    for start in range(0, rows, stack):
        for k in range(groups):
            part = source_ref[start : start + stack, k * LANES : (k + 1) * LANES]
            target_ref[pl.ds(start * groups + k, stack, stride=groups), :] = part.astype(jnp.float32)


def row_at(ref, index, groups):
    return ref[pl.ds(pl.multiple_of(index * groups, groups), groups), :]


def put_row(ref, index, groups, value):
    ref[pl.ds(pl.multiple_of(index * groups, groups), groups), :] = value


def power_sum(near_ref, lead_of, states, groups, near, count, init):

    def turn(n, acc):
        leads = lead_of(n)
        acc = list(acc)
        for a in range(count):
            acc[a * near] = acc[a * near] + leads[a][0]
        for u in range(1, near):
            real = row_at(near_ref, n * (2 * near) + 2 * u, groups)
            imag = row_at(near_ref, n * (2 * near) + 2 * u + 1, groups)
            for a in range(count):
                slot = a * near + u
                acc[slot] = acc[slot] + (leads[a][0] * real - leads[a][1] * imag)
        return tuple(acc)

    return lax.fori_loop(0, states, turn, tuple(init), unroll=32)


def power_of(base, exponent):
    result = None
    while exponent:
        if exponent & 1:
            result = base if result is None else cmul(result, base)
        exponent //= 2
        if exponent:
            base = cmul(base, base)
    return result


def start_copies(pairs, sems):
    copies = [pltpu.make_async_copy(pair[0], pair[1], sems.at[i]) for i, pair in enumerate(pairs)]
    for copy in copies:
        copy.start()
    return copies


def pair_at(ref, index, groups):
    return tuple(row_at(ref, index + part, groups) for part in range(2))


def put_pair(ref, index, groups, value):
    for part in range(2):
        put_row(ref, index + part, groups, value[part])


def decayed_sum(signal_sp, powers, tokens, groups):
    a_tile = min(4, tokens // SUM_NEAR)
    total = None
    for first in range(0, tokens // SUM_NEAR, a_tile):
        real, imag = [None] * a_tile, [None] * a_tile
        for u in range(SUM_NEAR):
            power = SUM_NEAR - 1 - u
            for a in range(a_tile):
                row = ((first + a) * SUM_NEAR + u) * groups
                drive = signal_sp[row : row + groups, :]
                if power:
                    add_real, add_imag = powers[power][0] * drive, powers[power][1] * drive
                    real[a] = add_real if real[a] is None else real[a] + add_real
                    imag[a] = add_imag if imag[a] is None else imag[a] + add_imag
                else:
                    real[a] = real[a] + drive
        for a in range(a_tile):
            if total is None:
                total = (real[a], imag[a])
            else:
                moved = cmul(powers[SUM_NEAR], total)
                total = (moved[0] + real[a], moved[1] + imag[a])
    return total


def encode(value, inverse):
    code = jnp.exp2(jnp.abs(value) * inverse * (2.0 * HALF_RANGE) - HALF_RANGE)
    return jnp.where(value < 0.0, -code, code)


def decode(code, scale):
    size = (jnp.log(jnp.maximum(jnp.abs(code), SMALLEST_CODE)) * (0.5 / HALF_RANGE / LOG_TWO) + 0.5) * scale
    return jnp.where(code < 0.0, -size, size)


def largest(value, most):
    return jnp.maximum(most, jnp.maximum(jnp.abs(value[0]), jnp.abs(value[1])))


def write_codes(value_of, code_ref, most, states, groups):
    scale = (1.01 * most).astype(jnp.bfloat16).astype(jnp.float32)
    inverse = jnp.where(scale > 1e-36, 1.0 / jnp.maximum(scale, 1e-36), 0.0)
    code_ref[states * 2 * groups :, :] = jnp.concatenate([scale, scale], axis=0).astype(jnp.bfloat16)

    def write(n, carry):
        value = value_of(n)
        code = jnp.concatenate([encode(value[part], inverse) for part in range(2)], axis=0)
        row = pl.multiple_of(n * (2 * groups), 2 * groups)
        code_ref[pl.ds(row, 2 * groups), :] = code.astype(jnp.bfloat16)
        return carry

    lax.fori_loop(0, states, write, 0, unroll=4)


def scale_at(code_ref, states, groups):
    return code_ref[states * 2 * groups :, :].astype(jnp.float32)[0:groups, :]


def decode_at(code_ref, n, scale, groups):
    row = pl.multiple_of(n * (2 * groups), 2 * groups)
    code = code_ref[pl.ds(row, 2 * groups), :].astype(jnp.float32)
    return tuple(decode(code[part * groups : (part + 1) * groups, :], scale) for part in range(2))


def sums_kernel(
    n_in, send, signal_hbm, step_hbm, decay_hbm, freq_hbm,
    result_ref,
    signal_ref, step_ref, decay_ref, freq_ref,
    signal_sp, decay_sp, freq_sp, base_ref, code_ref, sems,
):
    place = lax.axis_index("seqout")
    needed = place < lax.axis_size("seqout") - 1 if send else place > 0

    @pl.when(needed)
    def _():
        copies = start_copies(
            ((step_hbm, step_ref), (decay_hbm, decay_ref), (freq_hbm, freq_ref), (signal_hbm, signal_ref)), sems
        )
        states, channels = decay_ref.shape
        groups = channels // LANES
        tokens = signal_ref.shape[0]
        for copy in copies[:3]:
            copy.wait()
        for source, target in ((decay_ref, decay_sp), (freq_ref, freq_sp)):
            spread_rows(source, target, states, groups, 8)
        copies[3].wait()
        spread_rows(signal_ref, signal_sp, tokens, groups, 16)
        step = step_ref[...]
        target_ref = base_ref if send else result_ref

        def prepare(n, most):
            _, lam = decay_step(step, row_at(decay_sp, n, groups), row_at(freq_sp, n, groups))
            powers = power_list(lam, SUM_NEAR)
            own = decayed_sum(signal_sp, powers, tokens, groups)
            if not send:
                put_pair(target_ref, 4 * n, groups, power_of(powers[SUM_NEAR], tokens // SUM_NEAR * n_in))
            put_pair(target_ref, 4 * n + 2, groups, own)
            return largest(own, most)

        most = lax.fori_loop(0, states, prepare, jnp.zeros((groups, LANES), jnp.float32), unroll=4)
        if send:
            write_codes(lambda n: pair_at(base_ref, 4 * n + 2, groups), code_ref, most, states, groups)
            copy = pltpu.make_async_copy(code_ref, result_ref, sems.at[0])
            copy.start()
            copy.wait()


def messages_kernel(n_in, n_early, base_ref, sent_hbm, *refs):
    received_refs, out_refs, own_hbm = refs[:n_early], refs[n_early : n_early + n_in - 1], refs[n_early + n_in - 1]
    later_ref, own_ref, code_ref, sems = refs[n_early + n_in :]
    groups = (received_refs[0].shape[0] - base_ref.shape[0] // 2) // 2
    states = base_ref.shape[0] // (4 * groups)
    first_block = lax.axis_index("seqout") == 0

    @pl.when(first_block)
    def _():
        copy = pltpu.make_async_copy(sent_hbm, code_ref.at[0], sems.at[0])
        copy.start()
        own_ref[...] = jnp.zeros_like(own_ref)
        code_ref[1] = jnp.zeros_like(code_ref[1])
        copy.wait()

    @pl.when(jnp.logical_not(first_block))
    def _():
        scales = [scale_at(ref, states, groups) for ref in received_refs]

        def gather(n, most):
            block, own = pair_at(base_ref, 4 * n, groups), pair_at(base_ref, 4 * n + 2, groups)
            early = None
            for ref, scale in zip(reversed(received_refs), reversed(scales)):
                part = decode_at(ref, n, scale, groups)
                if early is not None:
                    moved = cmul(block, early)
                    part = (part[0] + moved[0], part[1] + moved[1])
                early = part
            moved = cmul(block, early)
            later = (own[0] + moved[0], own[1] + moved[1])
            put_pair(later_ref, 2 * n, groups, later)
            put_pair(own_ref, 2 * n, groups, early)
            return (largest(later, most[0]), largest(early, most[1]))

        zero = jnp.zeros((groups, LANES), jnp.float32)
        most = lax.fori_loop(0, states, gather, (zero, zero), unroll=4)
        write_codes(lambda n: pair_at(later_ref, 2 * n, groups), code_ref.at[0], most[0], states, groups)
        if n_early == 1:
            code_ref[1] = received_refs[0][...]
        else:
            write_codes(lambda n: pair_at(own_ref, 2 * n, groups), code_ref.at[1], most[1], states, groups)

    place = lax.axis_index("seqin")
    copies = [pltpu.make_async_copy(own_ref, own_hbm, sems.at[0])]
    for d in range(1, n_in):
        kind = (place + d) // n_in
        copies.append(pltpu.make_async_copy(code_ref.at[kind], out_refs[d - 1], sems.at[d]))
    for copy in copies:
        copy.start()
    for copy in copies:
        copy.wait()


def split_pack(pack_ref, tokens, states, groups):
    refs, start = [], 0
    for count in (tokens, states * 2 * FINAL_NEAR, 2 * states, 2 * states, 2 * states):
        refs.append(pack_ref.at[start * groups : (start + count) * groups])
        start += count
    return refs


def conv_kernel(
    signal_hbm, skip_hbm, step_hbm, decay_hbm, freq_hbm, real_hbm, imag_hbm, own_hbm, pack_ref,
    signal_ref, skip_ref, step_ref, decay_ref, freq_ref, real_ref, imag_ref,
    decay_sp, freq_sp, real_sp, imag_sp, near_ref, lead_ref, signal_sp, taps_pad, sems,
):
    tokens, channels = signal_ref.shape
    groups = channels // LANES
    states = decay_ref.shape[0]
    outer = tokens // NEAR
    tile = 8
    out_ref, few_ref, shift_ref, hop_ref, own_ref = split_pack(pack_ref, tokens, states, groups)
    copies = start_copies(
        (
            (step_hbm, step_ref), (decay_hbm, decay_ref), (freq_hbm, freq_ref), (real_hbm, real_ref),
            (imag_hbm, imag_ref), (signal_hbm, signal_ref), (skip_hbm, skip_ref), (own_hbm, own_ref),
        ),
        sems,
    )
    taps_pad[0 : tile * groups, :] = jnp.zeros((tile * groups, LANES), jnp.float32)
    for copy in copies[:5]:
        copy.wait()
    for source, target in ((decay_ref, decay_sp), (freq_ref, freq_sp), (real_ref, real_sp), (imag_ref, imag_sp)):
        spread_rows(source, target, states, groups, 8)
    step = step_ref[...]

    def prepare(n, carry):
        fade, lam = decay_step(step, row_at(decay_sp, n, groups), row_at(freq_sp, n, groups))
        gain = gain_of(fade)
        weight = (2.0 * row_at(real_sp, n, groups), 2.0 * row_at(imag_sp, n, groups))
        lead = (weight[0] * gain, weight[1] * gain)
        powers = power_list(lam, NEAR)
        for u in range(1, NEAR):
            put_pair(near_ref, n * (2 * NEAR) + 2 * u, groups, powers[u])
        for u in range(FINAL_NEAR):
            put_pair(few_ref, n * (2 * FINAL_NEAR) + 2 * u, groups, powers[u if u else FINAL_NEAR])
        put_pair(shift_ref, 2 * n, groups, cmul(lead, lam))
        put_pair(hop_ref, 2 * n, groups, power_of(powers[NEAR], outer))
        for a in range(outer):
            if a:
                lead = cmul(lead, powers[NEAR])
            put_pair(lead_ref, n * (2 * outer) + 2 * a, groups, lead)
        return carry

    lax.fori_loop(0, states, prepare, 0, unroll=2)
    for copy in copies[5:]:
        copy.wait()
    spread_rows(signal_ref, signal_sp, tokens, groups, 16)
    zero = jnp.zeros((groups, LANES), jnp.float32)
    count = min(2, outer)
    for first in range(0, outer, count):

        def lead_of(n, first=first):
            return [pair_at(lead_ref, n * (2 * outer) + 2 * (first + a), groups) for a in range(count)]

        acc = power_sum(near_ref, lead_of, states, groups, NEAR, count, [zero] * (count * NEAR))
        for t in range(count * NEAR):
            put_row(taps_pad, tile + first * NEAR + t, groups, acc[t])

    convolve(signal_sp, taps_pad, skip_ref[...], out_ref, tokens, groups)


def pair_sums_body(signal_hbm, step_hbm, decay_hbm, freq_hbm, base_hbm, base_ref, code_ref, buffers, sems):
    signal_ref, step_ref, decay_ref, freq_ref, signal_sp, decay_sp, freq_sp = buffers
    copies = start_copies(
        ((step_hbm, step_ref), (decay_hbm, decay_ref), (freq_hbm, freq_ref), (signal_hbm, signal_ref)), sems
    )
    states, channels = decay_ref.shape
    groups = channels // LANES
    tokens = signal_ref.shape[0]
    for copy in copies[:3]:
        copy.wait()
    for source, target in ((decay_ref, decay_sp), (freq_ref, freq_sp)):
        spread_rows(source, target, states, groups, 8)
    copies[3].wait()
    spread_rows(signal_ref, signal_sp, tokens, groups, 16)
    step = step_ref[...]

    def prepare(n, most):
        _, lam = decay_step(step, row_at(decay_sp, n, groups), row_at(freq_sp, n, groups))
        powers = power_list(lam, SUM_NEAR)
        own = decayed_sum(signal_sp, powers, tokens, groups)
        put_pair(base_ref, 4 * n, groups, power_of(powers[SUM_NEAR], tokens // SUM_NEAR))
        put_pair(base_ref, 4 * n + 2, groups, own)
        return largest(own, most)

    most = lax.fori_loop(0, states, prepare, jnp.zeros((groups, LANES), jnp.float32), unroll=8)
    base_copy = pltpu.make_async_copy(base_ref, base_hbm, sems.at[3])
    base_copy.start()
    write_codes(lambda n: pair_at(base_ref, 4 * n + 2, groups), code_ref, most, states, groups)
    return base_copy


def pair_sums_kernel(
    first_block, signal_hbm, step_hbm, decay_hbm, freq_hbm, *rest
):
    if not first_block:
        rest = rest[2:]
    *out_refs, signal_ref, step_ref, decay_ref, freq_ref, signal_sp, decay_sp, freq_sp, base_ref, code_ref, sems = rest
    buffers = (signal_ref, step_ref, decay_ref, freq_ref, signal_sp, decay_sp, freq_sp)

    @pl.when((lax.axis_index("seqout") == 0) == first_block)
    def _():
        base_copy = pair_sums_body(
            signal_hbm, step_hbm, decay_hbm, freq_hbm, out_refs[0], base_ref, code_ref, buffers, sems
        )
        for copy in start_copies([(code_ref, ref) for ref in out_refs[1:]], sems):
            copy.wait()
        base_copy.wait()


def joined(hop, mine, other, second):
    before = tuple(jnp.where(second, other[part], mine[part]) for part in range(2))
    after = tuple(jnp.where(second, mine[part], other[part]) for part in range(2))
    moved = cmul(hop, before)
    return (moved[0] + after[0], moved[1] + after[1])


def pair_early_kernel(base_ref, early_ref, early_partner_ref, held_ref):
    groups = (early_ref.shape[0] - base_ref.shape[0] // 2) // 2
    states = base_ref.shape[0] // (4 * groups)
    second = lax.rem(lax.axis_index("seqin"), 2) == 1
    scales = [scale_at(ref, states, groups) for ref in (early_ref, early_partner_ref)]

    def gather(n, carry):
        hop = pair_at(base_ref, 4 * n, groups)
        early, early_partner = (
            decode_at(ref, n, scale, groups) for ref, scale in zip((early_ref, early_partner_ref), scales)
        )
        put_pair(held_ref, 6 * n, groups, hop)
        put_pair(held_ref, 6 * n + 2, groups, pair_at(base_ref, 4 * n + 2, groups))
        put_pair(held_ref, 6 * n + 4, groups, joined(hop, early, early_partner, second))
        return carry

    lax.fori_loop(0, states, gather, 0, unroll=8)


def pair_message_kernel(held_ref, partner_ref, message_hbm, known_hbm, *scratch):
    message_ref, known_ref, code_ref, sems = scratch
    groups = (partner_ref.shape[0] - held_ref.shape[0] // 3) // 2
    states = held_ref.shape[0] // (6 * groups)
    place = lax.axis_index("seqin")
    second = lax.rem(place, 2) == 1
    upper = place >= 2
    scale = scale_at(partner_ref, states, groups)

    def gather(n, most):
        hop, own, early_total = (pair_at(held_ref, 6 * n + 2 * i, groups) for i in range(3))
        partner = decode_at(partner_ref, n, scale, groups)
        total = joined(hop, own, partner, second)
        hop2 = cmul(hop, hop)
        moved2 = cmul(hop2, early_total)
        moved4 = cmul(hop2, moved2)
        moved3 = cmul(hop, moved2)
        message = tuple(jnp.where(upper, early_total[part], total[part] + moved4[part]) for part in range(2))
        known = tuple(jnp.where(second, moved3[part] + partner[part], moved2[part]) for part in range(2))
        put_pair(message_ref, 2 * n, groups, message)
        put_pair(known_ref, 2 * n, groups, known)
        return largest(message, most)

    most = lax.fori_loop(0, states, gather, jnp.zeros((groups, LANES), jnp.float32), unroll=8)
    known_copy = pltpu.make_async_copy(known_ref, known_hbm, sems.at[0])
    known_copy.start()
    write_codes(lambda n: pair_at(message_ref, 2 * n, groups), code_ref, most, states, groups)
    copy = pltpu.make_async_copy(code_ref, message_hbm, sems.at[1])
    copy.start()
    known_copy.wait()
    copy.wait()


def taps_kernel(
    step_hbm, decay_hbm, freq_hbm, real_hbm, imag_hbm, base_hbm,
    taps_hbm, tables_hbm, late_hbm, base_ref,
    step_ref, decay_ref, freq_ref, real_ref, imag_ref,
    decay_sp, freq_sp, real_sp, imag_sp, near_ref, lead_ref, late_ref, taps_ref, tables_ref, sems,
):
    copies = start_copies(
        (
            (step_hbm, step_ref), (decay_hbm, decay_ref), (freq_hbm, freq_ref), (real_hbm, real_ref),
            (imag_hbm, imag_ref), (base_hbm, base_ref),
        ),
        sems,
    )
    states, channels = decay_ref.shape
    groups = channels // LANES
    half = taps_ref.shape[0] // groups
    outer = half // NEAR
    shift_row, hop_row = states * 2 * FINAL_NEAR, states * (2 * FINAL_NEAR + 2)
    for copy in copies[:5]:
        copy.wait()
    for source, target in ((decay_ref, decay_sp), (freq_ref, freq_sp), (real_ref, real_sp), (imag_ref, imag_sp)):
        spread_rows(source, target, states, groups, 8)
    step = step_ref[...]

    def prepare(n, carry):
        fade, lam = decay_step(step, row_at(decay_sp, n, groups), row_at(freq_sp, n, groups))
        gain = gain_of(fade)
        weight = (2.0 * row_at(real_sp, n, groups), 2.0 * row_at(imag_sp, n, groups))
        lead = (weight[0] * gain, weight[1] * gain)
        powers = power_list(lam, NEAR)
        for u in range(1, NEAR):
            put_pair(near_ref, n * (2 * NEAR) + 2 * u, groups, powers[u])
        for u in range(FINAL_NEAR):
            put_pair(tables_ref, n * (2 * FINAL_NEAR) + 2 * u, groups, powers[u if u else FINAL_NEAR])
        put_pair(tables_ref, shift_row + 2 * n, groups, cmul(lead, lam))
        put_pair(tables_ref, hop_row + 2 * n, groups, power_of(powers[NEAR], EARLY_PARTS * outer))
        for a in range(outer):
            if a:
                lead = cmul(lead, powers[NEAR])
            put_pair(lead_ref, n * (2 * outer) + 2 * a, groups, lead)
        put_pair(late_ref, 2 * n, groups, cmul(lead, powers[NEAR]))
        return carry

    tables_copies, chunks = [], 4
    for chunk in range(chunks):
        span = states // chunks
        lax.fori_loop(chunk * span, (chunk + 1) * span, prepare, 0, unroll=2)
        part = pl.ds(chunk * span * 2 * FINAL_NEAR * groups, span * 2 * FINAL_NEAR * groups)
        tables_copies.append(pltpu.make_async_copy(tables_ref.at[part], tables_hbm.at[part], sems.at[chunk]))
        tables_copies[-1].start()
    copies[5].wait()
    part = pl.ds(shift_row * groups, 4 * states * groups)
    tables_copies.append(pltpu.make_async_copy(tables_ref.at[part], tables_hbm.at[part], sems.at[chunks]))
    tables_copies.append(pltpu.make_async_copy(late_ref, late_hbm, sems.at[5]))
    for copy in tables_copies[chunks:]:
        copy.start()
    zero = jnp.zeros((groups, LANES), jnp.float32)
    count = min(2, outer)
    for first in range(0, outer, count):

        def lead_of(n, first=first):
            return [pair_at(lead_ref, n * (2 * outer) + 2 * (first + a), groups) for a in range(count)]

        acc = power_sum(near_ref, lead_of, states, groups, NEAR, count, [zero] * (count * NEAR))
        for t in range(count * NEAR):
            put_row(taps_ref, first * NEAR + t, groups, acc[t])
    taps_copy = pltpu.make_async_copy(taps_ref, taps_hbm, sems.at[6])
    taps_copy.start()
    for copy in tables_copies:
        copy.wait()
    taps_copy.wait()


def convolve(signal_sp, taps_pad, skip, out_ref, tokens, groups, low=0, high=None):
    tile = 8

    def col_tile(ji, acc, ti):
        gap = (ti - ji) * tile + 1
        window = [row_at(taps_pad, gap + m, groups) for m in range(2 * tile - 1)]
        acc = list(acc)
        for j in range(tile):
            drive = row_at(signal_sp, ji * tile + j, groups)
            for t in range(tile):
                acc[t] = acc[t] + window[t - j + tile - 1] * drive
        return tuple(acc)

    for ti in range(low, tokens // tile):
        first = 0 if high is None else max(0, ti - high + 1)
        if low:
            init = tuple(row_at(out_ref, ti * tile + t, groups) for t in range(tile))
        else:
            init = tuple(skip * row_at(signal_sp, ti * tile + t, groups) for t in range(tile))
        acc = lax.fori_loop(first, ti - low + 1, functools.partial(col_tile, ti=ti), init, unroll=4)
        for t in range(tile):
            put_row(out_ref, ti * tile + t, groups, acc[t])


def pair_conv_kernel(
    signal_hbm, skip_hbm, taps_hbm, tables_hbm, known_hbm, late_hbm, pack_ref,
    signal_ref, skip_ref, late_ref, signal_sp, taps_pad, sems,
):
    tokens, channels = signal_ref.shape
    groups = channels // LANES
    states = late_ref.shape[0] // (2 * groups)
    half, tile = tokens // EARLY_PARTS, 8
    first, last = tokens * groups, tokens * groups + tables_hbm.shape[0]
    near_ref = pack_ref.at[first:last]
    copies = start_copies(
        (
            (signal_hbm, signal_ref), (skip_hbm, skip_ref),
            (taps_hbm, taps_pad.at[tile * groups : (tile + half) * groups]),
            (late_hbm, late_ref), (tables_hbm, near_ref),
            (known_hbm, pack_ref.at[last : last + known_hbm.shape[0]]),
        ),
        sems,
    )
    taps_pad[0 : tile * groups, :] = jnp.zeros((tile * groups, LANES), jnp.float32)
    for copy in copies[:3]:
        copy.wait()
    spread_rows(signal_ref, signal_sp, tokens, groups, 16)
    skip = skip_ref[...]
    out_ref = pack_ref.at[0:first]
    convolve(signal_sp, taps_pad, skip, out_ref, tokens, groups, 0, half // tile)
    for copy in copies[3:]:
        copy.wait()
    zero = jnp.zeros((groups, LANES), jnp.float32)
    count = 32 // FINAL_NEAR

    def lead_of(n):
        hop = pair_at(near_ref, n * (2 * FINAL_NEAR), groups)
        leads = [pair_at(late_ref, 2 * n, groups)]
        for _ in range(count):
            leads.append(cmul(leads[-1], hop))
        put_pair(late_ref, 2 * n, groups, leads[count])
        return leads

    for start in range(half, tokens, count * FINAL_NEAR):
        acc = power_sum(near_ref, lead_of, states, groups, FINAL_NEAR, count, [zero] * (count * FINAL_NEAR))
        for t in range(count * FINAL_NEAR):
            put_row(taps_pad, tile + start + t, groups, acc[t])
    convolve(signal_sp, taps_pad, skip, out_ref, tokens, groups, half // tile)


def final_kernel(states, pairs, pack_ref, *refs):
    message_refs, out_ref = refs[:-5], refs[-5]
    state_sp, rows_ref, out_buf, sems = refs[-4:]
    tokens, channels = out_ref.shape
    groups = channels // LANES
    near = FINAL_NEAR
    outer = tokens // near
    local_ref, near_ref, shift_ref, hop_ref, own_ref = split_pack(pack_ref, tokens, states, groups)
    scales = [scale_at(ref, states, groups) for ref in message_refs]
    second = lax.rem(lax.axis_index("seqin"), 2).astype(jnp.float32)

    def enter(n, carry):
        hop = pair_at(hop_ref, 2 * n, groups)
        state = pair_at(own_ref, 2 * n, groups)
        if pairs:
            part = decode_at(message_refs[0], n, scales[0], groups)
            moved = cmul((1.0 + second * (hop[0] - 1.0), second * hop[1]), part)
            state = (moved[0] + state[0], moved[1] + state[1])
            put_pair(state_sp, 2 * n, groups, cmul(pair_at(shift_ref, 2 * n, groups), state))
            return carry
        for ref, scale in zip(reversed(message_refs), reversed(scales)):
            moved, part = cmul(hop, state), decode_at(ref, n, scale, groups)
            state = (moved[0] + part[0], moved[1] + part[1])
        put_pair(state_sp, 2 * n, groups, cmul(pair_at(shift_ref, 2 * n, groups), state))
        return carry

    lax.fori_loop(0, states, enter, 0, unroll=8)
    count = min(32 // near, outer)
    span = count * near
    copies = []
    for index in range(outer // count):
        last = index + 1 == outer // count

        def lead_of(n, last=last):
            hop = pair_at(near_ref, n * (2 * near), groups)
            leads = [pair_at(state_sp, 2 * n, groups)]
            for _ in range(count - 1 if last else count):
                leads.append(cmul(leads[-1], hop))
            if not last:
                for part in range(2):
                    put_row(state_sp, 2 * n + part, groups, leads[count][part])
            return leads

        start = index * span
        init = [local_ref[(start + t) * groups : (start + t + 1) * groups, :] for t in range(span)]
        acc = power_sum(near_ref, lead_of, states, groups, near, count, init)
        for t in range(span):
            rows_ref[t * groups : (t + 1) * groups, :] = acc[t]
        for t in range(0, span, 8):
            for k in range(groups):
                out_buf[start + t : start + t + 8, k * LANES : (k + 1) * LANES] = rows_ref[
                    pl.ds(t * groups + k, 8, stride=groups), :
                ]
        copy = pltpu.make_async_copy(
            out_buf.at[pl.ds(start, span)], out_ref.at[pl.ds(start, span)], sems.at[index]
        )
        copy.start()
        copies.append(copy)
    for copy in copies:
        copy.wait()


def per_device(n_in, n_out, inputs, time_step, decay_rate, frequency, output_real, output_imag, skip_gain):
    signal = inputs[0]
    tokens, channels = signal.shape
    states = decay_rate.shape[0]
    groups = channels // LANES
    outer = tokens // NEAR
    code_rows = 2 * groups * (states + 1)
    f32 = jnp.float32
    any_space = pl.BlockSpec(memory_space=pl.ANY)
    in_vmem = pl.BlockSpec(memory_space=pltpu.VMEM)
    in_hbm = pl.BlockSpec(memory_space=pltpu.HBM)

    def rows(count, dtype=f32):
        return pltpu.VMEM((count * groups, LANES), dtype)

    def shape(*dims):
        return jax.ShapeDtypeStruct(dims, f32)

    def kept(count):
        return pltpu.HBM((count * groups, LANES), f32)

    def hbm(array):
        return pltpu.with_memory_space_constraint(array, pltpu.HBM)

    def call(kernel, name, flops, **options):
        return pl.pallas_call(
            kernel,
            compiler_params=pltpu.CompilerParams(vmem_limit_bytes=24 * 1024 * 1024),
            cost_estimate=pl.CostEstimate(flops=flops, bytes_accessed=2_000_000, transcendentals=0),
            name=name,
            **options,
        )

    parameters = tuple(hbm(array) for array in (time_step.reshape(groups, LANES), decay_rate, frequency))
    codes = pltpu.HBM((code_rows, LANES), jnp.bfloat16)

    pairs = (n_in, n_out) == (4, 2) and tokens == 128
    if pairs:
        sum_buffers = [
            pltpu.VMEM((tokens, channels), signal.dtype),
            rows(1),
            *[pltpu.VMEM((states, channels), f32)] * 2,
            rows(tokens),
            *[rows(states)] * 2,
        ]
        code_buffer = pltpu.VMEM((code_rows, LANES), jnp.bfloat16)
        sum_scratch = [*sum_buffers, rows(4 * states), code_buffer, pltpu.SemaphoreType.DMA((4,))]
        base, kept_code, code = call(
            functools.partial(pair_sums_kernel, True),
            "sums",
            20_000_000,
            out_shape=(kept(4 * states), codes, codes),
            in_specs=[any_space] * 4,
            out_specs=(in_hbm,) * 3,
            scratch_shapes=sum_scratch,
        )(hbm(signal), *parameters)
        across = lax.ppermute(
            code, ("seqin", "seqout"), [(z * n_out, (z ^ 1) * n_out + 1) for z in range(n_in)]
        )
        early = lax.ppermute(code, "seqout", [(0, 1)])
        base, code = call(
            functools.partial(pair_sums_kernel, False),
            "base",
            20_000_000,
            out_shape=(kept(4 * states), codes),
            in_specs=[any_space] * 4 + [in_hbm] * 2,
            out_specs=(in_hbm,) * 2,
            input_output_aliases={4: 0, 5: 1},
            scratch_shapes=sum_scratch,
        )(hbm(signal), *parameters, base, kept_code)
        partner = lax.ppermute(code, "seqin", [(z, z ^ 1) for z in range(n_in)])

        table_rows = states * (2 * FINAL_NEAR + 4)
        taps, tables, late, base = call(
            taps_kernel,
            "taps",
            24_000_000,
            out_shape=(kept(tokens // EARLY_PARTS), kept(table_rows), kept(2 * states), shape(4 * states * groups, LANES)),
            in_specs=[any_space] * 6,
            out_specs=(in_hbm, in_hbm, in_hbm, in_vmem),
            scratch_shapes=[
                rows(1),
                *[pltpu.VMEM((states, channels), f32)] * 4,
                *[rows(states)] * 4,
                rows(2 * NEAR * states),
                rows(outer * states),
                rows(2 * states),
                rows(tokens // EARLY_PARTS),
                rows(table_rows),
                pltpu.SemaphoreType.DMA((7,)),
            ],
        )(*parameters, hbm(output_real), hbm(output_imag), hbm(base))

        held = call(
            pair_early_kernel,
            "early",
            100_000_000,
            out_shape=shape(6 * states * groups, LANES),
            in_specs=[in_vmem] * 3,
        )(base, early, across)

        message, own = call(
            pair_message_kernel,
            "messages",
            6_000_000,
            out_shape=(codes, kept(2 * states)),
            in_specs=[in_vmem] * 2,
            out_specs=(in_hbm, in_hbm),
            scratch_shapes=[
                rows(2 * states),
                rows(2 * states),
                code_buffer,
                pltpu.SemaphoreType.DMA((2,)),
            ],
        )(held, partner)

        received = [lax.ppermute(message, "seqin", [(z, z ^ 2) for z in range(n_in)])]

        pack = call(
            pair_conv_kernel,
            "conv",
            18_000_000,
            out_shape=shape((tokens + table_rows + 2 * states) * groups, LANES),
            in_specs=[any_space] * 6,
            scratch_shapes=[
                pltpu.VMEM((tokens, channels), signal.dtype),
                rows(1),
                rows(2 * states),
                rows(tokens),
                rows(tokens + 8),
                pltpu.SemaphoreType.DMA((6,)),
            ],
        )(hbm(signal), hbm(skip_gain.reshape(groups, LANES)), hbm(taps), hbm(tables), hbm(own), hbm(late))
    else:
        def sums(send, given):
            return call(
                functools.partial(sums_kernel, n_in, send),
                "sums" if send else "base",
                20_000_000,
                out_shape=codes if send else shape(4 * states * groups, LANES),
                in_specs=[any_space] * 4,
                out_specs=in_hbm if send else in_vmem,
                scratch_shapes=[
                    pltpu.VMEM((tokens, channels), signal.dtype),
                    rows(1),
                    *[pltpu.VMEM((states, channels), f32)] * 2,
                    rows(tokens),
                    *[rows(states)] * 2,
                    rows(4 * states if send else 1),
                    pltpu.VMEM((code_rows if send else 16, LANES), jnp.bfloat16),
                    pltpu.SemaphoreType.DMA((4,)),
                ],
            )(hbm(signal), *given)

        code = sums(True, parameters)
        early = [lax.ppermute(code, "seqout", [(i, i + j) for i in range(n_out - j)]) for j in range(1, n_out)]
        later = lax.optimization_barrier((code, *parameters))[1:]
        parameters = tuple(hbm(array) for array in later)
        base = sums(False, parameters)

        *messages, own = call(
            functools.partial(messages_kernel, n_in, n_out - 1),
            "messages",
            4_000_000,
            out_shape=(*[codes] * (n_in - 1), kept(2 * states)),
            in_specs=(in_vmem, any_space, *[in_vmem] * (n_out - 1)),
            out_specs=(in_hbm,) * n_in,
            scratch_shapes=[
                rows(2 * states),
                rows(2 * states),
                pltpu.VMEM((2, code_rows, LANES), jnp.bfloat16),
                pltpu.SemaphoreType.DMA((n_in,)),
            ],
        )(base, hbm(code), *early)

        received = [
            lax.ppermute(messages[d - 1], "seqin", [(i, (i + d) % n_in) for i in range(n_in)]) for d in range(1, n_in)
        ]

        pack = call(
            conv_kernel,
            "conv",
            40_000_000,
            out_shape=shape((tokens + states * (2 * FINAL_NEAR + 6)) * groups, LANES),
            in_specs=[any_space] * 8,
            scratch_shapes=[
                pltpu.VMEM((tokens, channels), signal.dtype),
                rows(1),
                rows(1),
                *[pltpu.VMEM((states, channels), f32)] * 4,
                *[rows(states)] * 4,
                rows(2 * NEAR * states),
                rows(2 * outer * states),
                rows(tokens),
                rows(tokens + 8),
                pltpu.SemaphoreType.DMA((8,)),
            ],
        )(
            hbm(signal), hbm(skip_gain.reshape(groups, LANES)), *parameters,
            hbm(output_real), hbm(output_imag), hbm(own),
        )

    count = min(32 // FINAL_NEAR, tokens // FINAL_NEAR)
    outputs = call(
        functools.partial(final_kernel, states, pairs),
        "final",
        20_000_000,
        out_shape=shape(tokens, channels),
        out_specs=any_space,
        scratch_shapes=[
            rows(2 * states),
            rows(count * FINAL_NEAR),
            pltpu.VMEM((tokens, channels), f32),
            pltpu.SemaphoreType.DMA((tokens // FINAL_NEAR // count,)),
        ],
    )(pack, *received)
    return outputs[None]


def solution(mesh):
    in_specs = (
        P(("groups", "seqout"), "seqin", "chan"),
        P("chan"),
        P(None, "chan"),
        P(None, "chan"),
        P(None, "chan"),
        P(None, "chan"),
        P("chan"),
    )
    out_specs = P(("groups", "seqout"), "seqin", "chan")
    return jax.shard_map(
        functools.partial(per_device, mesh.shape["seqin"], mesh.shape["seqout"]),
        mesh=mesh,
        in_specs=in_specs,
        out_specs=out_specs,
        check_vma=False,
    )
```
